32 devices in a mesh: lon: 2 (over core), lat: 4 (over y, x), lead: 4 (over z).
Axes of the slice: x: 2, y: 2, z: 4, core: 2. Of those that a mesh axis runs over, the one named last changes fastest.
Arguments:
- activation: bfloat16 [16, 64, 4096], P('lead', 'lat', 'lon'), may hold values from -6 to 6
- pre_activation: bfloat16 [16, 64, 4096], P('lead', 'lat', 'lon'), may hold values from -8 to 8
- cotangent: bfloat16 [16, 64, 4096], P('lead', 'lat', 'lon'), may hold values from -6 to 6
- mode_weight: float32 [4608, 1024], P('lon'), may hold values from -1 to 1
- local_weight: float32 [32, 32], replicated, may hold values from -1 to 1
Outputs:
- input_grad: bfloat16 [16, 64, 4096], P('lead', 'lat', 'lon')
- mode_grad: float32 [4608, 1024], P('lon')
The draws below stay inside these ranges and needn't reach their ends.
All inputs are finite; a program needn't handle non-finite values.
Results may differ from the reference program's by a relative error of at most 0.001.
Values sent between devices are 32-bit elements; how exact they have to be, the bound alone decides.
A program may use at most 64 MiB of HBM per device.

```python
import math
import jax
import jax.numpy as jnp
from jax import lax

C = 32
MX = 24
MY = 24
MZ = 8
CX = 64
NX = 128
NY = 64
NZ = 16
MODES = 4608


def levels(own_key, shape, cuts, smallest, largest):
    def one(position, shards_of):
        draws = jax.random.uniform(jax.random.fold_in(jax.random.fold_in(own_key, 6), position), (shards_of,), jnp.float32, smallest / len(cuts), largest / len(cuts))
        return jnp.repeat(jnp.exp(draws), shape[position] // shards_of).reshape((-1,) + (1,) * (len(shape) - position - 1))

    level = one(*cuts[0])
    for cut in cuts[1:]:
        level = level * one(*cut)
    return level


def normal_values(own_key, dims, deviation, most, pieces=(), held_as=jnp.bfloat16):
    values = jax.random.normal(own_key, dims, jnp.float32) * deviation
    if len(pieces) > 0:
        values = levels(own_key, dims, pieces, -0.22, 0.18) * values
    return jnp.clip(values, min=-most, max=most).astype(held_as)


def setup_inputs(seed: int = 0) -> dict:
    splits = jax.random.split(jax.random.key(seed), 6)
    return {
        "activation": normal_values(splits[0], (NZ, NY, NX * C), 1.0, 6.0, ((0, 4), (1, 4), (2, 2))),
        "pre_activation": normal_values(splits[1], (NZ, NY, NX * C), 1.5, 8.0, ((0, 4), (1, 4), (2, 2))),
        "cotangent": normal_values(splits[2], (NZ, NY, NX * C), 1.0, 6.0, ((0, 4), (1, 4), (2, 2))),
        "mode_weight": normal_values(splits[3], (MODES, C * C), C ** -0.5, 1.0, ((0, 2),), jnp.float32),
        "local_weight": normal_values(splits[4], (C, C), C ** -0.5, 1.0, (), jnp.float32),
    }


def make_basis(length, modes, start, count, stride):
    half = modes // 2
    order = jnp.arange(modes, dtype=jnp.int32)
    freq = jnp.where(order < half, order, order - half + 1).astype(jnp.int32)
    cells = (start + stride * jnp.arange(count, dtype=jnp.int32)).astype(jnp.int32)
    turns = freq[:, None] * cells[None, :] % length
    angle = 2.0 * math.pi / length * turns.astype(jnp.float32)
    waves = jnp.where(order[:, None] < half, jnp.cos(angle), jnp.sin(angle))
    weights = jnp.where(order == 0, jnp.float32(math.sqrt(1.0 / length)), jnp.float32(math.sqrt(2.0 / length)))
    return waves * weights[:, None]

def gelu_slope(value):
    normal_cdf = 0.5 * (1.0 + jax.scipy.special.erf(value / math.sqrt(2.0)))
    density = jnp.exp(-0.5 * value * value) / math.sqrt(2.0 * math.pi)
    return normal_cdf + value * density

def forward_modes(field, lon_basis, lat_basis, lead_basis):
    highest = lax.Precision.HIGHEST
    step = jnp.einsum('zyxc,kx->zykc', field, lon_basis, precision=highest)
    step = jnp.einsum('zykc,ly->zklc', step, lat_basis, precision=highest)
    step = jnp.einsum('zklc,qz->klqc', step, lead_basis, precision=highest)
    return step.reshape(-1, step.shape[-1])

def back_cells(coeffs, lon_basis, lat_basis, lead_basis):
    highest = lax.Precision.HIGHEST
    blocks = coeffs.reshape(lon_basis.shape[0], lat_basis.shape[0], lead_basis.shape[0], coeffs.shape[-1])
    step = jnp.einsum('klqc,qz->zklc', blocks, lead_basis, precision=highest)
    step = jnp.einsum('zklc,ly->zykc', step, lat_basis, precision=highest)
    return jnp.einsum('zykc,kx->zyxc', step, lon_basis, precision=highest)

def to_cells(field):
    owners = NX // CX
    return field.reshape(NZ, NY, owners, CX, C).transpose(0, 1, 3, 2, 4).reshape(NZ, NY, NX, C)

def from_cells(field):
    owners = NX // CX
    return field.reshape(NZ, NY, CX, owners, C).transpose(0, 1, 3, 2, 4).reshape(NZ, NY, NX * C)

def reference(activation, pre_activation, cotangent, mode_weight, local_weight):
    lon_basis = make_basis(NX, MX, 0, NX, 1)
    lat_basis = make_basis(NY, MY, 0, NY, 1)
    lead_basis = make_basis(NZ, MZ, 0, NZ, 1)
    grad_pre = to_cells(cotangent.astype(jnp.float32)) * gelu_slope(to_cells(pre_activation.astype(jnp.float32)))
    coef = forward_modes(to_cells(activation.astype(jnp.float32)), lon_basis, lat_basis, lead_basis)
    gain = math.sqrt(NX * NY * NZ / MODES)
    spectral = gain * forward_modes(grad_pre, lon_basis, lat_basis, lead_basis)
    mode_grad = (coef[:, :, None] * spectral[:, None, :]).reshape(MODES, C * C)
    mixing = mode_weight.reshape(MODES, C, C)
    mode_adjoint = lax.optimization_barrier(jnp.sum(mixing * spectral[:, None, :], axis=2))
    spread = back_cells(mode_adjoint, lon_basis, lat_basis, lead_basis)
    local = jnp.einsum('zyxo,io->zyxi', grad_pre, local_weight, precision=lax.Precision.HIGHEST)
    input_grad = from_cells(spread + local)
    return (input_grad.astype(jnp.bfloat16), mode_grad)
```

```python
import functools
import math

import jax
import jax.numpy as jnp
import ml_dtypes
import numpy as np
from jax import lax
from jax.experimental import pallas as pl
from jax.experimental.pallas import tpu as pltpu
from jax.sharding import PartitionSpec as P

MX = 24
MY = 24
MZ = 8
MODES = 4608


def make_basis(length, modes, start, count, stride):
    half = modes // 2
    order = jnp.arange(modes, dtype=jnp.int32)
    freq = jnp.where(order < half, order, order - half + 1)
    cells = start + stride * jnp.arange(count, dtype=jnp.int32)
    turns = freq[:, None] * cells[None, :] % length
    angle = 2.0 * math.pi / length * turns.astype(jnp.float32)
    waves = jnp.where(order[:, None] < half, jnp.cos(angle), jnp.sin(angle))
    weights = jnp.where(
        order == 0, jnp.float32(math.sqrt(1.0 / length)), jnp.float32(math.sqrt(2.0 / length))
    )
    return waves * weights[:, None]


def gelu_slope(value):
    normal_cdf = 0.5 * (1.0 + jax.scipy.special.erf(value / math.sqrt(2.0)))
    density = jnp.exp(-0.5 * value * value) / math.sqrt(2.0 * math.pi)
    return normal_cdf + value * density


def back_cells(coeffs, lon_basis, lat_basis, lead_basis):
    highest = lax.Precision.HIGHEST
    blocks = coeffs.reshape(
        lon_basis.shape[0], lat_basis.shape[0], lead_basis.shape[0], coeffs.shape[-1]
    )
    step = jnp.einsum("klqc,qz->zklc", blocks, lead_basis, precision=highest)
    step = jnp.einsum("zklc,ly->zykc", step, lat_basis, precision=highest)
    return jnp.einsum("zykc,kx->zyxc", step, lon_basis, precision=highest)


def on_device(activation, pre_activation, cotangent, mode_weight, local_weight):
    highest = lax.Precision.HIGHEST
    channels = local_weight.shape[0]
    lead_cells, lat_cells, merged = activation.shape
    lon_cells = merged // channels
    lon_count = lax.axis_size("lon")
    lon_total = lon_cells * lon_count
    lat_total = lat_cells * lax.axis_size("lat")
    lead_total = lead_cells * lax.axis_size("lead")
    lon_basis = make_basis(lon_total, MX, lax.axis_index("lon"), lon_cells, lon_count)
    lat_basis = make_basis(lat_total, MY, lax.axis_index("lat") * lat_cells, lat_cells, 1)
    lead_basis = make_basis(lead_total, MZ, lax.axis_index("lead") * lead_cells, lead_cells, 1)
    shape4 = (lead_cells, lat_cells, lon_cells, channels)
    grad_pre = cotangent.astype(jnp.float32).reshape(shape4) * gelu_slope(
        pre_activation.astype(jnp.float32).reshape(shape4)
    )
    stacked = jnp.concatenate([activation.astype(jnp.float32).reshape(shape4), grad_pre], axis=3)
    doubled = 2 * channels
    along_lon = jnp.einsum("zyxc,kx->zykc", stacked, lon_basis, precision=highest)
    along_lat = jnp.einsum("zykc,ly->zklc", along_lon, lat_basis, precision=highest)
    partial_sum = jnp.einsum("zklc,qz->klqc", along_lat, lead_basis, precision=highest).reshape(
        -1, doubled
    )
    summed = lax.psum(partial_sum, ("lat", "lead"))
    owned = lax.psum_scatter(summed, "lon", scatter_dimension=0, tiled=True)
    gain = math.sqrt(lon_total * lat_total * lead_total / MODES)
    coef = owned[:, :channels]
    spectral = gain * owned[:, channels:]
    owned_count = owned.shape[0]
    mode_grad = (coef[:, :, None] * spectral[:, None, :]).reshape(owned_count, channels * channels)
    mixing = mode_weight.reshape(owned_count, channels, channels)
    owned_adjoint = jnp.sum(mixing * spectral[:, None, :], axis=2)
    every_mode = lax.all_gather(owned_adjoint, "lon", axis=0, tiled=True)
    spread = back_cells(every_mode, lon_basis, lat_basis, lead_basis)
    local = jnp.einsum("zyxo,io->zyxi", grad_pre, local_weight, precision=highest)
    input_grad = (spread + local).reshape(lead_cells, lat_cells, merged)
    return (input_grad.astype(jnp.bfloat16), mode_grad)


F32 = jnp.float32
BF16 = jnp.bfloat16


def host_basis(length, modes):
    half = modes // 2
    order = np.arange(modes)
    freq = np.where(order < half, order, order - half + 1)
    turns = (freq[:, None] * np.arange(length)[None, :]) % length
    angle = 2.0 * np.pi / length * turns
    waves = np.where(order[:, None] < half, np.cos(angle), np.sin(angle))
    weights = np.where(order == 0, np.sqrt(1.0 / length), np.sqrt(2.0 / length))
    return waves * weights[:, None]


def halves(table):
    table = np.asarray(table, np.float32)
    high = table.astype(ml_dtypes.bfloat16)
    low = (table - high.astype(np.float32)).astype(ml_dtypes.bfloat16)
    return np.stack([high, low])


def cut(value):
    high = value.astype(BF16)
    return high, (value - high.astype(F32)).astype(BF16)


NN = (((1,), (0,)), ((), ()))
NT = (((1,), (1,)), ((), ()))


def mm(a, b, dims=NN):
    return lax.dot_general(a, b, dims, preferred_element_type=F32)


def mm3(table, b, dims=NN):
    bh, bl = cut(b)
    return mm(table[0], bh, dims) + mm(table[0], bl, dims) + mm(table[1], bh, dims)


def placed(shape, axis, channels, base):
    wide = lax.broadcasted_iota(jnp.int32, shape, axis) // channels
    narrow = lax.broadcasted_iota(jnp.int32, shape, 1 - axis) - base
    return jnp.where(wide == narrow, 1.0, 0.0).astype(BF16)


def fold(value):
    r, lanes = value.shape[0] // 4, value.shape[1] // 3
    last = jnp.concatenate([value[3 * r :, g * lanes : (g + 1) * lanes] for g in range(3)], axis=0)
    return jnp.concatenate([value[: 3 * r], last], axis=1)


def unfold(value):
    r, lanes = value.shape[0] // 3, value.shape[1] // 4
    last = jnp.concatenate([value[g * r : (g + 1) * r, 3 * lanes :] for g in range(3)], axis=1)
    return jnp.concatenate([value[:, : 3 * lanes], last], axis=0)


STEPS = 16
ROOT, BIG, SMALL = (float(np.cos(np.pi / v)) for v in (4, 8, 8 / 3))


def waves16(x):
    e = [x[n] + x[n + 8] for n in range(8)]
    o = [x[n] - x[n + 8] for n in range(8)]
    ee = [e[n] + e[n + 4] for n in range(4)]
    eo = [e[n] - e[n + 4] for n in range(4)]
    even, odd = ee[0] + ee[2], ee[1] + ee[3]
    minus, plus = ROOT * (eo[1] - eo[3]), ROOT * (eo[1] + eo[3])
    d1, d2, d3 = o[1] - o[7], ROOT * (o[2] - o[6]), o[3] - o[5]
    s1, s2, s3 = o[1] + o[7], ROOT * (o[2] + o[6]), o[3] + o[5]
    a, b = BIG * d1 + SMALL * d3, SMALL * d1 - BIG * d3
    g, h = SMALL * s1 + BIG * s3, BIG * s1 - SMALL * s3
    up, down = o[0] + d2, o[0] - d2
    high, low = o[4] + s2, o[4] - s2
    return [
        (even + odd, even - odd),
        (up + a, high + g),
        (eo[0] + minus, plus + eo[2]),
        (down + b, h - low),
        (ee[0] - ee[2], ee[1] - ee[3]),
        (down - b, h + low),
        (eo[0] - minus, plus - eo[2]),
        (up - a, g - high),
    ]


def cells16(u):
    (c0, c8), (c1, s1), (c2, s2), (c3, s3), (c4, s4), (c5, s5), (c6, s6), (c7, s7) = u
    even, odd = c0 + c8, c0 - c8
    ee = [even + c4, odd + s4, even - c4, odd - s4]
    m, p = ROOT * (c2 - c6), ROOT * (s2 + s6)
    eo = [c2 + c6, p + m, s2 - s6, p - m]
    e = [ee[n] + eo[n] for n in range(4)] + [ee[n] - eo[n] for n in range(4)]
    c17, c35, m17, m35 = c1 + c7, c3 + c5, c1 - c7, c3 - c5
    s17, s35, n17, n35 = s1 + s7, s3 + s5, s1 - s7, s3 - s5
    t1, r1 = BIG * m17 + SMALL * m35, SMALL * s17 + BIG * s35
    t2, r2 = ROOT * (c17 - c35), ROOT * (n17 + n35)
    t3, r3 = SMALL * m17 - BIG * m35, BIG * s17 - SMALL * s35
    o = [c17 + c35, r1 + t1, r2 + t2, r3 + t3, n17 - n35, r3 - t3, r2 - t2, r1 - t1]
    return [e[n] + o[n] for n in range(8)] + [e[n] - o[n] for n in range(8)]


def wave_groups(half):
    groups = []
    for g in range(STEPS // 2):
        orders = [0, 8] if g == 0 else [v for v in (g, STEPS - g) if v <= half]
        rows = []
        for order in orders:
            if order < half:
                rows.append((0, order, order))
            if order > 0:
                rows.append((1, order - 1, order))
        groups.append(rows)
    return groups


def wave_table(total, count, half, channels):
    fine = 128 // channels
    tables = []
    for d in range(count):
        rows = []
        for g, group in enumerate(wave_groups(half)):
            for sine, _, order in group:
                angle = 2 * np.pi * order * (count * np.arange(fine) + d) / total
                size = np.sqrt((1.0 if order == 0 else 2.0) / total)
                cos, sin = size * np.cos(angle), size * np.sin(angle)
                sign = 1.0 if order == g else -1.0
                first, last = (sin, sign * cos) if sine else (cos, -sign * sin)
                if g == 0:
                    zero = np.zeros(fine)
                    first, last = (first, zero) if order == 0 else (zero, first)
                rows.append(np.repeat(np.concatenate([first, last]), channels))
        tables.append(np.stack(rows))
    return np.stack(tables)


class Plan:
    def __init__(self, mesh, arg_shape, channels):
        self.nlon, self.nlat, self.nlead = (mesh.shape[n] for n in ("lon", "lat", "lead"))
        nz, ny, merged = arg_shape
        self.c = channels
        self.zl, self.yl = nz // self.nlead, ny // self.nlat
        self.nx = merged // channels
        self.xl = self.nx // self.nlon
        self.kp = MX // (self.nlon * self.nlat)
        self.kc = self.kp * channels
        self.lq = MY * MZ
        self.zy = self.zl * self.yl
        self.gain = math.sqrt(self.nx * ny * nz / MODES)
        eye_z, eye_l = np.eye(self.zl), np.eye(MY)
        by, bz = host_basis(ny, MY), host_basis(nz, MZ)
        c = channels
        self.groups = wave_groups(MX // 2)
        self.lon_table = halves(wave_table(self.nx, self.nlon, MX // 2, c)).transpose(1, 0, 2, 3)
        by_p = by.reshape(MY, self.nlat, self.yl)
        bz_s = bz.reshape(MZ, self.nlead, self.zl)
        eye_fz = np.eye(2 * self.zl)
        self.lat_table = halves(
            np.stack([np.kron(eye_fz, by_p[:, p]) for p in range(self.nlat)])
        )
        lead = np.einsum("qsz,lm->slqzm", bz_s, eye_l)
        self.lead_table = halves(lead.reshape(self.nlead, self.lq, self.zl * MY))
        self.lead_back = halves(
            lead.transpose(0, 3, 4, 1, 2).reshape(self.nlead, self.zl * MY, self.lq)
        )
        back = np.einsum("lpy,zw->pzywl", by_p, eye_z)
        self.lat_back = halves(back.reshape(self.nlat * self.zy, self.zl * MY))
        cc = c * c
        groups = 128 // c
        self.tile = np.concatenate(
            [np.kron(np.eye(groups)[:, [k]], np.tile(np.eye(c), (1, groups))) for k in range(groups)],
            axis=1,
        ).astype(ml_dtypes.bfloat16)
        wide = 256 // c
        self.fan = np.tile(np.eye(c), (1, wide)).astype(np.float32)
        self.block = np.kron(np.eye(wide), np.ones((c, c))).astype(np.float32)
        self.cc = cc


def remote_kernel(
    plan, act_h, pre_h, cot_h, weight, lw_h, lon_h, lat_th, lead_th, lead_bh, lat_bh, tile_h, fan_h, block_h,
    product, h_out, loc_out, tt,
    act, pre, cot, lw, lon_t, lat_t, lead_t, lead_b, lat_b, tile, fan, block,
    modes_out, xg, gs, spread, sbuf, lonbuf, latsend, latrecv, leadbuf, wbuf, vbuf,
    in_sem, wsem, lon_s, lon_r, lat_s, lat_r, lead_s, lead_r, g_s, g_r, v_s, v_r, f_s, f_r,
):
    pn = plan
    lon, lat, lead = (lax.axis_index(n) for n in ("lon", "lat", "lead"))
    mesh_id = pl.DeviceIdType.MESH
    other = 1 - lon
    barrier = pltpu.get_barrier_semaphore()
    pl.semaphore_signal(barrier, inc=1, device_id={"lon": other}, device_id_type=mesh_id)
    loads = []
    pairs = (
        (lon_h.at[lon], lon_t), (pre_h, pre), (cot_h, cot), (act_h, act), (lw_h, lw), (fan_h, fan),
        (block_h, block), (lat_th, lat_t), (lead_th, lead_t), (lead_bh, lead_b), (lat_bh, lat_b), (tile_h, tile),
    )
    for n, (source, target) in enumerate(pairs):
        copy = pltpu.make_async_copy(source, target, in_sem.at[n])
        copy.start()
        loads.append(copy)
        if n == 3:
            for d in range(1, pn.nlat):
                pl.semaphore_signal(
                    barrier, inc=1, device_id={"lat": lax.rem(lat + d, pn.nlat)}, device_id_type=mesh_id
                )
            for d in range(1, pn.nlead):
                pl.semaphore_signal(
                    barrier, inc=1, device_id={"lead": lax.rem(lead + d, pn.nlead)}, device_id_type=mesh_id
                )
    wcopy = pltpu.make_async_copy(
        weight.at[pl.ds(pl.multiple_of(lat * (pn.kp * pn.lq), 8), pn.kp * pn.lq), :], wbuf, wsem
    )
    c = pn.c
    zy = pn.zy
    lanes = lax.broadcasted_iota(jnp.int32, (c, 256), 1) % c
    mask = jnp.where(lanes == lax.broadcasted_iota(jnp.int32, (c, 256), 0), 1.0, 0.0).astype(BF16)
    loads[0].wait()
    for k in range(MX):
        for h in range(2):
            tt[h, k * c : (k + 1) * c, :] = lon_t[h, k : k + 1, :] * mask

    def spans(field, first):
        for n, (one, two) in enumerate(waves16(field)):
            for m, value in enumerate((one, two)):
                high, low = cut(value)
                xg[n, first : first + zy, m * 128 : (m + 1) * 128] = high
                xg[n, first + 2 * zy : first + 3 * zy, m * 128 : (m + 1) * 128] = low

    loads[1].wait()
    loads[2].wait()
    columns = []
    for n in range(STEPS):
        cols = slice(n * 128, (n + 1) * 128)
        v = pre[:, cols].astype(F32)
        cdf = 0.5 * (1.0 + lax.erf(v * (1.0 / math.sqrt(2.0))))
        density = jnp.exp(-0.5 * v * v) * (1.0 / math.sqrt(2.0 * math.pi))
        grad = cot[:, cols].astype(F32) * (cdf + v * density)
        gh, gl = cut(grad)
        gs[0, :, cols] = gh
        gs[1, :, cols] = gl
        columns.append(grad)
    spans(columns, zy)
    loads[3].wait()
    wcopy.start()
    spans([act[:, n * 128 : (n + 1) * 128].astype(F32) for n in range(STEPS)], 0)
    first = 0
    for n, rows in enumerate(pn.groups):
        part = slice(first, first + c * len(rows))
        p = mm(tt[0, part, :], xg[n], NT)
        q = mm(tt[1, part, :], xg[n, 0 : 2 * zy], NT)
        total = p[:, 0 : 2 * zy] + p[:, 2 * zy :] + q
        for m, (who, place, _) in enumerate(rows):
            sbuf[who, place * c : (place + 1) * c, :] = total[m * c : (m + 1) * c]
        first += c * len(rows)
    pl.semaphore_wait(barrier, 1 + (pn.nlat - 1) + (pn.nlead - 1))
    lon_copy = pltpu.make_async_remote_copy(
        src_ref=sbuf.at[other], dst_ref=lonbuf, send_sem=lon_s, recv_sem=lon_r,
        device_id={"lon": other}, device_id_type=mesh_id,
    )
    lon_copy.start()
    for copy in loads[4:]:
        copy.wait()
    lon_copy.wait()
    lat_copies = []
    for d in list(range(1, pn.nlat)) + [0]:
        p = lax.rem(lat + d, pn.nlat)
        rows = pl.ds(pl.multiple_of(p * pn.kc, pn.kc), pn.kc)
        value = sbuf[lon, rows, :] + lonbuf[rows, :]
        if d == 0:
            latrecv[lat] = value
        else:
            latsend[d - 1] = value
            copy = pltpu.make_async_remote_copy(
                src_ref=latsend.at[d - 1], dst_ref=latrecv.at[lat],
                send_sem=lat_s.at[d - 1], recv_sem=lat_r.at[d - 1],
                device_id={"lat": p}, device_id_type=mesh_id,
            )
            copy.start()
            lat_copies.append(copy)
    highest = lax.Precision.HIGHEST
    left = lax.dot_general(fan[...], lw[...], (((0,), (1,)), ((), ())), precision=highest, preferred_element_type=F32)
    both = jnp.dot(left, fan[...], precision=highest, preferred_element_type=F32) * block[...]
    bh, bl = cut(both)
    for t in range(pn.xl * c // 256):
        cols = slice(t * 256, (t + 1) * 256)
        hi, lo = gs[0, :, cols], gs[1, :, cols]
        loc_out[:, cols] = mm(hi, bh) + mm(lo, bh) + mm(hi, bl)
    for k in range(pn.kp + 1):
        spread[k] = placed((128, pn.cc), 1, c, k * c)
    for copy in lat_copies:
        copy.wait()
    total = None
    for p in range(pn.nlat):
        term = mm3((lat_t[0, p], lat_t[1, p]), latrecv[p], NT)
        total = term if total is None else total + term
    zm = pn.zl * MY
    lead_copies = {}
    for f in (1, 0):
        leadbuf[lead, f] = fold(total[f * zm : (f + 1) * zm, :])
        for d in range(1, pn.nlead):
            copy = pltpu.make_async_remote_copy(
                src_ref=leadbuf.at[lead, f], dst_ref=leadbuf.at[lead, f],
                send_sem=lead_s.at[f, d - 1], recv_sem=lead_r.at[f, d - 1],
                device_id={"lead": lax.rem(lead + d, pn.nlead)}, device_id_type=mesh_id,
            )
            copy.start()
            lead_copies[f, d] = copy
    g_copies = {}

    def finish_lead(f):
        for d in range(1, pn.nlead):
            lead_copies[f, d].wait()
        total = None
        for s in range(pn.nlead):
            term = mm3((lead_t[0, s], lead_t[1, s]), unfold(leadbuf[s, f]))
            total = term if total is None else total + term
        if f == 1:
            total = total * pn.gain
        modes_out[lat, f] = fold(total)
        for d in range(1, pn.nlat):
            copy = pltpu.make_async_remote_copy(
                src_ref=modes_out.at[lat, f], dst_ref=modes_out.at[lat, f],
                send_sem=g_s.at[f, d - 1], recv_sem=g_r.at[f, d - 1],
                device_id={"lat": lax.rem(lat + d, pn.nlat)}, device_id_type=mesh_id,
            )
            copy.start()
            g_copies[f, d] = copy
        return total

    spectral = finish_lead(1)
    wcopy.wait()
    sh, sl = cut(spectral)
    pick = tile[0 : pn.kc, 0 : pn.kp * 128]
    wide = mm(sh, pick) + mm(sl, pick)
    adjoint = None
    for k in range(pn.kp):
        four = wide[:, k * 128 : (k + 1) * 128]
        prod = wbuf[k * pn.lq : (k + 1) * pn.lq, :] * jnp.concatenate([four] * (pn.cc // 128), axis=1)
        ph, plow = cut(prod)
        pick = placed((pn.cc, pn.kc), 0, c, k * c)
        term = mm(ph, pick) + mm(plow, pick)
        adjoint = term if adjoint is None else adjoint + term
    mine = mm3((lead_b[0, lead], lead_b[1, lead]), adjoint)
    cells = mm3((lat_b[0], lat_b[1]), mine)
    for p in range(pn.nlat):
        vbuf[p] = fold(cells[p * zy : (p + 1) * zy, :])
    h_out[lon, lat] = vbuf[lat]
    v_copies = []
    for d in range(1, pn.nlat):
        p = lax.rem(lat + d, pn.nlat)
        copy = pltpu.make_async_remote_copy(
            src_ref=vbuf.at[p], dst_ref=h_out.at[lon, lat],
            send_sem=v_s.at[d - 1], recv_sem=v_r.at[d - 1],
            device_id={"lat": p}, device_id_type=mesh_id,
        )
        copy.start()
        v_copies.append(copy)
    finish_lead(0)

    def products(p):
        quarter = pn.lq // 4
        high, low = cut(modes_out[p, 0])
        sh, sl = cut(modes_out[p, 1])
        s4 = mm(sh, tile[...]) + mm(sl, tile[...])
        start = pl.multiple_of(p * (pn.kp * pn.lq), pn.kp * pn.lq)
        for k in range(pn.kp):
            part = slice(k * quarter, (k + 1) * quarter)
            whole = (slice(0, 3 * quarter), k, k * pn.lq)
            for source, which, offset in (whole, (part, pn.kp, k * pn.lq + 3 * quarter)):
                four = s4[source, which * 128 : (which + 1) * 128]
                two = jnp.concatenate([four, four], axis=1)
                rows = pl.ds(start + offset, four.shape[0])
                for j in range(pn.cc // 256):
                    cols = slice(j * 256, (j + 1) * 256)
                    table = spread[which, :, cols]
                    product[rows, cols] = (mm(high[source], table) + mm(low[source], table)) * two

    products(lat)
    f_copies = []
    for d in range(pn.nlat):
        if d > 0:
            v_copies[d - 1].wait_recv()
        s = lax.rem(lat + pn.nlat - d, pn.nlat)
        copy = pltpu.make_async_remote_copy(
            src_ref=h_out.at[lon, s], dst_ref=h_out.at[lon, s],
            send_sem=f_s.at[d], recv_sem=f_r.at[d],
            device_id={"lon": other}, device_id_type=mesh_id,
        )
        copy.start()
        f_copies.append(copy)
    for d in range(1, pn.nlat):
        for f in (1, 0):
            g_copies[f, d].wait_recv()
        products(lax.rem(lat + pn.nlat - d, pn.nlat))
    for copy in v_copies:
        copy.wait_send()
    for copy in f_copies:
        copy.wait()
    for copy in g_copies.values():
        copy.wait_send()


def finish_kernel(plan, product, h_in, loc, tt, grad_out, mode_grad, sem):
    pn = plan
    c = pn.c
    part = product.shape[0] // sem.shape[0]
    copies = []
    for n in range(sem.shape[0]):
        rows = slice(n * part, (n + 1) * part)
        copy = pltpu.make_async_copy(product.at[rows, :], mode_grad.at[rows, :], sem.at[n])
        copy.start()
        copies.append(copy)
    chunks = [[unfold(h_in[a, b]) for b in range(pn.nlat)] for a in range(pn.nlon)]
    waves = []
    first = 0
    for rows in pn.groups:
        part = slice(first, first + c * len(rows))
        pieces = []
        for who, place, _ in rows:
            at = place % pn.kp * c
            pieces.append(chunks[who][place // pn.kp][:, at : at + c])
        hh, hl = cut(jnp.concatenate(pieces, axis=1))
        wave = mm(hh, tt[0, part, :]) + mm(hl, tt[0, part, :]) + mm(hh, tt[1, part, :])
        waves.append((wave[:, :128], wave[:, 128:]))
        first += c * len(rows)
    for n, value in enumerate(cells16(waves)):
        cols = slice(n * 128, (n + 1) * 128)
        grad_out[:, cols] = (loc[:, cols] + value).astype(BF16)
    for copy in copies:
        copy.wait()


def fast_device(plan, activation, pre_activation, cotangent, mode_weight, local_weight):
    pn = plan
    merged = activation.shape[2]
    flat = [v.reshape(pn.zy, merged) for v in (activation, pre_activation, cotangent)]
    vm = pl.BlockSpec(memory_space=pltpu.VMEM)
    hbm = pl.BlockSpec(memory_space=pltpu.HBM)
    half = MX // pn.nlon * pn.c
    dma = pltpu.SemaphoreType.DMA
    tables = (
        pn.lon_table, pn.lat_table, pn.lead_table, pn.lead_back, pn.lat_back, pn.tile, pn.fan, pn.block,
    )
    modes = pn.nlat * pn.kp * pn.lq
    product, h, loc, tt = pl.pallas_call(
        functools.partial(remote_kernel, pn),
        out_shape=(
            pltpu.VMEM((modes, pn.cc), F32),
            pltpu.VMEM((pn.nlon, pn.nlat, pn.zy // 4 * 3, 128), F32),
            pltpu.VMEM((pn.zy, merged), F32),
            pltpu.VMEM((2, MX * pn.c, 256), BF16),
        ),
        in_specs=[hbm] * 13,
        out_specs=(vm,) * 4,
        scratch_shapes=[
            pltpu.VMEM((pn.zy, merged), BF16),
            pltpu.VMEM((pn.zy, merged), BF16),
            pltpu.VMEM((pn.zy, merged), BF16),
            pltpu.VMEM(local_weight.shape, F32),
            pltpu.VMEM(pn.lon_table.shape[1:], BF16),
        ]
        + [pltpu.VMEM(v.shape, v.dtype) for v in tables[1:]]
        + [
            pltpu.VMEM((pn.nlat, 2, pn.lq // 4 * 3, 128), F32),
            pltpu.VMEM((STEPS // 2, 4 * pn.zy, 256), BF16),
            pltpu.VMEM((2, pn.zy, merged), BF16),
            pltpu.VMEM((pn.kp + 1, 128, pn.cc), BF16),
            pltpu.VMEM((pn.nlon, half, 2 * pn.zy), F32),
            pltpu.VMEM((half, 2 * pn.zy), F32),
            pltpu.VMEM((pn.nlat - 1, pn.kc, 2 * pn.zy), F32),
            pltpu.VMEM((pn.nlat, pn.kc, 2 * pn.zy), F32),
            pltpu.VMEM((pn.nlead, 2, pn.zl * MY // 4 * 3, 128), F32),
            pltpu.VMEM((pn.kp * pn.lq, pn.cc), F32),
            pltpu.VMEM((pn.nlat, pn.zy // 4 * 3, 128), F32),
            dma((12,)), dma, dma, dma,
            dma((pn.nlat - 1,)), dma((pn.nlat - 1,)),
            dma((2, pn.nlead - 1)), dma((2, pn.nlead - 1)),
            dma((2, pn.nlat - 1)), dma((2, pn.nlat - 1)),
            dma((pn.nlat - 1,)), dma((pn.nlat - 1,)),
            dma((pn.nlat,)), dma((pn.nlat,)),
        ],
        compiler_params=pltpu.CompilerParams(
            collective_id=0, has_side_effects=True, vmem_limit_bytes=52 * 2**20
        ),
        name="modes",
    )(*flat, mode_weight, local_weight, *tables)
    grad, mode_grad = pl.pallas_call(
        functools.partial(finish_kernel, pn),
        out_shape=(
            jax.ShapeDtypeStruct((pn.zy, merged), BF16),
            jax.ShapeDtypeStruct((modes, pn.cc), F32),
        ),
        in_specs=[vm] * 4,
        out_specs=(vm, hbm),
        scratch_shapes=[dma((8,))],
        compiler_params=pltpu.CompilerParams(vmem_limit_bytes=16 * 2**20),
        name="finish",
    )(product, h, loc, tt)
    return grad.reshape(activation.shape), mode_grad


def solution(mesh):
    in_specs = (
        P("lead", "lat", "lon"),
        P("lead", "lat", "lon"),
        P("lead", "lat", "lon"),
        P("lon", None),
        P(),
    )
    out_specs = (P("lead", "lat", "lon"), P("lon", None))

    def whole(*args):
        shape = args[0].shape
        channels = args[4].shape[0]
        body = on_device
        if (
            mesh.shape["lon"] == 2
            and MX % (mesh.shape["lon"] * mesh.shape["lat"]) == 0
            and MX * MY * MZ == args[3].shape[0]
            and shape[2] == mesh.shape["lon"] * STEPS * 128
            and 4 * channels == 128
            and MX * channels == 96 * mesh.shape["lon"] * mesh.shape["lat"]
            and mesh.shape["lead"] * 4 == shape[0]
        ):
            body = functools.partial(fast_device, Plan(mesh, shape, channels))
        return jax.shard_map(
            body, mesh=mesh, in_specs=in_specs, out_specs=out_specs, check_vma=False
        )(*args)

    return whole
```

```python
import functools
import math

import jax
import jax.numpy as jnp
import ml_dtypes
import numpy as np
from jax import lax
from jax.experimental import pallas as pl
from jax.experimental.pallas import tpu as pltpu
from jax.sharding import PartitionSpec as P

MX = 24
MY = 24
MZ = 8
MODES = 4608


def make_basis(length, modes, start, count, stride):
    half = modes // 2
    order = jnp.arange(modes, dtype=jnp.int32)
    freq = jnp.where(order < half, order, order - half + 1)
    cells = start + stride * jnp.arange(count, dtype=jnp.int32)
    turns = freq[:, None] * cells[None, :] % length
    angle = 2.0 * math.pi / length * turns.astype(jnp.float32)
    waves = jnp.where(order[:, None] < half, jnp.cos(angle), jnp.sin(angle))
    weights = jnp.where(
        order == 0, jnp.float32(math.sqrt(1.0 / length)), jnp.float32(math.sqrt(2.0 / length))
    )
    return waves * weights[:, None]


def gelu_slope(value):
    normal_cdf = 0.5 * (1.0 + jax.scipy.special.erf(value / math.sqrt(2.0)))
    density = jnp.exp(-0.5 * value * value) / math.sqrt(2.0 * math.pi)
    return normal_cdf + value * density


def back_cells(coeffs, lon_basis, lat_basis, lead_basis):
    highest = lax.Precision.HIGHEST
    blocks = coeffs.reshape(
        lon_basis.shape[0], lat_basis.shape[0], lead_basis.shape[0], coeffs.shape[-1]
    )
    step = jnp.einsum("klqc,qz->zklc", blocks, lead_basis, precision=highest)
    step = jnp.einsum("zklc,ly->zykc", step, lat_basis, precision=highest)
    return jnp.einsum("zykc,kx->zyxc", step, lon_basis, precision=highest)


def on_device(activation, pre_activation, cotangent, mode_weight, local_weight):
    highest = lax.Precision.HIGHEST
    channels = local_weight.shape[0]
    lead_cells, lat_cells, merged = activation.shape
    lon_cells = merged // channels
    lon_count = lax.axis_size("lon")
    lon_total = lon_cells * lon_count
    lat_total = lat_cells * lax.axis_size("lat")
    lead_total = lead_cells * lax.axis_size("lead")
    lon_basis = make_basis(lon_total, MX, lax.axis_index("lon"), lon_cells, lon_count)
    lat_basis = make_basis(lat_total, MY, lax.axis_index("lat") * lat_cells, lat_cells, 1)
    lead_basis = make_basis(lead_total, MZ, lax.axis_index("lead") * lead_cells, lead_cells, 1)
    shape4 = (lead_cells, lat_cells, lon_cells, channels)
    grad_pre = cotangent.astype(jnp.float32).reshape(shape4) * gelu_slope(
        pre_activation.astype(jnp.float32).reshape(shape4)
    )
    stacked = jnp.concatenate([activation.astype(jnp.float32).reshape(shape4), grad_pre], axis=3)
    doubled = 2 * channels
    along_lon = jnp.einsum("zyxc,kx->zykc", stacked, lon_basis, precision=highest)
    along_lat = jnp.einsum("zykc,ly->zklc", along_lon, lat_basis, precision=highest)
    partial_sum = jnp.einsum("zklc,qz->klqc", along_lat, lead_basis, precision=highest).reshape(
        -1, doubled
    )
    summed = lax.psum(partial_sum, ("lat", "lead"))
    owned = lax.psum_scatter(summed, "lon", scatter_dimension=0, tiled=True)
    gain = math.sqrt(lon_total * lat_total * lead_total / MODES)
    coef = owned[:, :channels]
    spectral = gain * owned[:, channels:]
    owned_count = owned.shape[0]
    mode_grad = (coef[:, :, None] * spectral[:, None, :]).reshape(owned_count, channels * channels)
    mixing = mode_weight.reshape(owned_count, channels, channels)
    owned_adjoint = jnp.sum(mixing * spectral[:, None, :], axis=2)
    every_mode = lax.all_gather(owned_adjoint, "lon", axis=0, tiled=True)
    spread = back_cells(every_mode, lon_basis, lat_basis, lead_basis)
    local = jnp.einsum("zyxo,io->zyxi", grad_pre, local_weight, precision=highest)
    input_grad = (spread + local).reshape(lead_cells, lat_cells, merged)
    return (input_grad.astype(jnp.bfloat16), mode_grad)


F32 = jnp.float32
BF16 = jnp.bfloat16


def host_basis(length, modes):
    half = modes // 2
    order = np.arange(modes)
    freq = np.where(order < half, order, order - half + 1)
    turns = (freq[:, None] * np.arange(length)[None, :]) % length
    angle = 2.0 * np.pi / length * turns
    waves = np.where(order[:, None] < half, np.cos(angle), np.sin(angle))
    weights = np.where(order == 0, np.sqrt(1.0 / length), np.sqrt(2.0 / length))
    return waves * weights[:, None]


def halves(table):
    table = np.asarray(table, np.float32)
    high = table.astype(ml_dtypes.bfloat16)
    low = (table - high.astype(np.float32)).astype(ml_dtypes.bfloat16)
    return np.stack([high, low])


def cut(value):
    high = value.astype(BF16)
    return high, (value - high.astype(F32)).astype(BF16)


NN = (((1,), (0,)), ((), ()))
NT = (((1,), (1,)), ((), ()))


def mm(a, b, dims=NN):
    return lax.dot_general(a, b, dims, preferred_element_type=F32)


def mm3(table, b, dims=NN):
    bh, bl = cut(b)
    return mm(table[0], bh, dims) + mm(table[0], bl, dims) + mm(table[1], bh, dims)


def placed(shape, axis, channels, base):
    wide = lax.broadcasted_iota(jnp.int32, shape, axis) // channels
    narrow = lax.broadcasted_iota(jnp.int32, shape, 1 - axis) - base
    return jnp.where(wide == narrow, 1.0, 0.0).astype(BF16)


def fold(value):
    r, lanes = value.shape[0] // 4, value.shape[1] // 3
    last = jnp.concatenate([value[3 * r :, g * lanes : (g + 1) * lanes] for g in range(3)], axis=0)
    return jnp.concatenate([value[: 3 * r], last], axis=1)


def unfold(value):
    r, lanes = value.shape[0] // 3, value.shape[1] // 4
    last = jnp.concatenate([value[g * r : (g + 1) * r, 3 * lanes :] for g in range(3)], axis=1)
    return jnp.concatenate([value[:, : 3 * lanes], last], axis=0)


STEPS = 16
ROOT, BIG, SMALL = (float(np.cos(np.pi / v)) for v in (4, 8, 8 / 3))


def waves16(x):
    e = [x[n] + x[n + 8] for n in range(8)]
    o = [x[n] - x[n + 8] for n in range(8)]
    ee = [e[n] + e[n + 4] for n in range(4)]
    eo = [e[n] - e[n + 4] for n in range(4)]
    even, odd = ee[0] + ee[2], ee[1] + ee[3]
    minus, plus = ROOT * (eo[1] - eo[3]), ROOT * (eo[1] + eo[3])
    d1, d2, d3 = o[1] - o[7], ROOT * (o[2] - o[6]), o[3] - o[5]
    s1, s2, s3 = o[1] + o[7], ROOT * (o[2] + o[6]), o[3] + o[5]
    a, b = BIG * d1 + SMALL * d3, SMALL * d1 - BIG * d3
    g, h = SMALL * s1 + BIG * s3, BIG * s1 - SMALL * s3
    up, down = o[0] + d2, o[0] - d2
    high, low = o[4] + s2, o[4] - s2
    return [
        (even + odd, even - odd),
        (up + a, high + g),
        (eo[0] + minus, plus + eo[2]),
        (down + b, h - low),
        (ee[0] - ee[2], ee[1] - ee[3]),
        (down - b, h + low),
        (eo[0] - minus, plus - eo[2]),
        (up - a, g - high),
    ]


def cells16(u):
    (c0, c8), (c1, s1), (c2, s2), (c3, s3), (c4, s4), (c5, s5), (c6, s6), (c7, s7) = u
    even, odd = c0 + c8, c0 - c8
    ee = [even + c4, odd + s4, even - c4, odd - s4]
    m, p = ROOT * (c2 - c6), ROOT * (s2 + s6)
    eo = [c2 + c6, p + m, s2 - s6, p - m]
    e = [ee[n] + eo[n] for n in range(4)] + [ee[n] - eo[n] for n in range(4)]
    c17, c35, m17, m35 = c1 + c7, c3 + c5, c1 - c7, c3 - c5
    s17, s35, n17, n35 = s1 + s7, s3 + s5, s1 - s7, s3 - s5
    t1, r1 = BIG * m17 + SMALL * m35, SMALL * s17 + BIG * s35
    t2, r2 = ROOT * (c17 - c35), ROOT * (n17 + n35)
    t3, r3 = SMALL * m17 - BIG * m35, BIG * s17 - SMALL * s35
    o = [c17 + c35, r1 + t1, r2 + t2, r3 + t3, n17 - n35, r3 - t3, r2 - t2, r1 - t1]
    return [e[n] + o[n] for n in range(8)] + [e[n] - o[n] for n in range(8)]


def wave_groups(half):
    groups = []
    for g in range(STEPS // 2):
        orders = [0, 8] if g == 0 else [v for v in (g, STEPS - g) if v <= half]
        rows = []
        for order in orders:
            if order < half:
                rows.append((0, order, order))
            if order > 0:
                rows.append((1, order - 1, order))
        groups.append(rows)
    return groups


def wave_table(total, count, half, channels):
    fine = 128 // channels
    tables = []
    for d in range(count):
        rows = []
        for g, group in enumerate(wave_groups(half)):
            for sine, _, order in group:
                angle = 2 * np.pi * order * (count * np.arange(fine) + d) / total
                size = np.sqrt((1.0 if order == 0 else 2.0) / total)
                cos, sin = size * np.cos(angle), size * np.sin(angle)
                sign = 1.0 if order == g else -1.0
                first, last = (sin, sign * cos) if sine else (cos, -sign * sin)
                if g == 0:
                    zero = np.zeros(fine)
                    first, last = (first, zero) if order == 0 else (zero, first)
                rows.append(np.repeat(np.concatenate([first, last]), channels))
        tables.append(np.stack(rows))
    return np.stack(tables)


class Plan:
    def __init__(self, mesh, arg_shape, channels):
        self.nlon, self.nlat, self.nlead = (mesh.shape[n] for n in ("lon", "lat", "lead"))
        nz, ny, merged = arg_shape
        self.c = channels
        self.zl, self.yl = nz // self.nlead, ny // self.nlat
        self.nx = merged // channels
        self.xl = self.nx // self.nlon
        self.kp = MX // (self.nlon * self.nlat)
        self.kc = self.kp * channels
        self.lq = MY * MZ
        self.zy = self.zl * self.yl
        self.gain = math.sqrt(self.nx * ny * nz / MODES)
        eye_z, eye_l = np.eye(self.zl), np.eye(MY)
        by, bz = host_basis(ny, MY), host_basis(nz, MZ)
        c = channels
        self.groups = wave_groups(MX // 2)
        self.lon_table = halves(wave_table(self.nx, self.nlon, MX // 2, c)).transpose(1, 0, 2, 3)
        by_p = by.reshape(MY, self.nlat, self.yl)
        bz_s = bz.reshape(MZ, self.nlead, self.zl)
        self.lat_table = halves(
            np.einsum("lpy,zw->zlpwy", by_p, eye_z).reshape(self.zl * MY, self.nlat * self.zy)
        )
        lead = np.einsum("qsz,lm->slqzm", bz_s, eye_l)
        self.lead_table = halves(
            lead.reshape(self.nlead, self.lq, self.zl * MY).transpose(1, 0, 2).reshape(self.lq, -1)
        )
        self.lead_back = halves(
            lead.transpose(0, 3, 4, 1, 2).reshape(self.nlead, self.zl * MY, self.lq)
        )
        back = np.einsum("lpy,zw->pzywl", by_p, eye_z)
        self.lat_back = halves(back.reshape(self.nlat * self.zy, self.zl * MY))
        cc = c * c
        groups = 128 // c
        self.tile = np.concatenate(
            [np.kron(np.eye(groups)[:, [k]], np.tile(np.eye(c), (1, groups))) for k in range(groups)],
            axis=1,
        ).astype(ml_dtypes.bfloat16)
        wide = 256 // c
        self.fan = np.tile(np.eye(c), (1, wide)).astype(np.float32)
        self.block = np.kron(np.eye(wide), np.ones((c, c))).astype(np.float32)
        self.cc = cc


def products(plan, modes, tile, spread, product):
    pn = plan
    quarter = pn.lq // 4
    high, low = cut(modes[0])
    sh, sl = cut(modes[1])
    s4 = mm(sh, tile[...]) + mm(sl, tile[...])
    for k in range(pn.kp):
        part = slice(k * quarter, (k + 1) * quarter)
        whole = (slice(0, 3 * quarter), k, k * pn.lq)
        for source, which, offset in (whole, (part, pn.kp, k * pn.lq + 3 * quarter)):
            four = s4[source, which * 128 : (which + 1) * 128]
            two = jnp.concatenate([four, four], axis=1)
            rows = slice(offset, offset + four.shape[0])
            for j in range(pn.cc // 256):
                cols = slice(j * 256, (j + 1) * 256)
                table = spread[which, :, cols]
                product[rows, cols] = (mm(high[source], table) + mm(low[source], table)) * two


def remote_kernel(
    plan, act_h, pre_h, cot_h, weight, lw_h, lon_h, lat_th, lead_th, lead_bh, lat_bh, tile_h, fan_h, block_h,
    product, modes_out, h_out, loc_out, tt, tile, spread,
    act, pre, cot, lw, lon_t, lat_t, lead_t, lead_b, lat_b, fan, block,
    xg, gs, sbuf, lonbuf, latsend, latrecv, leadbuf, wbuf, vbuf,
    in_sem, wsem, lon_s, lon_r, lat_s, lat_r, lead_s, lead_r, g_s, g_r, v_s, v_r, f_s, f_r,
):
    pn = plan
    lon, lat, lead = (lax.axis_index(n) for n in ("lon", "lat", "lead"))
    mesh_id = pl.DeviceIdType.MESH
    other = 1 - lon
    barrier = pltpu.get_barrier_semaphore()
    pl.semaphore_signal(barrier, inc=1, device_id={"lon": other}, device_id_type=mesh_id)
    loads = []
    pairs = (
        (lon_h.at[lon], lon_t), (pre_h, pre), (cot_h, cot), (act_h, act), (lw_h, lw), (fan_h, fan),
        (block_h, block), (lat_th, lat_t), (lead_th, lead_t), (lead_bh, lead_b), (lat_bh, lat_b), (tile_h, tile),
    )
    for n, (source, target) in enumerate(pairs):
        copy = pltpu.make_async_copy(source, target, in_sem.at[n])
        copy.start()
        loads.append(copy)
        if n == 3:
            for d in range(1, pn.nlat):
                pl.semaphore_signal(
                    barrier, inc=1, device_id={"lat": lax.rem(lat + d, pn.nlat)}, device_id_type=mesh_id
                )
            for d in range(1, pn.nlead):
                pl.semaphore_signal(
                    barrier, inc=1, device_id={"lead": lax.rem(lead + d, pn.nlead)}, device_id_type=mesh_id
                )
    wcopy = pltpu.make_async_copy(
        weight.at[pl.ds(pl.multiple_of(lat * (pn.kp * pn.lq), 8), pn.kp * pn.lq), :], wbuf, wsem
    )
    c = pn.c
    zy = pn.zy
    lanes = lax.broadcasted_iota(jnp.int32, (c, 256), 1) % c
    mask = jnp.where(lanes == lax.broadcasted_iota(jnp.int32, (c, 256), 0), 1.0, 0.0).astype(BF16)
    loads[0].wait()
    for k in range(MX):
        for h in range(2):
            tt[h, k * c : (k + 1) * c, :] = lon_t[h, k : k + 1, :] * mask

    lon_copies = {}

    def along_lon(f, field):
        for n, (one, two) in enumerate(waves16(field)):
            for m, value in enumerate((one, two)):
                high, low = cut(value)
                xg[f, n, 0:zy, m * 128 : (m + 1) * 128] = high
                xg[f, n, zy : 2 * zy, m * 128 : (m + 1) * 128] = low
        first = 0
        deep = pn.kc // 2
        for n, rows in enumerate(pn.groups):
            part = slice(first, first + c * len(rows))
            p = mm(tt[0, part, :], xg[f, n], NT)
            q = mm(tt[1, part, :], xg[f, n, 0:zy], NT)
            total = p[:, 0:zy] + p[:, zy:] + q
            for m, (who, place, _) in enumerate(rows):
                base = place // pn.kp * deep
                for piece in range(0, c, 16):
                    at = place % pn.kp * c + piece
                    side = at // deep
                    sbuf[f, who, base + at - side * deep : base + at - side * deep + 16, side * zy : (side + 1) * zy] = (
                        total[m * c + piece : m * c + piece + 16]
                    )
            first += c * len(rows)
        if f == 1:
            pl.semaphore_wait(barrier, 1 + (pn.nlat - 1) + (pn.nlead - 1))
        copy = pltpu.make_async_remote_copy(
            src_ref=sbuf.at[f, other], dst_ref=lonbuf.at[f], send_sem=lon_s.at[f], recv_sem=lon_r.at[f],
            device_id={"lon": other}, device_id_type=mesh_id,
        )
        copy.start()
        lon_copies[f] = copy

    lat_copies = {}

    def send_lat(f):
        lon_copies[f].wait()
        deep = pn.kc // 2
        for d in list(range(1, pn.nlat)) + [0]:
            p = lax.rem(lat + d, pn.nlat)
            rows = pl.ds(pl.multiple_of(p * deep, deep), deep)
            value = sbuf[f, lon, rows, :] + lonbuf[f, rows, :]
            if d == 0:
                latrecv[f, lat] = value
            else:
                latsend[f, d - 1] = value
                copy = pltpu.make_async_remote_copy(
                    src_ref=latsend.at[f, d - 1], dst_ref=latrecv.at[f, lat],
                    send_sem=lat_s.at[f, d - 1], recv_sem=lat_r.at[f, d - 1],
                    device_id={"lat": p}, device_id_type=mesh_id,
                )
                copy.start()
                lat_copies[f, d] = copy

    loads[1].wait()
    loads[2].wait()
    columns = []
    for n in range(STEPS):
        cols = slice(n * 128, (n + 1) * 128)
        v = pre[:, cols].astype(F32)
        cdf = 0.5 * (1.0 + lax.erf(v * (1.0 / math.sqrt(2.0))))
        density = jnp.exp(-0.5 * v * v) * (1.0 / math.sqrt(2.0 * math.pi))
        grad = cot[:, cols].astype(F32) * (cdf + v * density)
        gh, gl = cut(grad)
        gs[0, :, cols] = gh
        gs[1, :, cols] = gl
        columns.append(grad)
    along_lon(1, columns)
    loads[3].wait()
    wcopy.start()
    along_lon(0, [act[:, n * 128 : (n + 1) * 128].astype(F32) for n in range(STEPS)])
    send_lat(1)
    send_lat(0)
    for copy in loads[4:]:
        copy.wait()
    highest = lax.Precision.HIGHEST
    left = lax.dot_general(fan[...], lw[...], (((0,), (1,)), ((), ())), precision=highest, preferred_element_type=F32)
    both = jnp.dot(left, fan[...], precision=highest, preferred_element_type=F32) * block[...]
    bh, bl = cut(both)
    for t in range(pn.xl * c // 256):
        cols = slice(t * 256, (t + 1) * 256)
        hi, lo = gs[0, :, cols], gs[1, :, cols]
        loc_out[:, cols] = mm(hi, bh) + mm(lo, bh) + mm(hi, bl)
    for k in range(pn.kp + 1):
        spread[k] = placed((128, pn.cc), 1, c, k * c)
    lead_copies = {}

    def send_lead(f):
        for d in range(1, pn.nlat):
            lat_copies[f, d].wait()
        got = [latrecv[f, p] for p in range(pn.nlat)]
        wide = jnp.concatenate(
            [jnp.concatenate([v[:, side * zy : (side + 1) * zy] for v in got], axis=1) for side in range(2)], axis=0
        )
        leadbuf[lead, f] = fold(mm3((lat_t[0], lat_t[1]), wide, NT))
        for d in range(1, pn.nlead):
            copy = pltpu.make_async_remote_copy(
                src_ref=leadbuf.at[lead, f], dst_ref=leadbuf.at[lead, f],
                send_sem=lead_s.at[f, d - 1], recv_sem=lead_r.at[f, d - 1],
                device_id={"lead": lax.rem(lead + d, pn.nlead)}, device_id_type=mesh_id,
            )
            copy.start()
            lead_copies[f, d] = copy

    send_lead(1)
    send_lead(0)
    g_copies = {}

    def finish_lead(f):
        for d in range(1, pn.nlead):
            lead_copies[f, d].wait()
        got = jnp.concatenate([unfold(leadbuf[s, f]) for s in range(pn.nlead)], axis=0)
        total = mm3((lead_t[0], lead_t[1]), got)
        if f == 1:
            total = total * pn.gain
        modes_out[lat, f] = fold(total)
        for d in range(1, pn.nlat):
            copy = pltpu.make_async_remote_copy(
                src_ref=modes_out.at[lat, f], dst_ref=modes_out.at[lat, f],
                send_sem=g_s.at[f, d - 1], recv_sem=g_r.at[f, d - 1],
                device_id={"lat": lax.rem(lat + d, pn.nlat)}, device_id_type=mesh_id,
            )
            copy.start()
            g_copies[f, d] = copy
        return total

    spectral = finish_lead(1)
    wcopy.wait()
    sh, sl = cut(spectral)
    pick = tile[0 : pn.kc, 0 : pn.kp * 128]
    wide = mm(sh, pick) + mm(sl, pick)
    adjoint = None
    for k in range(pn.kp):
        four = wide[:, k * 128 : (k + 1) * 128]
        prod = wbuf[k * pn.lq : (k + 1) * pn.lq, :] * jnp.concatenate([four] * (pn.cc // 128), axis=1)
        ph, plow = cut(prod)
        pick = placed((pn.cc, pn.kc), 0, c, k * c)
        term = mm(ph, pick) + mm(plow, pick)
        adjoint = term if adjoint is None else adjoint + term
    mine = mm3((lead_b[0, lead], lead_b[1, lead]), adjoint)
    cells = mm3((lat_b[0], lat_b[1]), mine)
    for p in range(pn.nlat):
        vbuf[p] = fold(cells[p * zy : (p + 1) * zy, :])
    h_out[lon, lat] = vbuf[lat]
    v_copies = []
    for d in range(1, pn.nlat):
        p = lax.rem(lat + d, pn.nlat)
        copy = pltpu.make_async_remote_copy(
            src_ref=vbuf.at[p], dst_ref=h_out.at[lon, lat],
            send_sem=v_s.at[d - 1], recv_sem=v_r.at[d - 1],
            device_id={"lat": p}, device_id_type=mesh_id,
        )
        copy.start()
        v_copies.append(copy)
    finish_lead(0)

    products(pn, modes_out.at[lat], tile, spread, product)
    f_copies = []
    for d in range(pn.nlat):
        if d > 0:
            v_copies[d - 1].wait_recv()
        s = lax.rem(lat + pn.nlat - d, pn.nlat)
        copy = pltpu.make_async_remote_copy(
            src_ref=h_out.at[lon, s], dst_ref=h_out.at[lon, s],
            send_sem=f_s.at[d], recv_sem=f_r.at[d],
            device_id={"lon": other}, device_id_type=mesh_id,
        )
        copy.start()
        f_copies.append(copy)
    for copy in v_copies:
        copy.wait_send()
    for copy in f_copies:
        copy.wait()
    for copy in g_copies.values():
        copy.wait()


def finish_kernel(plan, product, modes, h_in, loc, tt, tile, spread, grad_out, mode_grad, buf, sem):
    pn = plan
    c = pn.c
    lat = lax.axis_index("lat")
    size = pn.kp * pn.lq
    copies = []

    def write(source, p, n):
        rows = pl.ds(pl.multiple_of(p * size, size), size)
        copy = pltpu.make_async_copy(source, mode_grad.at[rows, :], sem.at[n])
        copy.start()
        copies.append(copy)

    write(product, lat, 0)
    for d in range(1, pn.nlat):
        p = lax.rem(lat + d, pn.nlat)
        products(pn, modes.at[p], tile, spread, buf.at[d - 1])
        write(buf.at[d - 1], p, d)
    chunks = [[unfold(h_in[a, b]) for b in range(pn.nlat)] for a in range(pn.nlon)]
    waves = []
    first = 0
    for rows in pn.groups:
        part = slice(first, first + c * len(rows))
        pieces = []
        for who, place, _ in rows:
            at = place % pn.kp * c
            pieces.append(chunks[who][place // pn.kp][:, at : at + c])
        hh, hl = cut(jnp.concatenate(pieces, axis=1))
        wave = mm(hh, tt[0, part, :]) + mm(hl, tt[0, part, :]) + mm(hh, tt[1, part, :])
        waves.append((wave[:, :128], wave[:, 128:]))
        first += c * len(rows)
    for n, value in enumerate(cells16(waves)):
        cols = slice(n * 128, (n + 1) * 128)
        grad_out[:, cols] = (loc[:, cols] + value).astype(BF16)
    for copy in copies:
        copy.wait()


def fast_device(plan, activation, pre_activation, cotangent, mode_weight, local_weight):
    pn = plan
    merged = activation.shape[2]
    flat = [v.reshape(pn.zy, merged) for v in (activation, pre_activation, cotangent)]
    vm = pl.BlockSpec(memory_space=pltpu.VMEM)
    hbm = pl.BlockSpec(memory_space=pltpu.HBM)
    half = MX // pn.nlon * pn.c
    dma = pltpu.SemaphoreType.DMA
    tables = (
        pn.lon_table, pn.lat_table, pn.lead_table, pn.lead_back, pn.lat_back, pn.tile, pn.fan, pn.block,
    )
    size = pn.kp * pn.lq
    product, modes, h, loc, tt, tile, spread = pl.pallas_call(
        functools.partial(remote_kernel, pn),
        out_shape=(
            pltpu.VMEM((size, pn.cc), F32),
            pltpu.VMEM((pn.nlat, 2, pn.lq // 4 * 3, 128), F32),
            pltpu.VMEM((pn.nlon, pn.nlat, pn.zy // 4 * 3, 128), F32),
            pltpu.VMEM((pn.zy, merged), F32),
            pltpu.VMEM((2, MX * pn.c, 256), BF16),
            pltpu.VMEM(pn.tile.shape, BF16),
            pltpu.VMEM((pn.kp + 1, 128, pn.cc), BF16),
        ),
        in_specs=[hbm] * 13,
        out_specs=(vm,) * 7,
        scratch_shapes=[
            pltpu.VMEM((pn.zy, merged), BF16),
            pltpu.VMEM((pn.zy, merged), BF16),
            pltpu.VMEM((pn.zy, merged), BF16),
            pltpu.VMEM(local_weight.shape, F32),
            pltpu.VMEM(pn.lon_table.shape[1:], BF16),
        ]
        + [pltpu.VMEM(v.shape, v.dtype) for v in tables[1:5] + tables[6:]]
        + [
            pltpu.VMEM((2, STEPS // 2, 2 * pn.zy, 256), BF16),
            pltpu.VMEM((2, pn.zy, merged), BF16),
            pltpu.VMEM((2, pn.nlon, half // 2, 2 * pn.zy), F32),
            pltpu.VMEM((2, half // 2, 2 * pn.zy), F32),
            pltpu.VMEM((2, pn.nlat - 1, pn.kc // 2, 2 * pn.zy), F32),
            pltpu.VMEM((2, pn.nlat, pn.kc // 2, 2 * pn.zy), F32),
            pltpu.VMEM((pn.nlead, 2, pn.zl * MY // 4 * 3, 128), F32),
            pltpu.VMEM((pn.kp * pn.lq, pn.cc), F32),
            pltpu.VMEM((pn.nlat, pn.zy // 4 * 3, 128), F32),
            dma((12,)), dma, dma((2,)), dma((2,)),
            dma((2, pn.nlat - 1)), dma((2, pn.nlat - 1)),
            dma((2, pn.nlead - 1)), dma((2, pn.nlead - 1)),
            dma((2, pn.nlat - 1)), dma((2, pn.nlat - 1)),
            dma((pn.nlat - 1,)), dma((pn.nlat - 1,)),
            dma((pn.nlat,)), dma((pn.nlat,)),
        ],
        compiler_params=pltpu.CompilerParams(
            collective_id=0, has_side_effects=True, vmem_limit_bytes=52 * 2**20
        ),
        name="modes",
    )(*flat, mode_weight, local_weight, *tables)
    grad, mode_grad = pl.pallas_call(
        functools.partial(finish_kernel, pn),
        out_shape=(
            jax.ShapeDtypeStruct((pn.zy, merged), BF16),
            jax.ShapeDtypeStruct((pn.nlat * size, pn.cc), F32),
        ),
        in_specs=[vm] * 7,
        out_specs=(vm, hbm),
        scratch_shapes=[pltpu.VMEM((pn.nlat - 1, size, pn.cc), F32), dma((pn.nlat,))],
        compiler_params=pltpu.CompilerParams(vmem_limit_bytes=24 * 2**20),
        name="finish",
    )(product, modes, h, loc, tt, tile, spread)
    return grad.reshape(activation.shape), mode_grad


def solution(mesh):
    in_specs = (
        P("lead", "lat", "lon"),
        P("lead", "lat", "lon"),
        P("lead", "lat", "lon"),
        P("lon", None),
        P(),
    )
    out_specs = (P("lead", "lat", "lon"), P("lon", None))

    def whole(*args):
        shape = args[0].shape
        channels = args[4].shape[0]
        body = on_device
        if (
            mesh.shape["lon"] == 2
            and MX % (mesh.shape["lon"] * mesh.shape["lat"]) == 0
            and MX * MY * MZ == args[3].shape[0]
            and shape[2] == mesh.shape["lon"] * STEPS * 128
            and 4 * channels == 128
            and MX * channels == 96 * mesh.shape["lon"] * mesh.shape["lat"]
            and mesh.shape["lead"] * 4 == shape[0]
        ):
            body = functools.partial(fast_device, Plan(mesh, shape, channels))
        return jax.shard_map(
            body, mesh=mesh, in_specs=in_specs, out_specs=out_specs, check_vma=False
        )(*args)

    return whole
```

```python
import functools
import math

import jax
import jax.numpy as jnp
import ml_dtypes
import numpy as np
from jax import lax
from jax.experimental import pallas as pl
from jax.experimental.pallas import tpu as pltpu
from jax.sharding import PartitionSpec as P

MX = 24
MY = 24
MZ = 8
MODES = 4608


def make_basis(length, modes, start, count, stride):
    half = modes // 2
    order = jnp.arange(modes, dtype=jnp.int32)
    freq = jnp.where(order < half, order, order - half + 1)
    cells = start + stride * jnp.arange(count, dtype=jnp.int32)
    turns = freq[:, None] * cells[None, :] % length
    angle = 2.0 * math.pi / length * turns.astype(jnp.float32)
    waves = jnp.where(order[:, None] < half, jnp.cos(angle), jnp.sin(angle))
    weights = jnp.where(
        order == 0, jnp.float32(math.sqrt(1.0 / length)), jnp.float32(math.sqrt(2.0 / length))
    )
    return waves * weights[:, None]


def gelu_slope(value):
    normal_cdf = 0.5 * (1.0 + jax.scipy.special.erf(value / math.sqrt(2.0)))
    density = jnp.exp(-0.5 * value * value) / math.sqrt(2.0 * math.pi)
    return normal_cdf + value * density


def back_cells(coeffs, lon_basis, lat_basis, lead_basis):
    highest = lax.Precision.HIGHEST
    blocks = coeffs.reshape(
        lon_basis.shape[0], lat_basis.shape[0], lead_basis.shape[0], coeffs.shape[-1]
    )
    step = jnp.einsum("klqc,qz->zklc", blocks, lead_basis, precision=highest)
    step = jnp.einsum("zklc,ly->zykc", step, lat_basis, precision=highest)
    return jnp.einsum("zykc,kx->zyxc", step, lon_basis, precision=highest)


def on_device(activation, pre_activation, cotangent, mode_weight, local_weight):
    highest = lax.Precision.HIGHEST
    channels = local_weight.shape[0]
    lead_cells, lat_cells, merged = activation.shape
    lon_cells = merged // channels
    lon_count = lax.axis_size("lon")
    lon_total = lon_cells * lon_count
    lat_total = lat_cells * lax.axis_size("lat")
    lead_total = lead_cells * lax.axis_size("lead")
    lon_basis = make_basis(lon_total, MX, lax.axis_index("lon"), lon_cells, lon_count)
    lat_basis = make_basis(lat_total, MY, lax.axis_index("lat") * lat_cells, lat_cells, 1)
    lead_basis = make_basis(lead_total, MZ, lax.axis_index("lead") * lead_cells, lead_cells, 1)
    shape4 = (lead_cells, lat_cells, lon_cells, channels)
    grad_pre = cotangent.astype(jnp.float32).reshape(shape4) * gelu_slope(
        pre_activation.astype(jnp.float32).reshape(shape4)
    )
    stacked = jnp.concatenate([activation.astype(jnp.float32).reshape(shape4), grad_pre], axis=3)
    doubled = 2 * channels
    along_lon = jnp.einsum("zyxc,kx->zykc", stacked, lon_basis, precision=highest)
    along_lat = jnp.einsum("zykc,ly->zklc", along_lon, lat_basis, precision=highest)
    partial_sum = jnp.einsum("zklc,qz->klqc", along_lat, lead_basis, precision=highest).reshape(
        -1, doubled
    )
    summed = lax.psum(partial_sum, ("lat", "lead"))
    owned = lax.psum_scatter(summed, "lon", scatter_dimension=0, tiled=True)
    gain = math.sqrt(lon_total * lat_total * lead_total / MODES)
    coef = owned[:, :channels]
    spectral = gain * owned[:, channels:]
    owned_count = owned.shape[0]
    mode_grad = (coef[:, :, None] * spectral[:, None, :]).reshape(owned_count, channels * channels)
    mixing = mode_weight.reshape(owned_count, channels, channels)
    owned_adjoint = jnp.sum(mixing * spectral[:, None, :], axis=2)
    every_mode = lax.all_gather(owned_adjoint, "lon", axis=0, tiled=True)
    spread = back_cells(every_mode, lon_basis, lat_basis, lead_basis)
    local = jnp.einsum("zyxo,io->zyxi", grad_pre, local_weight, precision=highest)
    input_grad = (spread + local).reshape(lead_cells, lat_cells, merged)
    return (input_grad.astype(jnp.bfloat16), mode_grad)


F32 = jnp.float32
BF16 = jnp.bfloat16


def host_basis(length, modes):
    half = modes // 2
    order = np.arange(modes)
    freq = np.where(order < half, order, order - half + 1)
    turns = (freq[:, None] * np.arange(length)[None, :]) % length
    angle = 2.0 * np.pi / length * turns
    waves = np.where(order[:, None] < half, np.cos(angle), np.sin(angle))
    weights = np.where(order == 0, np.sqrt(1.0 / length), np.sqrt(2.0 / length))
    return waves * weights[:, None]


def halves(table):
    table = np.asarray(table, np.float32)
    high = table.astype(ml_dtypes.bfloat16)
    low = (table - high.astype(np.float32)).astype(ml_dtypes.bfloat16)
    return np.stack([high, low])


def cut(value):
    high = value.astype(BF16)
    return high, (value - high.astype(F32)).astype(BF16)


NN = (((1,), (0,)), ((), ()))
NT = (((1,), (1,)), ((), ()))


def mm(a, b, dims=NN):
    return lax.dot_general(a, b, dims, preferred_element_type=F32)


def mm3(table, b, dims=NN):
    bh, bl = cut(b)
    return mm(table[0], bh, dims) + mm(table[0], bl, dims) + mm(table[1], bh, dims)


def placed(shape, axis, channels, base):
    wide = lax.broadcasted_iota(jnp.int32, shape, axis) // channels
    narrow = lax.broadcasted_iota(jnp.int32, shape, 1 - axis) - base
    return jnp.where(wide == narrow, 1.0, 0.0).astype(BF16)


def fold(value):
    r, lanes = value.shape[0] // 4, value.shape[1] // 3
    last = jnp.concatenate([value[3 * r :, g * lanes : (g + 1) * lanes] for g in range(3)], axis=0)
    return jnp.concatenate([value[: 3 * r], last], axis=1)


def unfold(value):
    r, lanes = value.shape[0] // 3, value.shape[1] // 4
    last = jnp.concatenate([value[g * r : (g + 1) * r, 3 * lanes :] for g in range(3)], axis=1)
    return jnp.concatenate([value[:, : 3 * lanes], last], axis=0)


STEPS = 16
FAR = (3, 2, 1)
ROOT, BIG, SMALL = (float(np.cos(np.pi / v)) for v in (4, 8, 8 / 3))


def waves16(x):
    e = [x[n] + x[n + 8] for n in range(8)]
    o = [x[n] - x[n + 8] for n in range(8)]
    ee = [e[n] + e[n + 4] for n in range(4)]
    eo = [e[n] - e[n + 4] for n in range(4)]
    even, odd = ee[0] + ee[2], ee[1] + ee[3]
    minus, plus = ROOT * (eo[1] - eo[3]), ROOT * (eo[1] + eo[3])
    d1, d2, d3 = o[1] - o[7], ROOT * (o[2] - o[6]), o[3] - o[5]
    s1, s2, s3 = o[1] + o[7], ROOT * (o[2] + o[6]), o[3] + o[5]
    a, b = BIG * d1 + SMALL * d3, SMALL * d1 - BIG * d3
    g, h = SMALL * s1 + BIG * s3, BIG * s1 - SMALL * s3
    up, down = o[0] + d2, o[0] - d2
    high, low = o[4] + s2, o[4] - s2
    return [
        (even + odd, even - odd),
        (up + a, high + g),
        (eo[0] + minus, plus + eo[2]),
        (down + b, h - low),
        (ee[0] - ee[2], ee[1] - ee[3]),
        (down - b, h + low),
        (eo[0] - minus, plus - eo[2]),
        (up - a, g - high),
    ]


def cells16(u):
    (c0, c8), (c1, s1), (c2, s2), (c3, s3), (c4, s4), (c5, s5), (c6, s6), (c7, s7) = u
    even, odd = c0 + c8, c0 - c8
    ee = [even + c4, odd + s4, even - c4, odd - s4]
    m, p = ROOT * (c2 - c6), ROOT * (s2 + s6)
    eo = [c2 + c6, p + m, s2 - s6, p - m]
    e = [ee[n] + eo[n] for n in range(4)] + [ee[n] - eo[n] for n in range(4)]
    c17, c35, m17, m35 = c1 + c7, c3 + c5, c1 - c7, c3 - c5
    s17, s35, n17, n35 = s1 + s7, s3 + s5, s1 - s7, s3 - s5
    t1, r1 = BIG * m17 + SMALL * m35, SMALL * s17 + BIG * s35
    t2, r2 = ROOT * (c17 - c35), ROOT * (n17 + n35)
    t3, r3 = SMALL * m17 - BIG * m35, BIG * s17 - SMALL * s35
    o = [c17 + c35, r1 + t1, r2 + t2, r3 + t3, n17 - n35, r3 - t3, r2 - t2, r1 - t1]
    return [e[n] + o[n] for n in range(8)] + [e[n] - o[n] for n in range(8)]


def wave_groups(half):
    groups = []
    for g in range(STEPS // 2):
        orders = [0, 8] if g == 0 else [v for v in (g, STEPS - g) if v <= half]
        rows = []
        for order in orders:
            if order < half:
                rows.append((0, order, order))
            if order > 0:
                rows.append((1, order - 1, order))
        groups.append(rows)
    return groups


def wave_table(total, count, half, channels):
    fine = 128 // channels
    tables = []
    for d in range(count):
        rows = []
        for g, group in enumerate(wave_groups(half)):
            for sine, _, order in group:
                angle = 2 * np.pi * order * (count * np.arange(fine) + d) / total
                size = np.sqrt((1.0 if order == 0 else 2.0) / total)
                cos, sin = size * np.cos(angle), size * np.sin(angle)
                sign = 1.0 if order == g else -1.0
                first, last = (sin, sign * cos) if sine else (cos, -sign * sin)
                if g == 0:
                    zero = np.zeros(fine)
                    first, last = (first, zero) if order == 0 else (zero, first)
                rows.append(np.repeat(np.concatenate([first, last]), channels))
        tables.append(np.stack(rows))
    return np.stack(tables)


class Plan:
    def __init__(self, mesh, arg_shape, channels):
        self.nlon, self.nlat, self.nlead = (mesh.shape[n] for n in ("lon", "lat", "lead"))
        nz, ny, merged = arg_shape
        self.c = channels
        self.zl, self.yl = nz // self.nlead, ny // self.nlat
        self.nx = merged // channels
        self.xl = self.nx // self.nlon
        self.kp = MX // (self.nlon * self.nlat)
        self.kc = self.kp * channels
        self.lq = MY * MZ
        self.zy = self.zl * self.yl
        self.gain = math.sqrt(self.nx * ny * nz / MODES)
        eye_z, eye_l = np.eye(self.zl), np.eye(MY)
        by, bz = host_basis(ny, MY), host_basis(nz, MZ)
        c = channels
        self.groups = wave_groups(MX // 2)
        self.lon_table = halves(wave_table(self.nx, self.nlon, MX // 2, c)).transpose(1, 0, 2, 3)
        by_p = by.reshape(MY, self.nlat, self.yl)
        bz_s = bz.reshape(MZ, self.nlead, self.zl)
        self.lat_table = halves(
            np.einsum("lpy,zw->zlpwy", by_p, eye_z).reshape(self.zl * MY, self.nlat * self.zy)
        )
        lead = np.einsum("qsz,lm->slqzm", bz_s, eye_l)
        self.lead_table = halves(
            lead.reshape(self.nlead, self.lq, self.zl * MY).transpose(1, 0, 2).reshape(self.lq, -1)
        )
        self.lead_back = halves(
            lead.transpose(0, 3, 4, 1, 2).reshape(self.nlead, self.zl * MY, self.lq)
        )
        back = np.einsum("lpy,zw->pzywl", by_p, eye_z)
        self.lat_back = halves(back.reshape(self.nlat * self.zy, self.zl * MY))
        cc = c * c
        groups = 128 // c
        self.tile = np.concatenate(
            [np.kron(np.eye(groups)[:, [k]], np.tile(np.eye(c), (1, groups))) for k in range(groups)],
            axis=1,
        ).astype(ml_dtypes.bfloat16)
        wide = 256 // c
        self.fan = np.tile(np.eye(c), (1, wide)).astype(np.float32)
        self.block = np.kron(np.eye(wide), np.ones((c, c))).astype(np.float32)
        self.cc = cc


def peer(me, d):
    if d == 1:
        return me + 1 - 2 * lax.rem(me, 2)
    if d == 2:
        return lax.rem(me + 2, 4)
    return 3 - me


def products(plan, modes, tile, spread, product):
    pn = plan
    quarter = pn.lq // 4
    high, low = cut(modes[0])
    sh, sl = cut(modes[1])
    s4 = mm(sh, tile[...]) + mm(sl, tile[...])
    for k in range(pn.kp):
        part = slice(k * quarter, (k + 1) * quarter)
        whole = (slice(0, 3 * quarter), k, k * pn.lq)
        for source, which, offset in (whole, (part, pn.kp, k * pn.lq + 3 * quarter)):
            four = s4[source, which * 128 : (which + 1) * 128]
            two = jnp.concatenate([four, four], axis=1)
            rows = slice(offset, offset + four.shape[0])
            for j in range(pn.cc // 256):
                cols = slice(j * 256, (j + 1) * 256)
                table = spread[which, :, cols]
                product[rows, cols] = (mm(high[source], table) + mm(low[source], table)) * two


def remote_kernel(
    plan, act_h, pre_h, cot_h, weight, lw_h, lon_h, lat_th, lead_th, lead_bh, lat_bh, tile_h, fan_h, block_h,
    product, modes_out, grad_out, tile, spread,
    act, pre, cot, lw, lon_t, lat_t, lead_t, lead_b, lat_b, fan, block,
    h_out, loc_out, tt, xg, gs, sbuf, lonbuf, latsend, latrecv, leadbuf, wbuf, vbuf,
    in_sem, wsem, lon_s, lon_r, lat_s, lat_r, lead_s, lead_r, g_s, g_r, v_s, v_r, f_s, f_r, e_s, e_r,
):
    pn = plan
    lon, lat, lead = (lax.axis_index(n) for n in ("lon", "lat", "lead"))
    mesh_id = pl.DeviceIdType.MESH
    other = 1 - lon
    barrier = pltpu.get_barrier_semaphore()
    pl.semaphore_signal(barrier, inc=1, device_id={"lon": other}, device_id_type=mesh_id)
    loads = []
    pairs = (
        (lon_h.at[lon], lon_t), (pre_h, pre), (cot_h, cot), (act_h, act), (lw_h, lw), (fan_h, fan),
        (block_h, block), (lat_th, lat_t), (lead_th, lead_t), (lead_bh, lead_b), (lat_bh, lat_b), (tile_h, tile),
    )
    for n, (source, target) in enumerate(pairs):
        copy = pltpu.make_async_copy(source, target, in_sem.at[n])
        copy.start()
        loads.append(copy)
        if n == 3:
            for d in range(1, pn.nlat):
                pl.semaphore_signal(
                    barrier, inc=1, device_id={"lat": lax.rem(lat + d, pn.nlat)}, device_id_type=mesh_id
                )
            for d in range(1, pn.nlead):
                pl.semaphore_signal(
                    barrier, inc=1, device_id={"lead": lax.rem(lead + d, pn.nlead)}, device_id_type=mesh_id
                )
    wcopy = pltpu.make_async_copy(
        weight.at[pl.ds(pl.multiple_of(lat * (pn.kp * pn.lq), 8), pn.kp * pn.lq), :], wbuf, wsem
    )
    c = pn.c
    zy = pn.zy
    lanes = lax.broadcasted_iota(jnp.int32, (c, 256), 1) % c
    mask = jnp.where(lanes == lax.broadcasted_iota(jnp.int32, (c, 256), 0), 1.0, 0.0).astype(BF16)
    loads[0].wait()
    for k in range(MX):
        for h in range(2):
            tt[h, k * c : (k + 1) * c, :] = lon_t[h, k : k + 1, :] * mask

    lon_copies = {}

    def along_lon(f, field):
        for n, (one, two) in enumerate(waves16(field)):
            for m, value in enumerate((one, two)):
                high, low = cut(value)
                xg[f, n, 0:zy, m * 128 : (m + 1) * 128] = high
                xg[f, n, zy : 2 * zy, m * 128 : (m + 1) * 128] = low
        first = 0
        deep = pn.kc // 2
        for n, rows in enumerate(pn.groups):
            part = slice(first, first + c * len(rows))
            p = mm(tt[0, part, :], xg[f, n], NT)
            q = mm(tt[1, part, :], xg[f, n, 0:zy], NT)
            total = p[:, 0:zy] + p[:, zy:] + q
            for m, (who, place, _) in enumerate(rows):
                base = place // pn.kp * deep
                for piece in range(0, c, 16):
                    at = place % pn.kp * c + piece
                    side = at // deep
                    sbuf[f, who, base + at - side * deep : base + at - side * deep + 16, side * zy : (side + 1) * zy] = (
                        total[m * c + piece : m * c + piece + 16]
                    )
            first += c * len(rows)
        if f == 1:
            pl.semaphore_wait(barrier, 1 + (pn.nlat - 1) + (pn.nlead - 1))
        copy = pltpu.make_async_remote_copy(
            src_ref=sbuf.at[f, other], dst_ref=lonbuf.at[f], send_sem=lon_s.at[f], recv_sem=lon_r.at[f],
            device_id={"lon": other}, device_id_type=mesh_id,
        )
        copy.start()
        lon_copies[f] = copy

    lat_copies = {}

    def send_lat(f):
        lon_copies[f].wait()
        deep = pn.kc // 2
        for d in FAR + (0,):
            p = peer(lat, d) if d else lat
            rows = pl.ds(pl.multiple_of(p * deep, deep), deep)
            value = sbuf[f, lon, rows, :] + lonbuf[f, rows, :]
            if d == 0:
                latrecv[f, lat] = value
            else:
                latsend[f, d - 1] = value
                copy = pltpu.make_async_remote_copy(
                    src_ref=latsend.at[f, d - 1], dst_ref=latrecv.at[f, lat],
                    send_sem=lat_s.at[f, d - 1], recv_sem=lat_r.at[f, d - 1],
                    device_id={"lat": p}, device_id_type=mesh_id,
                )
                copy.start()
                lat_copies[f, d] = copy

    loads[1].wait()
    loads[2].wait()
    columns = []
    for n in range(STEPS):
        cols = slice(n * 128, (n + 1) * 128)
        v = pre[:, cols].astype(F32)
        cdf = 0.5 * (1.0 + lax.erf(v * (1.0 / math.sqrt(2.0))))
        density = jnp.exp(-0.5 * v * v) * (1.0 / math.sqrt(2.0 * math.pi))
        grad = cot[:, cols].astype(F32) * (cdf + v * density)
        gh, gl = cut(grad)
        gs[0, :, cols] = gh
        gs[1, :, cols] = gl
        columns.append(grad)
    along_lon(1, columns)
    loads[3].wait()
    wcopy.start()
    along_lon(0, [act[:, n * 128 : (n + 1) * 128].astype(F32) for n in range(STEPS)])
    send_lat(1)
    send_lat(0)
    for copy in loads[4:]:
        copy.wait()
    highest = lax.Precision.HIGHEST
    left = lax.dot_general(fan[...], lw[...], (((0,), (1,)), ((), ())), precision=highest, preferred_element_type=F32)
    both = jnp.dot(left, fan[...], precision=highest, preferred_element_type=F32) * block[...]
    bh, bl = cut(both)
    for t in range(pn.xl * c // 256):
        cols = slice(t * 256, (t + 1) * 256)
        hi, lo = gs[0, :, cols], gs[1, :, cols]
        loc_out[:, cols] = mm(hi, bh) + mm(lo, bh) + mm(hi, bl)
    for k in range(pn.kp + 1):
        spread[k] = placed((128, pn.cc), 1, c, k * c)
    lead_copies = {}

    def send_lead(f):
        for d in range(1, pn.nlat):
            lat_copies[f, d].wait()
        got = [latrecv[f, p] for p in range(pn.nlat)]
        wide = jnp.concatenate(
            [jnp.concatenate([v[:, side * zy : (side + 1) * zy] for v in got], axis=1) for side in range(2)], axis=0
        )
        leadbuf[lead, f] = fold(mm3((lat_t[0], lat_t[1]), wide, NT))
        for d in FAR:
            copy = pltpu.make_async_remote_copy(
                src_ref=leadbuf.at[lead, f], dst_ref=leadbuf.at[lead, f],
                send_sem=lead_s.at[f, d - 1], recv_sem=lead_r.at[f, d - 1],
                device_id={"lead": peer(lead, d)}, device_id_type=mesh_id,
            )
            copy.start()
            lead_copies[f, d] = copy

    send_lead(1)
    send_lead(0)
    g_copies = {}
    deep = modes_out.shape[2] // 2
    mine = pl.ds(pl.multiple_of(lax.rem(lead, 2) * deep, 8), deep)

    def finish_lead(f):
        for d in range(1, pn.nlead):
            lead_copies[f, d].wait()
        got = jnp.concatenate([unfold(leadbuf[s, f]) for s in range(pn.nlead)], axis=0)
        total = mm3((lead_t[0], lead_t[1]), got)
        if f == 1:
            total = total * pn.gain
        modes_out[lat, f] = fold(total)
        for d in FAR:
            if f == 1:
                part = modes_out.at[lat, f, mine, :]
            else:
                part = modes_out.at[lat, f]
            copy = pltpu.make_async_remote_copy(
                src_ref=part, dst_ref=part, send_sem=g_s.at[f, d - 1], recv_sem=g_r.at[f, d - 1],
                device_id={"lat": peer(lat, d)}, device_id_type=mesh_id,
            )
            copy.start()
            g_copies[f, d] = copy
        return total

    spectral = finish_lead(1)
    wcopy.wait()
    sh, sl = cut(spectral)
    pick = tile[0 : pn.kc, 0 : pn.kp * 128]
    wide = mm(sh, pick) + mm(sl, pick)
    adjoint = None
    for k in range(pn.kp):
        four = wide[:, k * 128 : (k + 1) * 128]
        prod = wbuf[k * pn.lq : (k + 1) * pn.lq, :] * jnp.concatenate([four] * (pn.cc // 128), axis=1)
        ph, plow = cut(prod)
        pick = placed((pn.cc, pn.kc), 0, c, k * c)
        term = mm(ph, pick) + mm(plow, pick)
        adjoint = term if adjoint is None else adjoint + term
    back = mm3((lead_b[0, lead], lead_b[1, lead]), adjoint)
    cells = mm3((lat_b[0], lat_b[1]), back)
    for p in range(pn.nlat):
        vbuf[p] = fold(cells[p * zy : (p + 1) * zy, :])
    h_out[lon, lat] = vbuf[lat]
    v_copies = {}
    for d in FAR:
        p = peer(lat, d)
        copy = pltpu.make_async_remote_copy(
            src_ref=vbuf.at[p], dst_ref=h_out.at[lon, lat],
            send_sem=v_s.at[d - 1], recv_sem=v_r.at[d - 1],
            device_id={"lat": p}, device_id_type=mesh_id,
        )
        copy.start()
        v_copies[d] = copy
    finish_lead(0)
    products(pn, modes_out.at[lat], tile, spread, product)
    pair_copies = []
    for d in (1, 2, 3):
        g_copies[1, d].wait_recv()
        part = modes_out.at[peer(lat, d), 1, mine, :]
        copy = pltpu.make_async_remote_copy(
            src_ref=part, dst_ref=part, send_sem=e_s.at[d - 1], recv_sem=e_r.at[d - 1],
            device_id={"lead": peer(lead, 1)}, device_id_type=mesh_id,
        )
        copy.start()
        pair_copies.append(copy)
    f_copies = []
    for d in range(pn.nlat):
        if d > 0:
            v_copies[d].wait_recv()
        s = peer(lat, d) if d else lat
        copy = pltpu.make_async_remote_copy(
            src_ref=h_out.at[lon, s], dst_ref=h_out.at[lon, s],
            send_sem=f_s.at[d], recv_sem=f_r.at[d],
            device_id={"lon": other}, device_id_type=mesh_id,
        )
        copy.start()
        f_copies.append(copy)
    for copy in f_copies:
        copy.wait()
    chunks = [[unfold(h_out[a, b]) for b in range(pn.nlat)] for a in range(pn.nlon)]
    waves = []
    first = 0
    for rows in pn.groups:
        part = slice(first, first + c * len(rows))
        pieces = []
        for who, place, _ in rows:
            at = place % pn.kp * c
            pieces.append(chunks[who][place // pn.kp][:, at : at + c])
        hh, hl = cut(jnp.concatenate(pieces, axis=1))
        wave = mm(hh, tt[0, part, :]) + mm(hl, tt[0, part, :]) + mm(hh, tt[1, part, :])
        waves.append((wave[:, :128], wave[:, 128:]))
        first += c * len(rows)
    for n, value in enumerate(cells16(waves)):
        cols = slice(n * 128, (n + 1) * 128)
        grad_out[:, cols] = (loc_out[:, cols] + value).astype(BF16)
    for copy in v_copies.values():
        copy.wait_send()
    for (f, d), copy in g_copies.items():
        if f == 1:
            copy.wait_send()
        else:
            copy.wait()
    for copy in pair_copies:
        copy.wait()


def finish_kernel(plan, product, modes, grad, tile, spread, grad_out, mode_grad, buf, sem, grad_sem):
    pn = plan
    lat = lax.axis_index("lat")
    size = pn.kp * pn.lq
    copies = []

    def write(source, p, n):
        rows = pl.ds(pl.multiple_of(p * size, size), size)
        copy = pltpu.make_async_copy(source, mode_grad.at[rows, :], sem.at[n])
        copy.start()
        copies.append(copy)

    write(product, lat, 0)
    copy = pltpu.make_async_copy(grad, grad_out, grad_sem)
    copy.start()
    copies.append(copy)
    for d in range(1, pn.nlat):
        p = peer(lat, d)
        products(pn, modes.at[p], tile, spread, buf.at[d - 1])
        write(buf.at[d - 1], p, d)
    for copy in copies:
        copy.wait()


def fast_device(plan, activation, pre_activation, cotangent, mode_weight, local_weight):
    pn = plan
    merged = activation.shape[2]
    flat = [v.reshape(pn.zy, merged) for v in (activation, pre_activation, cotangent)]
    vm = pl.BlockSpec(memory_space=pltpu.VMEM)
    hbm = pl.BlockSpec(memory_space=pltpu.HBM)
    half = MX // pn.nlon * pn.c
    dma = pltpu.SemaphoreType.DMA
    tables = (
        pn.lon_table, pn.lat_table, pn.lead_table, pn.lead_back, pn.lat_back, pn.tile, pn.fan, pn.block,
    )
    size = pn.kp * pn.lq
    product, modes, grad, tile, spread = pl.pallas_call(
        functools.partial(remote_kernel, pn),
        out_shape=(
            pltpu.VMEM((size, pn.cc), F32),
            pltpu.VMEM((pn.nlat, 2, pn.lq // 4 * 3, 128), F32),
            pltpu.VMEM((pn.zy, merged), BF16),
            pltpu.VMEM(pn.tile.shape, BF16),
            pltpu.VMEM((pn.kp + 1, 128, pn.cc), BF16),
        ),
        in_specs=[hbm] * 13,
        out_specs=(vm,) * 5,
        scratch_shapes=[
            pltpu.VMEM((pn.zy, merged), BF16),
            pltpu.VMEM((pn.zy, merged), BF16),
            pltpu.VMEM((pn.zy, merged), BF16),
            pltpu.VMEM(local_weight.shape, F32),
            pltpu.VMEM(pn.lon_table.shape[1:], BF16),
        ]
        + [pltpu.VMEM(v.shape, v.dtype) for v in tables[1:5] + tables[6:]]
        + [
            pltpu.VMEM((pn.nlon, pn.nlat, pn.zy // 4 * 3, 128), F32),
            pltpu.VMEM((pn.zy, merged), F32),
            pltpu.VMEM((2, MX * pn.c, 256), BF16),
            pltpu.VMEM((2, STEPS // 2, 2 * pn.zy, 256), BF16),
            pltpu.VMEM((2, pn.zy, merged), BF16),
            pltpu.VMEM((2, pn.nlon, half // 2, 2 * pn.zy), F32),
            pltpu.VMEM((2, half // 2, 2 * pn.zy), F32),
            pltpu.VMEM((2, pn.nlat - 1, pn.kc // 2, 2 * pn.zy), F32),
            pltpu.VMEM((2, pn.nlat, pn.kc // 2, 2 * pn.zy), F32),
            pltpu.VMEM((pn.nlead, 2, pn.zl * MY // 4 * 3, 128), F32),
            pltpu.VMEM((pn.kp * pn.lq, pn.cc), F32),
            pltpu.VMEM((pn.nlat, pn.zy // 4 * 3, 128), F32),
            dma((12,)), dma, dma((2,)), dma((2,)),
            dma((2, pn.nlat - 1)), dma((2, pn.nlat - 1)),
            dma((2, pn.nlead - 1)), dma((2, pn.nlead - 1)),
            dma((2, pn.nlat - 1)), dma((2, pn.nlat - 1)),
            dma((pn.nlat - 1,)), dma((pn.nlat - 1,)),
            dma((pn.nlat,)), dma((pn.nlat,)),
            dma((pn.nlat - 1,)), dma((pn.nlat - 1,)),
        ],
        compiler_params=pltpu.CompilerParams(
            collective_id=0, has_side_effects=True, vmem_limit_bytes=52 * 2**20
        ),
        name="modes",
    )(*flat, mode_weight, local_weight, *tables)
    grad, mode_grad = pl.pallas_call(
        functools.partial(finish_kernel, pn),
        out_shape=(
            jax.ShapeDtypeStruct((pn.zy, merged), BF16),
            jax.ShapeDtypeStruct((pn.nlat * size, pn.cc), F32),
        ),
        in_specs=[vm] * 5,
        out_specs=(hbm, hbm),
        scratch_shapes=[pltpu.VMEM((pn.nlat - 1, size, pn.cc), F32), dma((pn.nlat,)), dma],
        compiler_params=pltpu.CompilerParams(vmem_limit_bytes=24 * 2**20),
        name="finish",
    )(product, modes, grad, tile, spread)
    return grad.reshape(activation.shape), mode_grad


def solution(mesh):
    in_specs = (
        P("lead", "lat", "lon"),
        P("lead", "lat", "lon"),
        P("lead", "lat", "lon"),
        P("lon", None),
        P(),
    )
    out_specs = (P("lead", "lat", "lon"), P("lon", None))

    def whole(*args):
        shape = args[0].shape
        channels = args[4].shape[0]
        body = on_device
        if (
            mesh.shape["lon"] == 2
            and mesh.shape["lat"] == 4
            and mesh.shape["lead"] == 4
            and MX % (mesh.shape["lon"] * mesh.shape["lat"]) == 0
            and MX * MY * MZ == args[3].shape[0]
            and shape[2] == mesh.shape["lon"] * STEPS * 128
            and 4 * channels == 128
            and MX * channels == 96 * mesh.shape["lon"] * mesh.shape["lat"]
            and mesh.shape["lead"] * 4 == shape[0]
        ):
            body = functools.partial(fast_device, Plan(mesh, shape, channels))
        return jax.shard_map(
            body, mesh=mesh, in_specs=in_specs, out_specs=out_specs, check_vma=False
        )(*args)

    return whole
```

```python
import functools
import math

import jax
import jax.numpy as jnp
import ml_dtypes
import numpy as np
from jax import lax
from jax.experimental import pallas as pl
from jax.experimental.pallas import tpu as pltpu
from jax.sharding import PartitionSpec as P

MX = 24
MY = 24
MZ = 8
MODES = 4608


def make_basis(length, modes, start, count, stride):
    half = modes // 2
    order = jnp.arange(modes, dtype=jnp.int32)
    freq = jnp.where(order < half, order, order - half + 1)
    cells = start + stride * jnp.arange(count, dtype=jnp.int32)
    turns = freq[:, None] * cells[None, :] % length
    angle = 2.0 * math.pi / length * turns.astype(jnp.float32)
    waves = jnp.where(order[:, None] < half, jnp.cos(angle), jnp.sin(angle))
    weights = jnp.where(
        order == 0, jnp.float32(math.sqrt(1.0 / length)), jnp.float32(math.sqrt(2.0 / length))
    )
    return waves * weights[:, None]


def gelu_slope(value):
    normal_cdf = 0.5 * (1.0 + jax.scipy.special.erf(value / math.sqrt(2.0)))
    density = jnp.exp(-0.5 * value * value) / math.sqrt(2.0 * math.pi)
    return normal_cdf + value * density


def back_cells(coeffs, lon_basis, lat_basis, lead_basis):
    highest = lax.Precision.HIGHEST
    blocks = coeffs.reshape(
        lon_basis.shape[0], lat_basis.shape[0], lead_basis.shape[0], coeffs.shape[-1]
    )
    step = jnp.einsum("klqc,qz->zklc", blocks, lead_basis, precision=highest)
    step = jnp.einsum("zklc,ly->zykc", step, lat_basis, precision=highest)
    return jnp.einsum("zykc,kx->zyxc", step, lon_basis, precision=highest)


def on_device(activation, pre_activation, cotangent, mode_weight, local_weight):
    highest = lax.Precision.HIGHEST
    channels = local_weight.shape[0]
    lead_cells, lat_cells, merged = activation.shape
    lon_cells = merged // channels
    lon_count = lax.axis_size("lon")
    lon_total = lon_cells * lon_count
    lat_total = lat_cells * lax.axis_size("lat")
    lead_total = lead_cells * lax.axis_size("lead")
    lon_basis = make_basis(lon_total, MX, lax.axis_index("lon"), lon_cells, lon_count)
    lat_basis = make_basis(lat_total, MY, lax.axis_index("lat") * lat_cells, lat_cells, 1)
    lead_basis = make_basis(lead_total, MZ, lax.axis_index("lead") * lead_cells, lead_cells, 1)
    shape4 = (lead_cells, lat_cells, lon_cells, channels)
    grad_pre = cotangent.astype(jnp.float32).reshape(shape4) * gelu_slope(
        pre_activation.astype(jnp.float32).reshape(shape4)
    )
    stacked = jnp.concatenate([activation.astype(jnp.float32).reshape(shape4), grad_pre], axis=3)
    doubled = 2 * channels
    along_lon = jnp.einsum("zyxc,kx->zykc", stacked, lon_basis, precision=highest)
    along_lat = jnp.einsum("zykc,ly->zklc", along_lon, lat_basis, precision=highest)
    partial_sum = jnp.einsum("zklc,qz->klqc", along_lat, lead_basis, precision=highest).reshape(
        -1, doubled
    )
    summed = lax.psum(partial_sum, ("lat", "lead"))
    owned = lax.psum_scatter(summed, "lon", scatter_dimension=0, tiled=True)
    gain = math.sqrt(lon_total * lat_total * lead_total / MODES)
    coef = owned[:, :channels]
    spectral = gain * owned[:, channels:]
    owned_count = owned.shape[0]
    mode_grad = (coef[:, :, None] * spectral[:, None, :]).reshape(owned_count, channels * channels)
    mixing = mode_weight.reshape(owned_count, channels, channels)
    owned_adjoint = jnp.sum(mixing * spectral[:, None, :], axis=2)
    every_mode = lax.all_gather(owned_adjoint, "lon", axis=0, tiled=True)
    spread = back_cells(every_mode, lon_basis, lat_basis, lead_basis)
    local = jnp.einsum("zyxo,io->zyxi", grad_pre, local_weight, precision=highest)
    input_grad = (spread + local).reshape(lead_cells, lat_cells, merged)
    return (input_grad.astype(jnp.bfloat16), mode_grad)


F32 = jnp.float32
BF16 = jnp.bfloat16


def host_basis(length, modes):
    half = modes // 2
    order = np.arange(modes)
    freq = np.where(order < half, order, order - half + 1)
    turns = (freq[:, None] * np.arange(length)[None, :]) % length
    angle = 2.0 * np.pi / length * turns
    waves = np.where(order[:, None] < half, np.cos(angle), np.sin(angle))
    weights = np.where(order == 0, np.sqrt(1.0 / length), np.sqrt(2.0 / length))
    return waves * weights[:, None]


def halves(table):
    table = np.asarray(table, np.float32)
    high = table.astype(ml_dtypes.bfloat16)
    low = (table - high.astype(np.float32)).astype(ml_dtypes.bfloat16)
    return np.stack([high, low])


def cut(value):
    high = value.astype(BF16)
    return high, (value - high.astype(F32)).astype(BF16)


NN = (((1,), (0,)), ((), ()))
NT = (((1,), (1,)), ((), ()))


def mm(a, b, dims=NN):
    return lax.dot_general(a, b, dims, preferred_element_type=F32)


def mm3(table, b, dims=NN):
    bh, bl = cut(b)
    return mm(table[0], bh, dims) + mm(table[0], bl, dims) + mm(table[1], bh, dims)


def placed(shape, axis, channels, base):
    wide = lax.broadcasted_iota(jnp.int32, shape, axis) // channels
    narrow = lax.broadcasted_iota(jnp.int32, shape, 1 - axis) - base
    return jnp.where(wide == narrow, 1.0, 0.0).astype(BF16)


def fold(value):
    r, lanes = value.shape[0] // 4, value.shape[1] // 3
    last = jnp.concatenate([value[3 * r :, g * lanes : (g + 1) * lanes] for g in range(3)], axis=0)
    return jnp.concatenate([value[: 3 * r], last], axis=1)


def unfold(value):
    r, lanes = value.shape[0] // 3, value.shape[1] // 4
    last = jnp.concatenate([value[g * r : (g + 1) * r, 3 * lanes :] for g in range(3)], axis=1)
    return jnp.concatenate([value[:, : 3 * lanes], last], axis=0)


STEPS = 16
FAR = (3, 2, 1)
ROOT, BIG, SMALL = (float(np.cos(np.pi / v)) for v in (4, 8, 8 / 3))


def waves16(x):
    e = [x[n] + x[n + 8] for n in range(8)]
    o = [x[n] - x[n + 8] for n in range(8)]
    ee = [e[n] + e[n + 4] for n in range(4)]
    eo = [e[n] - e[n + 4] for n in range(4)]
    even, odd = ee[0] + ee[2], ee[1] + ee[3]
    minus, plus = ROOT * (eo[1] - eo[3]), ROOT * (eo[1] + eo[3])
    d1, d2, d3 = o[1] - o[7], ROOT * (o[2] - o[6]), o[3] - o[5]
    s1, s2, s3 = o[1] + o[7], ROOT * (o[2] + o[6]), o[3] + o[5]
    a, b = BIG * d1 + SMALL * d3, SMALL * d1 - BIG * d3
    g, h = SMALL * s1 + BIG * s3, BIG * s1 - SMALL * s3
    up, down = o[0] + d2, o[0] - d2
    high, low = o[4] + s2, o[4] - s2
    return [
        (even + odd, even - odd),
        (up + a, high + g),
        (eo[0] + minus, plus + eo[2]),
        (down + b, h - low),
        (ee[0] - ee[2], ee[1] - ee[3]),
        (down - b, h + low),
        (eo[0] - minus, plus - eo[2]),
        (up - a, g - high),
    ]


def cells16(u):
    (c0, c8), (c1, s1), (c2, s2), (c3, s3), (c4, s4), (c5, s5), (c6, s6), (c7, s7) = u
    even, odd = c0 + c8, c0 - c8
    ee = [even + c4, odd + s4, even - c4, odd - s4]
    m, p = ROOT * (c2 - c6), ROOT * (s2 + s6)
    eo = [c2 + c6, p + m, s2 - s6, p - m]
    e = [ee[n] + eo[n] for n in range(4)] + [ee[n] - eo[n] for n in range(4)]
    c17, c35, m17, m35 = c1 + c7, c3 + c5, c1 - c7, c3 - c5
    s17, s35, n17, n35 = s1 + s7, s3 + s5, s1 - s7, s3 - s5
    t1, r1 = BIG * m17 + SMALL * m35, SMALL * s17 + BIG * s35
    t2, r2 = ROOT * (c17 - c35), ROOT * (n17 + n35)
    t3, r3 = SMALL * m17 - BIG * m35, BIG * s17 - SMALL * s35
    o = [c17 + c35, r1 + t1, r2 + t2, r3 + t3, n17 - n35, r3 - t3, r2 - t2, r1 - t1]
    return [e[n] + o[n] for n in range(8)] + [e[n] - o[n] for n in range(8)]


def wave_groups(half):
    groups = []
    for g in range(STEPS // 2):
        orders = [0, 8] if g == 0 else [v for v in (g, STEPS - g) if v <= half]
        rows = []
        for order in orders:
            if order < half:
                rows.append((0, order, order))
            if order > 0:
                rows.append((1, order - 1, order))
        groups.append(rows)
    return groups


def wave_table(total, count, half, channels):
    fine = 128 // channels
    tables = []
    for d in range(count):
        rows = []
        for g, group in enumerate(wave_groups(half)):
            for sine, _, order in group:
                angle = 2 * np.pi * order * (count * np.arange(fine) + d) / total
                size = np.sqrt((1.0 if order == 0 else 2.0) / total)
                cos, sin = size * np.cos(angle), size * np.sin(angle)
                sign = 1.0 if order == g else -1.0
                first, last = (sin, sign * cos) if sine else (cos, -sign * sin)
                if g == 0:
                    zero = np.zeros(fine)
                    first, last = (first, zero) if order == 0 else (zero, first)
                rows.append(np.repeat(np.concatenate([first, last]), channels))
        tables.append(np.stack(rows))
    return np.stack(tables)


class Plan:
    def __init__(self, mesh, arg_shape, channels):
        self.nlon, self.nlat, self.nlead = (mesh.shape[n] for n in ("lon", "lat", "lead"))
        nz, ny, merged = arg_shape
        self.c = channels
        self.zl, self.yl = nz // self.nlead, ny // self.nlat
        self.nx = merged // channels
        self.xl = self.nx // self.nlon
        self.kp = MX // (self.nlon * self.nlat)
        self.kc = self.kp * channels
        self.lq = MY * MZ
        self.zy = self.zl * self.yl
        self.gain = math.sqrt(self.nx * ny * nz / MODES)
        eye_z, eye_l = np.eye(self.zl), np.eye(MY)
        by, bz = host_basis(ny, MY), host_basis(nz, MZ)
        c = channels
        self.groups = wave_groups(MX // 2)
        self.lon_table = halves(wave_table(self.nx, self.nlon, MX // 2, c)).transpose(1, 0, 2, 3)
        by_p = by.reshape(MY, self.nlat, self.yl)
        bz_s = bz.reshape(MZ, self.nlead, self.zl)
        self.lat_table = halves(
            np.einsum("lpy,zw->zlpwy", by_p, eye_z).reshape(self.zl * MY, self.nlat * self.zy)
        )
        lead = np.einsum("qsz,lm->slqzm", bz_s, eye_l)
        self.lead_table = halves(
            lead.reshape(self.nlead, self.lq, self.zl * MY).transpose(1, 0, 2).reshape(self.lq, -1)
        )
        self.lead_first = halves(
            np.einsum("qsz,yw->qyszw", bz_s, np.eye(self.yl)).reshape(MZ * self.yl, self.nlead * self.zy)
        )
        self.lat_last = halves(
            np.einsum("lpy,qr->lqpry", by_p, np.eye(MZ)).reshape(self.lq, self.nlat * MZ * self.yl)
        )
        self.lead_back = halves(
            lead.transpose(0, 3, 4, 1, 2).reshape(self.nlead, self.zl * MY, self.lq)
        )
        back = np.einsum("lpy,zw->pzywl", by_p, eye_z)
        self.lat_back = halves(back.reshape(self.nlat * self.zy, self.zl * MY))
        cc = c * c
        groups = 128 // c
        self.tile = np.concatenate(
            [np.kron(np.eye(groups)[:, [k]], np.tile(np.eye(c), (1, groups))) for k in range(groups)],
            axis=1,
        ).astype(ml_dtypes.bfloat16)
        wide = 256 // c
        self.fan = np.tile(np.eye(c), (1, wide)).astype(np.float32)
        self.block = np.kron(np.eye(wide), np.ones((c, c))).astype(np.float32)
        self.cc = cc


def peer(me, d):
    if d == 1:
        return me + 1 - 2 * lax.rem(me, 2)
    if d == 2:
        return lax.rem(me + 2, 4)
    return 3 - me


def products(plan, modes, chunk, tile, spread, product):
    pn = plan
    quarter = pn.lq // 4
    high, low = cut(modes[0, chunk])
    sh, sl = cut(modes[1, chunk])
    s4 = mm(sh, tile[...]) + mm(sl, tile[...])
    for k in range(pn.kp):
        part = slice(k * quarter, (k + 1) * quarter)
        whole = (slice(0, 3 * quarter), k, k * pn.lq)
        for source, which, offset in (whole, (part, pn.kp, k * pn.lq + 3 * quarter)):
            four = s4[source, which * 128 : (which + 1) * 128]
            two = jnp.concatenate([four, four], axis=1)
            rows = slice(offset, offset + four.shape[0])
            for j in range(pn.cc // 256):
                cols = slice(j * 256, (j + 1) * 256)
                table = spread[which, :, cols]
                product[rows, cols] = (mm(high[source], table) + mm(low[source], table)) * two


def remote_kernel(
    plan, act_h, pre_h, cot_h, weight, lw_h, lon_h, lat_th, lead_th, lead_fh, lat_lh, lead_bh, lat_bh, tile_h, fan_h, block_h,
    product, modes_out, grad_out, tile, spread,
    act, pre, cot, lw, lon_t, lat_t, lead_t, lead_f, lat_l, lead_b, lat_b, fan, block,
    h_out, loc_out, tt, xg, gs, sbuf, lonbuf, firstsend, firstrecv, leadbuf, latbuf, wbuf, vbuf,
    in_sem, wsem, lon_s, lon_r, first_s, first_r, next_s, next_r, g_s, g_r, v_s, v_r, f_s, f_r,
):
    pn = plan
    lon, lat, lead = (lax.axis_index(n) for n in ("lon", "lat", "lead"))
    mesh_id = pl.DeviceIdType.MESH
    other = 1 - lon
    barrier = pltpu.get_barrier_semaphore()
    pl.semaphore_signal(barrier, inc=1, device_id={"lon": other}, device_id_type=mesh_id)
    loads = []
    pairs = (
        (lon_h.at[lon], lon_t), (pre_h, pre), (cot_h, cot), (act_h, act), (lw_h, lw), (fan_h, fan),
        (block_h, block), (lat_th, lat_t), (lead_th, lead_t),
        (lead_fh, lead_f), (lat_lh, lat_l), (lead_bh, lead_b), (lat_bh, lat_b), (tile_h, tile),
    )
    for n, (source, target) in enumerate(pairs):
        copy = pltpu.make_async_copy(source, target, in_sem.at[n])
        copy.start()
        loads.append(copy)
        if n == 3:
            for d in range(1, pn.nlat):
                pl.semaphore_signal(
                    barrier, inc=1, device_id={"lat": lax.rem(lat + d, pn.nlat)}, device_id_type=mesh_id
                )
            for d in range(1, pn.nlead):
                pl.semaphore_signal(
                    barrier, inc=1, device_id={"lead": lax.rem(lead + d, pn.nlead)}, device_id_type=mesh_id
                )
    wcopy = pltpu.make_async_copy(
        weight.at[pl.ds(pl.multiple_of(lat * (pn.kp * pn.lq), 8), pn.kp * pn.lq), :], wbuf, wsem
    )
    c = pn.c
    zy = pn.zy
    lanes = lax.broadcasted_iota(jnp.int32, (c, 256), 1) % c
    mask = jnp.where(lanes == lax.broadcasted_iota(jnp.int32, (c, 256), 0), 1.0, 0.0).astype(BF16)
    loads[0].wait()
    for k in range(MX):
        for h in range(2):
            tt[h, k * c : (k + 1) * c, :] = lon_t[h, k : k + 1, :] * mask

    lon_copies = {}

    def along_lon(f, field):
        for n, (one, two) in enumerate(waves16(field)):
            for m, value in enumerate((one, two)):
                high, low = cut(value)
                xg[f, n, 0:zy, m * 128 : (m + 1) * 128] = high
                xg[f, n, zy : 2 * zy, m * 128 : (m + 1) * 128] = low
        first = 0
        deep = pn.kc // 2
        for n, rows in enumerate(pn.groups):
            part = slice(first, first + c * len(rows))
            p = mm(tt[0, part, :], xg[f, n], NT)
            q = mm(tt[1, part, :], xg[f, n, 0:zy], NT)
            total = p[:, 0:zy] + p[:, zy:] + q
            for m, (who, place, _) in enumerate(rows):
                base = place // pn.kp * deep
                for piece in range(0, c, 16):
                    at = place % pn.kp * c + piece
                    side = at // deep
                    sbuf[f, who, base + at - side * deep : base + at - side * deep + 16, side * zy : (side + 1) * zy] = (
                        total[m * c + piece : m * c + piece + 16]
                    )
            first += c * len(rows)
        if f == 1:
            pl.semaphore_wait(barrier, 1 + (pn.nlat - 1) + (pn.nlead - 1))
        copy = pltpu.make_async_remote_copy(
            src_ref=sbuf.at[f, other], dst_ref=lonbuf.at[f], send_sem=lon_s.at[f], recv_sem=lon_r.at[f],
            device_id={"lon": other}, device_id_type=mesh_id,
        )
        copy.start()
        lon_copies[f] = copy

    first_copies, next_copies, g_copies = {}, {}, {}

    def send(f, d, axis, source, target, send_sem, recv_sem):
        copy = pltpu.make_async_remote_copy(
            src_ref=source, dst_ref=target, send_sem=send_sem.at[f, d - 1], recv_sem=recv_sem.at[f, d - 1],
            device_id={axis: peer(lat if axis == "lat" else lead, d)}, device_id_type=mesh_id,
        )
        copy.start()
        return copy

    def send_first(f):
        axis, me = ("lat", lat) if f else ("lead", lead)
        lon_copies[f].wait()
        deep = pn.kc // 2
        for d in FAR + (0,):
            p = peer(me, d) if d else me
            rows = pl.ds(pl.multiple_of(p * deep, deep), deep)
            value = sbuf[f, lon, rows, :] + lonbuf[f, rows, :]
            if d == 0:
                firstrecv[f, me] = value
            else:
                firstsend[f, d - 1] = value
                first_copies[f, d] = send(
                    f, d, axis, firstsend.at[f, d - 1], firstrecv.at[f, me], first_s, first_r
                )

    loads[1].wait()
    loads[2].wait()
    columns = []
    for n in range(STEPS):
        cols = slice(n * 128, (n + 1) * 128)
        v = pre[:, cols].astype(F32)
        cdf = 0.5 * (1.0 + lax.erf(v * (1.0 / math.sqrt(2.0))))
        density = jnp.exp(-0.5 * v * v) * (1.0 / math.sqrt(2.0 * math.pi))
        grad = cot[:, cols].astype(F32) * (cdf + v * density)
        gh, gl = cut(grad)
        gs[0, :, cols] = gh
        gs[1, :, cols] = gl
        columns.append(grad)
    along_lon(1, columns)
    loads[3].wait()
    wcopy.start()
    along_lon(0, [act[:, n * 128 : (n + 1) * 128].astype(F32) for n in range(STEPS)])
    send_first(1)
    send_first(0)
    for copy in loads[4:]:
        copy.wait()
    highest = lax.Precision.HIGHEST
    left = lax.dot_general(fan[...], lw[...], (((0,), (1,)), ((), ())), precision=highest, preferred_element_type=F32)
    both = jnp.dot(left, fan[...], precision=highest, preferred_element_type=F32) * block[...]
    bh, bl = cut(both)
    for t in range(pn.xl * c // 256):
        cols = slice(t * 256, (t + 1) * 256)
        hi, lo = gs[0, :, cols], gs[1, :, cols]
        loc_out[:, cols] = mm(hi, bh) + mm(lo, bh) + mm(hi, bl)
    for k in range(pn.kp + 1):
        spread[k] = placed((128, pn.cc), 1, c, k * c)
    def send_next(f):
        axis, me, count, buf, table = (
            ("lead", lead, pn.nlat, leadbuf, lat_t) if f else ("lat", lat, pn.nlead, latbuf, lead_f)
        )
        for d in FAR:
            first_copies[f, d].wait()
        got = [firstrecv[f, p] for p in range(count)]
        wide = jnp.concatenate(
            [jnp.concatenate([v[:, side * zy : (side + 1) * zy] for v in got], axis=1) for side in range(2)], axis=0
        )
        buf[me] = fold(mm3((table[0], table[1]), wide, NT))
        for d in FAR:
            next_copies[f, d] = send(f, d, axis, buf.at[me], buf.at[me], next_s, next_r)

    send_next(1)
    send_next(0)

    def finish(f):
        axis, me, count, buf, table = (
            ("lat", lat, pn.nlead, leadbuf, lead_t) if f else ("lead", lead, pn.nlat, latbuf, lat_l)
        )
        for d in FAR:
            next_copies[f, d].wait()
        got = jnp.concatenate([unfold(buf[s]) for s in range(count)], axis=0)
        total = mm3((table[0], table[1]), got)
        if f == 1:
            total = total * pn.gain
        modes_out[f, me] = fold(total)
        for d in FAR:
            g_copies[f, d] = send(f, d, axis, modes_out.at[f, me], modes_out.at[f, me], g_s, g_r)
        return total

    spectral = finish(1)
    finish(0)
    wcopy.wait()
    sh, sl = cut(spectral)
    pick = tile[0 : pn.kc, 0 : pn.kp * 128]
    wide = mm(sh, pick) + mm(sl, pick)
    adjoint = None
    for k in range(pn.kp):
        four = wide[:, k * 128 : (k + 1) * 128]
        prod = wbuf[k * pn.lq : (k + 1) * pn.lq, :] * jnp.concatenate([four] * (pn.cc // 128), axis=1)
        ph, plow = cut(prod)
        pick = placed((pn.cc, pn.kc), 0, c, k * c)
        term = mm(ph, pick) + mm(plow, pick)
        adjoint = term if adjoint is None else adjoint + term
    back = mm3((lead_b[0, lead], lead_b[1, lead]), adjoint)
    cells = mm3((lat_b[0], lat_b[1]), back)
    for p in range(pn.nlat):
        vbuf[p] = fold(cells[p * zy : (p + 1) * zy, :])
    h_out[lon, lat] = vbuf[lat]
    v_copies = {}
    for d in FAR:
        p = peer(lat, d)
        copy = pltpu.make_async_remote_copy(
            src_ref=vbuf.at[p], dst_ref=h_out.at[lon, lat],
            send_sem=v_s.at[d - 1], recv_sem=v_r.at[d - 1],
            device_id={"lat": p}, device_id_type=mesh_id,
        )
        copy.start()
        v_copies[d] = copy
    f_copies = []
    for d in range(pn.nlat):
        if d > 0:
            v_copies[d].wait_recv()
        s = peer(lat, d) if d else lat
        copy = pltpu.make_async_remote_copy(
            src_ref=h_out.at[lon, s], dst_ref=h_out.at[lon, s],
            send_sem=f_s.at[d], recv_sem=f_r.at[d],
            device_id={"lon": other}, device_id_type=mesh_id,
        )
        copy.start()
        f_copies.append(copy)
    for copy in f_copies:
        copy.wait()
    chunks = [[unfold(h_out[a, b]) for b in range(pn.nlat)] for a in range(pn.nlon)]
    waves = []
    first = 0
    for rows in pn.groups:
        part = slice(first, first + c * len(rows))
        pieces = []
        for who, place, _ in rows:
            at = place % pn.kp * c
            pieces.append(chunks[who][place // pn.kp][:, at : at + c])
        hh, hl = cut(jnp.concatenate(pieces, axis=1))
        wave = mm(hh, tt[0, part, :]) + mm(hl, tt[0, part, :]) + mm(hh, tt[1, part, :])
        waves.append((wave[:, :128], wave[:, 128:]))
        first += c * len(rows)
    for n, value in enumerate(cells16(waves)):
        cols = slice(n * 128, (n + 1) * 128)
        grad_out[:, cols] = (loc_out[:, cols] + value).astype(BF16)
    for d in FAR:
        g_copies[1, d].wait()
    products(pn, modes_out, lead, tile, spread, product)
    for d in FAR:
        v_copies[d].wait_send()
        g_copies[0, d].wait()


def finish_kernel(plan, product, modes, grad, tile, spread, grad_out, mode_grad, buf, sem, grad_sem):
    pn = plan
    lead = lax.axis_index("lead")
    size = pn.kp * pn.lq
    copies = []

    def write(source, p, n):
        rows = pl.ds(pl.multiple_of(p * size, size), size)
        copy = pltpu.make_async_copy(source, mode_grad.at[rows, :], sem.at[n])
        copy.start()
        copies.append(copy)

    write(product, lead, 0)
    copy = pltpu.make_async_copy(grad, grad_out, grad_sem)
    copy.start()
    copies.append(copy)
    for d in range(1, pn.nlat):
        p = peer(lead, d)
        products(pn, modes, p, tile, spread, buf.at[d - 1])
        write(buf.at[d - 1], p, d)
    for copy in copies:
        copy.wait()


def fast_device(plan, activation, pre_activation, cotangent, mode_weight, local_weight):
    pn = plan
    merged = activation.shape[2]
    flat = [v.reshape(pn.zy, merged) for v in (activation, pre_activation, cotangent)]
    vm = pl.BlockSpec(memory_space=pltpu.VMEM)
    hbm = pl.BlockSpec(memory_space=pltpu.HBM)
    half = MX // pn.nlon * pn.c
    dma = pltpu.SemaphoreType.DMA
    tables = (
        pn.lon_table, pn.lat_table, pn.lead_table, pn.lead_first, pn.lat_last, pn.lead_back, pn.lat_back,
        pn.tile, pn.fan, pn.block,
    )
    size = pn.kp * pn.lq
    product, modes, grad, tile, spread = pl.pallas_call(
        functools.partial(remote_kernel, pn),
        out_shape=(
            pltpu.VMEM((size, pn.cc), F32),
            pltpu.VMEM((2, pn.nlat, pn.lq // 4 * 3, 128), F32),
            pltpu.VMEM((pn.zy, merged), BF16),
            pltpu.VMEM(pn.tile.shape, BF16),
            pltpu.VMEM((pn.kp + 1, 128, pn.cc), BF16),
        ),
        in_specs=[hbm] * 15,
        out_specs=(vm,) * 5,
        scratch_shapes=[
            pltpu.VMEM((pn.zy, merged), BF16),
            pltpu.VMEM((pn.zy, merged), BF16),
            pltpu.VMEM((pn.zy, merged), BF16),
            pltpu.VMEM(local_weight.shape, F32),
            pltpu.VMEM(pn.lon_table.shape[1:], BF16),
        ]
        + [pltpu.VMEM(v.shape, v.dtype) for v in tables[1:7] + tables[8:]]
        + [
            pltpu.VMEM((pn.nlon, pn.nlat, pn.zy // 4 * 3, 128), F32),
            pltpu.VMEM((pn.zy, merged), F32),
            pltpu.VMEM((2, MX * pn.c, 256), BF16),
            pltpu.VMEM((2, STEPS // 2, 2 * pn.zy, 256), BF16),
            pltpu.VMEM((2, pn.zy, merged), BF16),
            pltpu.VMEM((2, pn.nlon, half // 2, 2 * pn.zy), F32),
            pltpu.VMEM((2, half // 2, 2 * pn.zy), F32),
            pltpu.VMEM((2, pn.nlat - 1, pn.kc // 2, 2 * pn.zy), F32),
            pltpu.VMEM((2, pn.nlat, pn.kc // 2, 2 * pn.zy), F32),
            pltpu.VMEM((pn.nlead, pn.zl * MY // 4 * 3, 128), F32),
            pltpu.VMEM((pn.nlat, pn.yl * MZ // 4 * 3, 128), F32),
            pltpu.VMEM((pn.kp * pn.lq, pn.cc), F32),
            pltpu.VMEM((pn.nlat, pn.zy // 4 * 3, 128), F32),
            dma((14,)), dma, dma((2,)), dma((2,)),
            dma((2, pn.nlat - 1)), dma((2, pn.nlat - 1)),
            dma((2, pn.nlead - 1)), dma((2, pn.nlead - 1)),
            dma((2, pn.nlat - 1)), dma((2, pn.nlat - 1)),
            dma((pn.nlat - 1,)), dma((pn.nlat - 1,)),
            dma((pn.nlat,)), dma((pn.nlat,)),
        ],
        compiler_params=pltpu.CompilerParams(
            collective_id=0, has_side_effects=True, vmem_limit_bytes=52 * 2**20
        ),
        name="modes",
    )(*flat, mode_weight, local_weight, *tables)
    grad, mode_grad = pl.pallas_call(
        functools.partial(finish_kernel, pn),
        out_shape=(
            jax.ShapeDtypeStruct((pn.zy, merged), BF16),
            jax.ShapeDtypeStruct((pn.nlat * size, pn.cc), F32),
        ),
        in_specs=[vm] * 5,
        out_specs=(hbm, hbm),
        scratch_shapes=[pltpu.VMEM((pn.nlat - 1, size, pn.cc), F32), dma((pn.nlat,)), dma],
        compiler_params=pltpu.CompilerParams(vmem_limit_bytes=24 * 2**20),
        name="finish",
    )(product, modes, grad, tile, spread)
    return grad.reshape(activation.shape), mode_grad


def solution(mesh):
    in_specs = (
        P("lead", "lat", "lon"),
        P("lead", "lat", "lon"),
        P("lead", "lat", "lon"),
        P("lon", None),
        P(),
    )
    out_specs = (P("lead", "lat", "lon"), P("lon", None))

    def whole(*args):
        shape = args[0].shape
        channels = args[4].shape[0]
        body = on_device
        if (
            mesh.shape["lon"] == 2
            and mesh.shape["lat"] == 4
            and mesh.shape["lead"] == 4
            and MX % (mesh.shape["lon"] * mesh.shape["lat"]) == 0
            and MX * MY * MZ == args[3].shape[0]
            and shape[2] == mesh.shape["lon"] * STEPS * 128
            and 4 * channels == 128
            and MX * channels == 96 * mesh.shape["lon"] * mesh.shape["lat"]
            and mesh.shape["lead"] * 4 == shape[0]
        ):
            body = functools.partial(fast_device, Plan(mesh, shape, channels))
        return jax.shard_map(
            body, mesh=mesh, in_specs=in_specs, out_specs=out_specs, check_vma=False
        )(*args)

    return whole
```

```python
import functools
import math

import jax
import jax.numpy as jnp
import ml_dtypes
import numpy as np
from jax import lax
from jax.experimental import pallas as pl
from jax.experimental.pallas import tpu as pltpu
from jax.sharding import PartitionSpec as P

MX = 24
MY = 24
MZ = 8
MODES = 4608


def make_basis(length, modes, start, count, stride):
    half = modes // 2
    order = jnp.arange(modes, dtype=jnp.int32)
    freq = jnp.where(order < half, order, order - half + 1)
    cells = start + stride * jnp.arange(count, dtype=jnp.int32)
    turns = freq[:, None] * cells[None, :] % length
    angle = 2.0 * math.pi / length * turns.astype(jnp.float32)
    waves = jnp.where(order[:, None] < half, jnp.cos(angle), jnp.sin(angle))
    weights = jnp.where(
        order == 0, jnp.float32(math.sqrt(1.0 / length)), jnp.float32(math.sqrt(2.0 / length))
    )
    return waves * weights[:, None]


def gelu_slope(value):
    normal_cdf = 0.5 * (1.0 + jax.scipy.special.erf(value / math.sqrt(2.0)))
    density = jnp.exp(-0.5 * value * value) / math.sqrt(2.0 * math.pi)
    return normal_cdf + value * density


def back_cells(coeffs, lon_basis, lat_basis, lead_basis):
    highest = lax.Precision.HIGHEST
    blocks = coeffs.reshape(
        lon_basis.shape[0], lat_basis.shape[0], lead_basis.shape[0], coeffs.shape[-1]
    )
    step = jnp.einsum("klqc,qz->zklc", blocks, lead_basis, precision=highest)
    step = jnp.einsum("zklc,ly->zykc", step, lat_basis, precision=highest)
    return jnp.einsum("zykc,kx->zyxc", step, lon_basis, precision=highest)


def on_device(activation, pre_activation, cotangent, mode_weight, local_weight):
    highest = lax.Precision.HIGHEST
    channels = local_weight.shape[0]
    lead_cells, lat_cells, merged = activation.shape
    lon_cells = merged // channels
    lon_count = lax.axis_size("lon")
    lon_total = lon_cells * lon_count
    lat_total = lat_cells * lax.axis_size("lat")
    lead_total = lead_cells * lax.axis_size("lead")
    lon_basis = make_basis(lon_total, MX, lax.axis_index("lon"), lon_cells, lon_count)
    lat_basis = make_basis(lat_total, MY, lax.axis_index("lat") * lat_cells, lat_cells, 1)
    lead_basis = make_basis(lead_total, MZ, lax.axis_index("lead") * lead_cells, lead_cells, 1)
    shape4 = (lead_cells, lat_cells, lon_cells, channels)
    grad_pre = cotangent.astype(jnp.float32).reshape(shape4) * gelu_slope(
        pre_activation.astype(jnp.float32).reshape(shape4)
    )
    stacked = jnp.concatenate([activation.astype(jnp.float32).reshape(shape4), grad_pre], axis=3)
    doubled = 2 * channels
    along_lon = jnp.einsum("zyxc,kx->zykc", stacked, lon_basis, precision=highest)
    along_lat = jnp.einsum("zykc,ly->zklc", along_lon, lat_basis, precision=highest)
    partial_sum = jnp.einsum("zklc,qz->klqc", along_lat, lead_basis, precision=highest).reshape(
        -1, doubled
    )
    summed = lax.psum(partial_sum, ("lat", "lead"))
    owned = lax.psum_scatter(summed, "lon", scatter_dimension=0, tiled=True)
    gain = math.sqrt(lon_total * lat_total * lead_total / MODES)
    coef = owned[:, :channels]
    spectral = gain * owned[:, channels:]
    owned_count = owned.shape[0]
    mode_grad = (coef[:, :, None] * spectral[:, None, :]).reshape(owned_count, channels * channels)
    mixing = mode_weight.reshape(owned_count, channels, channels)
    owned_adjoint = jnp.sum(mixing * spectral[:, None, :], axis=2)
    every_mode = lax.all_gather(owned_adjoint, "lon", axis=0, tiled=True)
    spread = back_cells(every_mode, lon_basis, lat_basis, lead_basis)
    local = jnp.einsum("zyxo,io->zyxi", grad_pre, local_weight, precision=highest)
    input_grad = (spread + local).reshape(lead_cells, lat_cells, merged)
    return (input_grad.astype(jnp.bfloat16), mode_grad)


F32 = jnp.float32
BF16 = jnp.bfloat16


def host_basis(length, modes):
    half = modes // 2
    order = np.arange(modes)
    freq = np.where(order < half, order, order - half + 1)
    turns = (freq[:, None] * np.arange(length)[None, :]) % length
    angle = 2.0 * np.pi / length * turns
    waves = np.where(order[:, None] < half, np.cos(angle), np.sin(angle))
    weights = np.where(order == 0, np.sqrt(1.0 / length), np.sqrt(2.0 / length))
    return waves * weights[:, None]


def halves(table):
    table = np.asarray(table, np.float32)
    high = table.astype(ml_dtypes.bfloat16)
    low = (table - high.astype(np.float32)).astype(ml_dtypes.bfloat16)
    return np.stack([high, low])


def cut(value):
    high = value.astype(BF16)
    return high, (value - high.astype(F32)).astype(BF16)


NN = (((1,), (0,)), ((), ()))
NT = (((1,), (1,)), ((), ()))


def mm(a, b, dims=NN):
    return lax.dot_general(a, b, dims, preferred_element_type=F32)


def mm3(table, b, dims=NN):
    bh, bl = cut(b)
    return mm(table[0], bh, dims) + mm(table[0], bl, dims) + mm(table[1], bh, dims)


def placed(shape, axis, channels, base):
    wide = lax.broadcasted_iota(jnp.int32, shape, axis) // channels
    narrow = lax.broadcasted_iota(jnp.int32, shape, 1 - axis) - base
    return jnp.where(wide == narrow, 1.0, 0.0).astype(BF16)


def fold(value):
    r, lanes = value.shape[0] // 4, value.shape[1] // 3
    last = jnp.concatenate([value[3 * r :, g * lanes : (g + 1) * lanes] for g in range(3)], axis=0)
    return jnp.concatenate([value[: 3 * r], last], axis=1)


def unfold(value):
    r, lanes = value.shape[0] // 3, value.shape[1] // 4
    last = jnp.concatenate([value[g * r : (g + 1) * r, 3 * lanes :] for g in range(3)], axis=1)
    return jnp.concatenate([value[:, : 3 * lanes], last], axis=0)


STEPS = 16
FAR = (3, 2, 1)
ROOT, BIG, SMALL = (float(np.cos(np.pi / v)) for v in (4, 8, 8 / 3))


def waves16(x):
    e = [x[n] + x[n + 8] for n in range(8)]
    o = [x[n] - x[n + 8] for n in range(8)]
    ee = [e[n] + e[n + 4] for n in range(4)]
    eo = [e[n] - e[n + 4] for n in range(4)]
    even, odd = ee[0] + ee[2], ee[1] + ee[3]
    minus, plus = ROOT * (eo[1] - eo[3]), ROOT * (eo[1] + eo[3])
    d1, d2, d3 = o[1] - o[7], ROOT * (o[2] - o[6]), o[3] - o[5]
    s1, s2, s3 = o[1] + o[7], ROOT * (o[2] + o[6]), o[3] + o[5]
    a, b = BIG * d1 + SMALL * d3, SMALL * d1 - BIG * d3
    g, h = SMALL * s1 + BIG * s3, BIG * s1 - SMALL * s3
    up, down = o[0] + d2, o[0] - d2
    high, low = o[4] + s2, o[4] - s2
    return [
        (even + odd, even - odd),
        (up + a, high + g),
        (eo[0] + minus, plus + eo[2]),
        (down + b, h - low),
        (ee[0] - ee[2], ee[1] - ee[3]),
        (down - b, h + low),
        (eo[0] - minus, plus - eo[2]),
        (up - a, g - high),
    ]


def cells16(u):
    (c0, c8), (c1, s1), (c2, s2), (c3, s3), (c4, s4), (c5, s5), (c6, s6), (c7, s7) = u
    even, odd = c0 + c8, c0 - c8
    ee = [even + c4, odd + s4, even - c4, odd - s4]
    m, p = ROOT * (c2 - c6), ROOT * (s2 + s6)
    eo = [c2 + c6, p + m, s2 - s6, p - m]
    e = [ee[n] + eo[n] for n in range(4)] + [ee[n] - eo[n] for n in range(4)]
    c17, c35, m17, m35 = c1 + c7, c3 + c5, c1 - c7, c3 - c5
    s17, s35, n17, n35 = s1 + s7, s3 + s5, s1 - s7, s3 - s5
    t1, r1 = BIG * m17 + SMALL * m35, SMALL * s17 + BIG * s35
    t2, r2 = ROOT * (c17 - c35), ROOT * (n17 + n35)
    t3, r3 = SMALL * m17 - BIG * m35, BIG * s17 - SMALL * s35
    o = [c17 + c35, r1 + t1, r2 + t2, r3 + t3, n17 - n35, r3 - t3, r2 - t2, r1 - t1]
    return [e[n] + o[n] for n in range(8)] + [e[n] - o[n] for n in range(8)]


def wave_groups(half):
    groups = []
    for g in range(STEPS // 2):
        orders = [0, 8] if g == 0 else [v for v in (g, STEPS - g) if v <= half]
        rows = []
        for order in orders:
            if order < half:
                rows.append((0, order, order))
            if order > 0:
                rows.append((1, order - 1, order))
        groups.append(rows)
    return groups


def wave_table(total, count, half, channels):
    fine = 128 // channels
    tables = []
    for d in range(count):
        rows = []
        for g, group in enumerate(wave_groups(half)):
            for sine, _, order in group:
                angle = 2 * np.pi * order * (count * np.arange(fine) + d) / total
                size = np.sqrt((1.0 if order == 0 else 2.0) / total)
                cos, sin = size * np.cos(angle), size * np.sin(angle)
                sign = 1.0 if order == g else -1.0
                first, last = (sin, sign * cos) if sine else (cos, -sign * sin)
                if g == 0:
                    zero = np.zeros(fine)
                    first, last = (first, zero) if order == 0 else (zero, first)
                rows.append(np.repeat(np.concatenate([first, last]), channels))
        tables.append(np.stack(rows))
    return np.stack(tables)


class Plan:
    def __init__(self, mesh, arg_shape, channels):
        self.nlon, self.nlat, self.nlead = (mesh.shape[n] for n in ("lon", "lat", "lead"))
        nz, ny, merged = arg_shape
        self.c = channels
        self.zl, self.yl = nz // self.nlead, ny // self.nlat
        self.nx = merged // channels
        self.xl = self.nx // self.nlon
        self.kp = MX // (self.nlon * self.nlat)
        self.kc = self.kp * channels
        self.lq = MY * MZ
        self.zy = self.zl * self.yl
        self.gain = math.sqrt(self.nx * ny * nz / MODES)
        eye_z, eye_l = np.eye(self.zl), np.eye(MY)
        by, bz = host_basis(ny, MY), host_basis(nz, MZ)
        c = channels
        self.groups = wave_groups(MX // 2)
        self.lon_table = halves(wave_table(self.nx, self.nlon, MX // 2, c)).transpose(1, 0, 2, 3)
        by_p = by.reshape(MY, self.nlat, self.yl)
        bz_s = bz.reshape(MZ, self.nlead, self.zl)
        self.lat_table = halves(
            np.einsum("lpy,zw->zlpwy", by_p, eye_z).reshape(self.zl * MY, self.nlat * self.zy)
        )
        lead = np.einsum("qsz,lm->slqzm", bz_s, eye_l)
        self.lead_table = halves(
            lead.reshape(self.nlead, self.lq, self.zl * MY).transpose(1, 0, 2).reshape(self.lq, -1)
        )
        self.lead_first = halves(
            np.einsum("qsz,yw->qyszw", bz_s, np.eye(self.yl)).reshape(MZ * self.yl, self.nlead * self.zy)
        )
        self.lat_last = halves(
            np.einsum("lpy,qr->lqpry", by_p, np.eye(MZ)).reshape(self.lq, self.nlat * MZ * self.yl)
        )
        self.lead_back = halves(
            lead.transpose(0, 3, 4, 1, 2).reshape(self.nlead, self.zl * MY, self.lq)
        )
        back = np.einsum("lpy,zw->pzywl", by_p, eye_z)
        self.lat_back = halves(back.reshape(self.nlat * self.zy, self.zl * MY))
        cc = c * c
        groups = 128 // c
        self.tile = np.concatenate(
            [np.kron(np.eye(groups)[:, [k]], np.tile(np.eye(c), (1, groups))) for k in range(groups)],
            axis=1,
        ).astype(ml_dtypes.bfloat16)
        wide = 256 // c
        self.fan = np.tile(np.eye(c), (1, wide)).astype(np.float32)
        self.block = np.kron(np.eye(wide), np.ones((c, c))).astype(np.float32)
        self.cc = cc


def peer(me, d):
    if d == 1:
        return me + 1 - 2 * lax.rem(me, 2)
    if d == 2:
        return lax.rem(me + 2, 4)
    return 3 - me


def products(plan, modes, chunk, tile, spread, product):
    pn = plan
    quarter = pn.lq // 4
    high, low = cut(modes[0, chunk])
    sh, sl = cut(modes[1, chunk])
    s4 = mm(sh, tile[...]) + mm(sl, tile[...])
    for k in range(pn.kp):
        part = slice(k * quarter, (k + 1) * quarter)
        whole = (slice(0, 3 * quarter), k, k * pn.lq)
        for source, which, offset in (whole, (part, pn.kp, k * pn.lq + 3 * quarter)):
            four = s4[source, which * 128 : (which + 1) * 128]
            two = jnp.concatenate([four, four], axis=1)
            rows = slice(offset, offset + four.shape[0])
            for j in range(pn.cc // 256):
                cols = slice(j * 256, (j + 1) * 256)
                table = spread[which, :, cols]
                product[rows, cols] = (mm(high[source], table) + mm(low[source], table)) * two


def remote_kernel(
    plan, act_h, pre_h, cot_h, weight, lw_h, lon_h, lat_th, lead_th, lead_fh, lat_lh, lead_bh, lat_bh, tile_h, fan_h, block_h,
    product, modes_out, grad_out, tile, spread,
    act, pre, cot, lw, lon_t, lat_t, lead_t, lead_f, lat_l, lead_b, lat_b, fan, block,
    h_out, loc_out, tt, xg, gs, sbuf, lonbuf, firstsend, firstrecv, leadbuf, latbuf, wbuf, vbuf,
    in_sem, wsem, lon_s, lon_r, first_s, first_r, next_s, next_r, g_s, g_r, v_s, v_r, f_s, f_r,
):
    pn = plan
    lon, lat, lead = (lax.axis_index(n) for n in ("lon", "lat", "lead"))
    mesh_id = pl.DeviceIdType.MESH
    other = 1 - lon
    barrier = pltpu.get_barrier_semaphore()
    pl.semaphore_signal(barrier, inc=1, device_id={"lon": other}, device_id_type=mesh_id)
    loads = []
    pairs = (
        (lon_h.at[lon], lon_t), (pre_h, pre), (cot_h, cot), (act_h, act), (lw_h, lw), (fan_h, fan),
        (block_h, block), (lat_th, lat_t), (lead_th, lead_t),
        (lead_fh, lead_f), (lat_lh, lat_l), (lead_bh, lead_b), (lat_bh, lat_b), (tile_h, tile),
    )
    for n, (source, target) in enumerate(pairs):
        copy = pltpu.make_async_copy(source, target, in_sem.at[n])
        copy.start()
        loads.append(copy)
        if n == 3:
            for d in range(1, pn.nlat):
                pl.semaphore_signal(
                    barrier, inc=1, device_id={"lat": lax.rem(lat + d, pn.nlat)}, device_id_type=mesh_id
                )
            for d in range(1, pn.nlead):
                pl.semaphore_signal(
                    barrier, inc=1, device_id={"lead": lax.rem(lead + d, pn.nlead)}, device_id_type=mesh_id
                )
    wcopy = pltpu.make_async_copy(
        weight.at[pl.ds(pl.multiple_of(lat * (pn.kp * pn.lq), 8), pn.kp * pn.lq), :], wbuf, wsem
    )
    c = pn.c
    zy = pn.zy
    lanes = lax.broadcasted_iota(jnp.int32, (c, 256), 1) % c
    mask = jnp.where(lanes == lax.broadcasted_iota(jnp.int32, (c, 256), 0), 1.0, 0.0).astype(BF16)
    loads[0].wait()
    for k in range(MX):
        for h in range(2):
            tt[h, k * c : (k + 1) * c, :] = lon_t[h, k : k + 1, :] * mask

    lon_copies = {}

    def along_lon(f, field):
        for n, (one, two) in enumerate(waves16(field)):
            for m, value in enumerate((one, two)):
                high, low = cut(value)
                xg[f, n, 0:zy, m * 128 : (m + 1) * 128] = high
                xg[f, n, zy : 2 * zy, m * 128 : (m + 1) * 128] = low
        first = 0
        deep = pn.kc // 2
        for n, rows in enumerate(pn.groups):
            part = slice(first, first + c * len(rows))
            p = mm(tt[0, part, :], xg[f, n], NT)
            q = mm(tt[1, part, :], xg[f, n, 0:zy], NT)
            total = p[:, 0:zy] + p[:, zy:] + q
            for m, (who, place, _) in enumerate(rows):
                base = place // pn.kp * deep
                for piece in range(0, c, 16):
                    at = place % pn.kp * c + piece
                    side = at // deep
                    sbuf[f, who, base + at - side * deep : base + at - side * deep + 16, side * zy : (side + 1) * zy] = (
                        total[m * c + piece : m * c + piece + 16]
                    )
            first += c * len(rows)
        if f == 1:
            pl.semaphore_wait(barrier, 1 + (pn.nlat - 1) + (pn.nlead - 1))
        copy = pltpu.make_async_remote_copy(
            src_ref=sbuf.at[f, other], dst_ref=lonbuf.at[f], send_sem=lon_s.at[f], recv_sem=lon_r.at[f],
            device_id={"lon": other}, device_id_type=mesh_id,
        )
        copy.start()
        lon_copies[f] = copy

    first_copies, next_copies, g_copies = {}, {}, {}

    def send(f, d, axis, source, target, send_sem, recv_sem):
        copy = pltpu.make_async_remote_copy(
            src_ref=source, dst_ref=target, send_sem=send_sem.at[f, d - 1], recv_sem=recv_sem.at[f, d - 1],
            device_id={axis: peer(lat if axis == "lat" else lead, d)}, device_id_type=mesh_id,
        )
        copy.start()
        return copy

    def send_first(f):
        axis, me = ("lat", lat) if f else ("lead", lead)
        lon_copies[f].wait()
        deep = pn.kc // 2
        for d in FAR + (0,):
            p = peer(me, d) if d else me
            rows = pl.ds(pl.multiple_of(p * deep, deep), deep)
            value = sbuf[f, lon, rows, :] + lonbuf[f, rows, :]
            if d == 0:
                firstrecv[f, me] = value
            else:
                firstsend[f, d - 1] = value
                first_copies[f, d] = send(
                    f, d, axis, firstsend.at[f, d - 1], firstrecv.at[f, me], first_s, first_r
                )

    loads[1].wait()
    loads[2].wait()
    columns = []
    for n in range(STEPS):
        cols = slice(n * 128, (n + 1) * 128)
        v = pre[:, cols].astype(F32)
        cdf = 0.5 * (1.0 + lax.erf(v * (1.0 / math.sqrt(2.0))))
        density = jnp.exp(-0.5 * v * v) * (1.0 / math.sqrt(2.0 * math.pi))
        grad = cot[:, cols].astype(F32) * (cdf + v * density)
        gh, gl = cut(grad)
        gs[0, :, cols] = gh
        gs[1, :, cols] = gl
        columns.append(grad)
    along_lon(1, columns)
    loads[3].wait()
    wcopy.start()
    along_lon(0, [act[:, n * 128 : (n + 1) * 128].astype(F32) for n in range(STEPS)])
    send_first(1)
    send_first(0)
    for copy in loads[4:]:
        copy.wait()
    highest = lax.Precision.HIGHEST
    left = lax.dot_general(fan[...], lw[...], (((0,), (1,)), ((), ())), precision=highest, preferred_element_type=F32)
    both = jnp.dot(left, fan[...], precision=highest, preferred_element_type=F32) * block[...]
    bh, bl = cut(both)
    for t in range(pn.xl * c // 256):
        cols = slice(t * 256, (t + 1) * 256)
        hi, lo = gs[0, :, cols], gs[1, :, cols]
        loc_out[:, cols] = mm(hi, bh) + mm(lo, bh) + mm(hi, bl)
    for k in range(pn.kp + 1):
        spread[k] = placed((128, pn.cc), 1, c, k * c)
    def send_next(f):
        axis, me, count, buf, table = (
            ("lead", lead, pn.nlat, leadbuf, lat_t) if f else ("lat", lat, pn.nlead, latbuf, lead_f)
        )
        for d in FAR:
            first_copies[f, d].wait()
        got = [firstrecv[f, p] for p in range(count)]
        wide = jnp.concatenate(
            [jnp.concatenate([v[:, side * zy : (side + 1) * zy] for v in got], axis=1) for side in range(2)], axis=0
        )
        buf[me] = fold(mm3((table[0], table[1]), wide, NT))
        for d in FAR:
            next_copies[f, d] = send(f, d, axis, buf.at[me], buf.at[me], next_s, next_r)

    send_next(1)
    send_next(0)

    def finish(f):
        axis, me, count, buf, table = (
            ("lat", lat, pn.nlead, leadbuf, lead_t) if f else ("lead", lead, pn.nlat, latbuf, lat_l)
        )
        for d in FAR:
            next_copies[f, d].wait()
        got = jnp.concatenate([unfold(buf[s]) for s in range(count)], axis=0)
        total = mm3((table[0], table[1]), got)
        if f == 1:
            total = total * pn.gain
        modes_out[f, me] = fold(total)
        for d in FAR:
            g_copies[f, d] = send(f, d, axis, modes_out.at[f, me], modes_out.at[f, me], g_s, g_r)
        return total

    finish(0)
    spectral = finish(1)
    wcopy.wait()
    sh, sl = cut(spectral)
    pick = tile[0 : pn.kc, 0 : pn.kp * 128]
    wide = mm(sh, pick) + mm(sl, pick)
    adjoint = None
    for k in range(pn.kp):
        four = wide[:, k * 128 : (k + 1) * 128]
        prod = wbuf[k * pn.lq : (k + 1) * pn.lq, :] * jnp.concatenate([four] * (pn.cc // 128), axis=1)
        ph, plow = cut(prod)
        pick = placed((pn.cc, pn.kc), 0, c, k * c)
        term = mm(ph, pick) + mm(plow, pick)
        adjoint = term if adjoint is None else adjoint + term
    back = mm3((lead_b[0, lead], lead_b[1, lead]), adjoint)
    cells = mm3((lat_b[0], lat_b[1]), back)
    for p in range(pn.nlat):
        vbuf[p] = fold(cells[p * zy : (p + 1) * zy, :])
    h_out[lon, lat] = vbuf[lat]
    v_copies = {}
    for d in FAR:
        p = peer(lat, d)
        copy = pltpu.make_async_remote_copy(
            src_ref=vbuf.at[p], dst_ref=h_out.at[lon, lat],
            send_sem=v_s.at[d - 1], recv_sem=v_r.at[d - 1],
            device_id={"lat": p}, device_id_type=mesh_id,
        )
        copy.start()
        v_copies[d] = copy
    f_copies = []
    for d in range(pn.nlat):
        if d > 0:
            v_copies[d].wait_recv()
        s = peer(lat, d) if d else lat
        copy = pltpu.make_async_remote_copy(
            src_ref=h_out.at[lon, s], dst_ref=h_out.at[lon, s],
            send_sem=f_s.at[d], recv_sem=f_r.at[d],
            device_id={"lon": other}, device_id_type=mesh_id,
        )
        copy.start()
        f_copies.append(copy)
    for d in FAR:
        g_copies[1, d].wait()
    products(pn, modes_out, lead, tile, spread, product)
    for copy in f_copies:
        copy.wait()
    chunks = [[unfold(h_out[a, b]) for b in range(pn.nlat)] for a in range(pn.nlon)]
    waves = []
    first = 0
    for rows in pn.groups:
        part = slice(first, first + c * len(rows))
        pieces = []
        for who, place, _ in rows:
            at = place % pn.kp * c
            pieces.append(chunks[who][place // pn.kp][:, at : at + c])
        hh, hl = cut(jnp.concatenate(pieces, axis=1))
        wave = mm(hh, tt[0, part, :]) + mm(hl, tt[0, part, :]) + mm(hh, tt[1, part, :])
        waves.append((wave[:, :128], wave[:, 128:]))
        first += c * len(rows)
    for n, value in enumerate(cells16(waves)):
        cols = slice(n * 128, (n + 1) * 128)
        grad_out[:, cols] = (loc_out[:, cols] + value).astype(BF16)
    for d in FAR:
        v_copies[d].wait_send()
        g_copies[0, d].wait()


def finish_kernel(plan, product, modes, grad, tile, spread, grad_out, mode_grad, buf, sem, grad_sem):
    pn = plan
    lead = lax.axis_index("lead")
    size = pn.kp * pn.lq
    copies = []

    def write(source, p, n):
        rows = pl.ds(pl.multiple_of(p * size, size), size)
        copy = pltpu.make_async_copy(source, mode_grad.at[rows, :], sem.at[n])
        copy.start()
        copies.append(copy)

    write(product, lead, 0)
    copy = pltpu.make_async_copy(grad, grad_out, grad_sem)
    copy.start()
    copies.append(copy)
    for d in range(1, pn.nlat):
        p = peer(lead, d)
        products(pn, modes, p, tile, spread, buf.at[d - 1])
        write(buf.at[d - 1], p, d)
    for copy in copies:
        copy.wait()


def fast_device(plan, activation, pre_activation, cotangent, mode_weight, local_weight):
    pn = plan
    merged = activation.shape[2]
    flat = [v.reshape(pn.zy, merged) for v in (activation, pre_activation, cotangent)]
    vm = pl.BlockSpec(memory_space=pltpu.VMEM)
    hbm = pl.BlockSpec(memory_space=pltpu.HBM)
    half = MX // pn.nlon * pn.c
    dma = pltpu.SemaphoreType.DMA
    tables = (
        pn.lon_table, pn.lat_table, pn.lead_table, pn.lead_first, pn.lat_last, pn.lead_back, pn.lat_back,
        pn.tile, pn.fan, pn.block,
    )
    size = pn.kp * pn.lq
    product, modes, grad, tile, spread = pl.pallas_call(
        functools.partial(remote_kernel, pn),
        out_shape=(
            pltpu.VMEM((size, pn.cc), F32),
            pltpu.VMEM((2, pn.nlat, pn.lq // 4 * 3, 128), F32),
            pltpu.VMEM((pn.zy, merged), BF16),
            pltpu.VMEM(pn.tile.shape, BF16),
            pltpu.VMEM((pn.kp + 1, 128, pn.cc), BF16),
        ),
        in_specs=[hbm] * 15,
        out_specs=(vm,) * 5,
        scratch_shapes=[
            pltpu.VMEM((pn.zy, merged), BF16),
            pltpu.VMEM((pn.zy, merged), BF16),
            pltpu.VMEM((pn.zy, merged), BF16),
            pltpu.VMEM(local_weight.shape, F32),
            pltpu.VMEM(pn.lon_table.shape[1:], BF16),
        ]
        + [pltpu.VMEM(v.shape, v.dtype) for v in tables[1:7] + tables[8:]]
        + [
            pltpu.VMEM((pn.nlon, pn.nlat, pn.zy // 4 * 3, 128), F32),
            pltpu.VMEM((pn.zy, merged), F32),
            pltpu.VMEM((2, MX * pn.c, 256), BF16),
            pltpu.VMEM((2, STEPS // 2, 2 * pn.zy, 256), BF16),
            pltpu.VMEM((2, pn.zy, merged), BF16),
            pltpu.VMEM((2, pn.nlon, half // 2, 2 * pn.zy), F32),
            pltpu.VMEM((2, half // 2, 2 * pn.zy), F32),
            pltpu.VMEM((2, pn.nlat - 1, pn.kc // 2, 2 * pn.zy), F32),
            pltpu.VMEM((2, pn.nlat, pn.kc // 2, 2 * pn.zy), F32),
            pltpu.VMEM((pn.nlead, pn.zl * MY // 4 * 3, 128), F32),
            pltpu.VMEM((pn.nlat, pn.yl * MZ // 4 * 3, 128), F32),
            pltpu.VMEM((pn.kp * pn.lq, pn.cc), F32),
            pltpu.VMEM((pn.nlat, pn.zy // 4 * 3, 128), F32),
            dma((14,)), dma, dma((2,)), dma((2,)),
            dma((2, pn.nlat - 1)), dma((2, pn.nlat - 1)),
            dma((2, pn.nlead - 1)), dma((2, pn.nlead - 1)),
            dma((2, pn.nlat - 1)), dma((2, pn.nlat - 1)),
            dma((pn.nlat - 1,)), dma((pn.nlat - 1,)),
            dma((pn.nlat,)), dma((pn.nlat,)),
        ],
        compiler_params=pltpu.CompilerParams(
            collective_id=0, has_side_effects=True, vmem_limit_bytes=52 * 2**20
        ),
        name="modes",
    )(*flat, mode_weight, local_weight, *tables)
    grad, mode_grad = pl.pallas_call(
        functools.partial(finish_kernel, pn),
        out_shape=(
            jax.ShapeDtypeStruct((pn.zy, merged), BF16),
            jax.ShapeDtypeStruct((pn.nlat * size, pn.cc), F32),
        ),
        in_specs=[vm] * 5,
        out_specs=(hbm, hbm),
        scratch_shapes=[pltpu.VMEM((pn.nlat - 1, size, pn.cc), F32), dma((pn.nlat,)), dma],
        compiler_params=pltpu.CompilerParams(vmem_limit_bytes=24 * 2**20),
        name="finish",
    )(product, modes, grad, tile, spread)
    return grad.reshape(activation.shape), mode_grad


def solution(mesh):
    in_specs = (
        P("lead", "lat", "lon"),
        P("lead", "lat", "lon"),
        P("lead", "lat", "lon"),
        P("lon", None),
        P(),
    )
    out_specs = (P("lead", "lat", "lon"), P("lon", None))

    def whole(*args):
        shape = args[0].shape
        channels = args[4].shape[0]
        body = on_device
        if (
            mesh.shape["lon"] == 2
            and mesh.shape["lat"] == 4
            and mesh.shape["lead"] == 4
            and MX % (mesh.shape["lon"] * mesh.shape["lat"]) == 0
            and MX * MY * MZ == args[3].shape[0]
            and shape[2] == mesh.shape["lon"] * STEPS * 128
            and 4 * channels == 128
            and MX * channels == 96 * mesh.shape["lon"] * mesh.shape["lat"]
            and mesh.shape["lead"] * 4 == shape[0]
        ):
            body = functools.partial(fast_device, Plan(mesh, shape, channels))
        return jax.shard_map(
            body, mesh=mesh, in_specs=in_specs, out_specs=out_specs, check_vma=False
        )(*args)

    return whole
```

```python
import functools
import math

import jax
import jax.numpy as jnp
import ml_dtypes
import numpy as np
from jax import lax
from jax.experimental import pallas as pl
from jax.experimental.pallas import tpu as pltpu
from jax.sharding import PartitionSpec as P

MX = 24
MY = 24
MZ = 8
MODES = 4608


def make_basis(length, modes, start, count, stride):
    half = modes // 2
    order = jnp.arange(modes, dtype=jnp.int32)
    freq = jnp.where(order < half, order, order - half + 1)
    cells = start + stride * jnp.arange(count, dtype=jnp.int32)
    turns = freq[:, None] * cells[None, :] % length
    angle = 2.0 * math.pi / length * turns.astype(jnp.float32)
    waves = jnp.where(order[:, None] < half, jnp.cos(angle), jnp.sin(angle))
    weights = jnp.where(
        order == 0, jnp.float32(math.sqrt(1.0 / length)), jnp.float32(math.sqrt(2.0 / length))
    )
    return waves * weights[:, None]


def gelu_slope(value):
    normal_cdf = 0.5 * (1.0 + jax.scipy.special.erf(value / math.sqrt(2.0)))
    density = jnp.exp(-0.5 * value * value) / math.sqrt(2.0 * math.pi)
    return normal_cdf + value * density


def back_cells(coeffs, lon_basis, lat_basis, lead_basis):
    highest = lax.Precision.HIGHEST
    blocks = coeffs.reshape(
        lon_basis.shape[0], lat_basis.shape[0], lead_basis.shape[0], coeffs.shape[-1]
    )
    step = jnp.einsum("klqc,qz->zklc", blocks, lead_basis, precision=highest)
    step = jnp.einsum("zklc,ly->zykc", step, lat_basis, precision=highest)
    return jnp.einsum("zykc,kx->zyxc", step, lon_basis, precision=highest)


def on_device(activation, pre_activation, cotangent, mode_weight, local_weight):
    highest = lax.Precision.HIGHEST
    channels = local_weight.shape[0]
    lead_cells, lat_cells, merged = activation.shape
    lon_cells = merged // channels
    lon_count = lax.axis_size("lon")
    lon_total = lon_cells * lon_count
    lat_total = lat_cells * lax.axis_size("lat")
    lead_total = lead_cells * lax.axis_size("lead")
    lon_basis = make_basis(lon_total, MX, lax.axis_index("lon"), lon_cells, lon_count)
    lat_basis = make_basis(lat_total, MY, lax.axis_index("lat") * lat_cells, lat_cells, 1)
    lead_basis = make_basis(lead_total, MZ, lax.axis_index("lead") * lead_cells, lead_cells, 1)
    shape4 = (lead_cells, lat_cells, lon_cells, channels)
    grad_pre = cotangent.astype(jnp.float32).reshape(shape4) * gelu_slope(
        pre_activation.astype(jnp.float32).reshape(shape4)
    )
    stacked = jnp.concatenate([activation.astype(jnp.float32).reshape(shape4), grad_pre], axis=3)
    doubled = 2 * channels
    along_lon = jnp.einsum("zyxc,kx->zykc", stacked, lon_basis, precision=highest)
    along_lat = jnp.einsum("zykc,ly->zklc", along_lon, lat_basis, precision=highest)
    partial_sum = jnp.einsum("zklc,qz->klqc", along_lat, lead_basis, precision=highest).reshape(
        -1, doubled
    )
    summed = lax.psum(partial_sum, ("lat", "lead"))
    owned = lax.psum_scatter(summed, "lon", scatter_dimension=0, tiled=True)
    gain = math.sqrt(lon_total * lat_total * lead_total / MODES)
    coef = owned[:, :channels]
    spectral = gain * owned[:, channels:]
    owned_count = owned.shape[0]
    mode_grad = (coef[:, :, None] * spectral[:, None, :]).reshape(owned_count, channels * channels)
    mixing = mode_weight.reshape(owned_count, channels, channels)
    owned_adjoint = jnp.sum(mixing * spectral[:, None, :], axis=2)
    every_mode = lax.all_gather(owned_adjoint, "lon", axis=0, tiled=True)
    spread = back_cells(every_mode, lon_basis, lat_basis, lead_basis)
    local = jnp.einsum("zyxo,io->zyxi", grad_pre, local_weight, precision=highest)
    input_grad = (spread + local).reshape(lead_cells, lat_cells, merged)
    return (input_grad.astype(jnp.bfloat16), mode_grad)


F32 = jnp.float32
BF16 = jnp.bfloat16


def host_basis(length, modes):
    half = modes // 2
    order = np.arange(modes)
    freq = np.where(order < half, order, order - half + 1)
    turns = (freq[:, None] * np.arange(length)[None, :]) % length
    angle = 2.0 * np.pi / length * turns
    waves = np.where(order[:, None] < half, np.cos(angle), np.sin(angle))
    weights = np.where(order == 0, np.sqrt(1.0 / length), np.sqrt(2.0 / length))
    return waves * weights[:, None]


def halves(table):
    table = np.asarray(table, np.float32)
    high = table.astype(ml_dtypes.bfloat16)
    low = (table - high.astype(np.float32)).astype(ml_dtypes.bfloat16)
    return np.stack([high, low])


def cut(value):
    high = value.astype(BF16)
    return high, (value - high.astype(F32)).astype(BF16)


NN = (((1,), (0,)), ((), ()))
NT = (((1,), (1,)), ((), ()))


def mm(a, b, dims=NN):
    return lax.dot_general(a, b, dims, preferred_element_type=F32)


def mm3(table, b, dims=NN):
    bh, bl = cut(b)
    return mm(table[0], bh, dims) + mm(table[0], bl, dims) + mm(table[1], bh, dims)


def placed(shape, axis, channels, base):
    wide = lax.broadcasted_iota(jnp.int32, shape, axis) // channels
    narrow = lax.broadcasted_iota(jnp.int32, shape, 1 - axis) - base
    return jnp.where(wide == narrow, 1.0, 0.0).astype(BF16)


def fold(value):
    r, lanes = value.shape[0] // 4, value.shape[1] // 3
    last = jnp.concatenate([value[3 * r :, g * lanes : (g + 1) * lanes] for g in range(3)], axis=0)
    return jnp.concatenate([value[: 3 * r], last], axis=1)


def unfold(value):
    r, lanes = value.shape[0] // 3, value.shape[1] // 4
    last = jnp.concatenate([value[g * r : (g + 1) * r, 3 * lanes :] for g in range(3)], axis=1)
    return jnp.concatenate([value[:, : 3 * lanes], last], axis=0)


STEPS = 16
FAR = (3, 2, 1)
ROOT, BIG, SMALL = (float(np.cos(np.pi / v)) for v in (4, 8, 8 / 3))


def waves16(x):
    e = [x[n] + x[n + 8] for n in range(8)]
    o = [x[n] - x[n + 8] for n in range(8)]
    ee = [e[n] + e[n + 4] for n in range(4)]
    eo = [e[n] - e[n + 4] for n in range(4)]
    even, odd = ee[0] + ee[2], ee[1] + ee[3]
    minus, plus = ROOT * (eo[1] - eo[3]), ROOT * (eo[1] + eo[3])
    d1, d2, d3 = o[1] - o[7], ROOT * (o[2] - o[6]), o[3] - o[5]
    s1, s2, s3 = o[1] + o[7], ROOT * (o[2] + o[6]), o[3] + o[5]
    a, b = BIG * d1 + SMALL * d3, SMALL * d1 - BIG * d3
    g, h = SMALL * s1 + BIG * s3, BIG * s1 - SMALL * s3
    up, down = o[0] + d2, o[0] - d2
    high, low = o[4] + s2, o[4] - s2
    return [
        (even + odd, even - odd),
        (up + a, high + g),
        (eo[0] + minus, plus + eo[2]),
        (down + b, h - low),
        (ee[0] - ee[2], ee[1] - ee[3]),
        (down - b, h + low),
        (eo[0] - minus, plus - eo[2]),
        (up - a, g - high),
    ]


def cells16(u):
    (c0, c8), (c1, s1), (c2, s2), (c3, s3), (c4, s4), (c5, s5), (c6, s6), (c7, s7) = u
    even, odd = c0 + c8, c0 - c8
    ee = [even + c4, odd + s4, even - c4, odd - s4]
    m, p = ROOT * (c2 - c6), ROOT * (s2 + s6)
    eo = [c2 + c6, p + m, s2 - s6, p - m]
    e = [ee[n] + eo[n] for n in range(4)] + [ee[n] - eo[n] for n in range(4)]
    c17, c35, m17, m35 = c1 + c7, c3 + c5, c1 - c7, c3 - c5
    s17, s35, n17, n35 = s1 + s7, s3 + s5, s1 - s7, s3 - s5
    t1, r1 = BIG * m17 + SMALL * m35, SMALL * s17 + BIG * s35
    t2, r2 = ROOT * (c17 - c35), ROOT * (n17 + n35)
    t3, r3 = SMALL * m17 - BIG * m35, BIG * s17 - SMALL * s35
    o = [c17 + c35, r1 + t1, r2 + t2, r3 + t3, n17 - n35, r3 - t3, r2 - t2, r1 - t1]
    return [e[n] + o[n] for n in range(8)] + [e[n] - o[n] for n in range(8)]


def wave_groups(half):
    groups = []
    for g in range(STEPS // 2):
        orders = [0, 8] if g == 0 else [v for v in (g, STEPS - g) if v <= half]
        rows = []
        for order in orders:
            if order < half:
                rows.append((0, order, order))
            if order > 0:
                rows.append((1, order - 1, order))
        groups.append(rows)
    return groups


def wave_table(total, count, half, channels):
    fine = 128 // channels
    tables = []
    for d in range(count):
        rows = []
        for g, group in enumerate(wave_groups(half)):
            for sine, _, order in group:
                angle = 2 * np.pi * order * (count * np.arange(fine) + d) / total
                size = np.sqrt((1.0 if order == 0 else 2.0) / total)
                cos, sin = size * np.cos(angle), size * np.sin(angle)
                sign = 1.0 if order == g else -1.0
                first, last = (sin, sign * cos) if sine else (cos, -sign * sin)
                if g == 0:
                    zero = np.zeros(fine)
                    first, last = (first, zero) if order == 0 else (zero, first)
                rows.append(np.repeat(np.concatenate([first, last]), channels))
        tables.append(np.stack(rows))
    return np.stack(tables)


class Plan:
    def __init__(self, mesh, arg_shape, channels):
        self.nlon, self.nlat, self.nlead = (mesh.shape[n] for n in ("lon", "lat", "lead"))
        nz, ny, merged = arg_shape
        self.c = channels
        self.zl, self.yl = nz // self.nlead, ny // self.nlat
        self.nx = merged // channels
        self.xl = self.nx // self.nlon
        self.kp = MX // (self.nlon * self.nlat)
        self.kc = self.kp * channels
        self.lq = MY * MZ
        self.zy = self.zl * self.yl
        self.gain = math.sqrt(self.nx * ny * nz / MODES)
        eye_z, eye_l = np.eye(self.zl), np.eye(MY)
        by, bz = host_basis(ny, MY), host_basis(nz, MZ)
        c = channels
        self.groups = wave_groups(MX // 2)
        self.lon_table = halves(wave_table(self.nx, self.nlon, MX // 2, c)).transpose(1, 0, 2, 3)
        by_p = by.reshape(MY, self.nlat, self.yl)
        bz_s = bz.reshape(MZ, self.nlead, self.zl)
        self.lat_table = halves(
            np.einsum("lpy,zw->zlpwy", by_p, eye_z).reshape(self.zl * MY, self.nlat * self.zy)
        )
        lead = np.einsum("qsz,lm->slqzm", bz_s, eye_l)
        self.lead_table = halves(
            lead.reshape(self.nlead, self.lq, self.zl * MY).transpose(1, 0, 2).reshape(self.lq, -1)
        )
        self.lead_first = halves(
            np.einsum("qsz,yw->qyszw", bz_s, np.eye(self.yl)).reshape(MZ * self.yl, self.nlead * self.zy)
        )
        self.lat_last = halves(
            np.einsum("lpy,qr->lqpry", by_p, np.eye(MZ)).reshape(self.lq, self.nlat * MZ * self.yl)
        )
        self.lead_back = halves(
            lead.transpose(0, 3, 4, 1, 2).reshape(self.nlead, self.zl * MY, self.lq)
        )
        back = np.einsum("lpy,zw->pzywl", by_p, eye_z)
        self.lat_back = halves(back.reshape(self.nlat * self.zy, self.zl * MY))
        cc = c * c
        groups = 128 // c
        self.tile = np.concatenate(
            [np.kron(np.eye(groups)[:, [k]], np.tile(np.eye(c), (1, groups))) for k in range(groups)],
            axis=1,
        ).astype(ml_dtypes.bfloat16)
        wide = 256 // c
        self.fan = np.tile(np.eye(c), (1, wide)).astype(np.float32)
        self.block = np.kron(np.eye(wide), np.ones((c, c))).astype(np.float32)
        self.cc = cc


def peer(me, d):
    if d == 1:
        return me + 1 - 2 * lax.rem(me, 2)
    if d == 2:
        return lax.rem(me + 2, 4)
    return 3 - me


def products(plan, modes, chunk, tile, spread, product):
    pn = plan
    quarter = pn.lq // 4
    high, low = cut(modes[0, chunk])
    sh, sl = cut(modes[1, chunk])
    s4 = mm(sh, tile[...]) + mm(sl, tile[...])
    for k in range(pn.kp):
        part = slice(k * quarter, (k + 1) * quarter)
        whole = (slice(0, 3 * quarter), k, k * pn.lq)
        for source, which, offset in (whole, (part, pn.kp, k * pn.lq + 3 * quarter)):
            four = s4[source, which * 128 : (which + 1) * 128]
            two = jnp.concatenate([four, four], axis=1)
            rows = slice(offset, offset + four.shape[0])
            for j in range(pn.cc // 256):
                cols = slice(j * 256, (j + 1) * 256)
                table = spread[which, :, cols]
                product[rows, cols] = (mm(high[source], table) + mm(low[source], table)) * two


def remote_kernel(
    plan, act_h, pre_h, cot_h, weight, lw_h, lon_h, lat_th, lead_th, lead_fh, lat_lh, lead_bh, lat_bh, tile_h, fan_h, block_h,
    product, modes_out, grad_out, tile, spread,
    act, pre, cot, lw, lon_t, lat_t, lead_t, lead_f, lat_l, lead_b, lat_b, fan, block,
    h_out, loc_out, tt, xg, gs, sbuf, lonbuf, firstsend, firstrecv, leadbuf, latbuf, wbuf, vbuf,
    in_sem, wsem, lon_s, lon_r, first_s, first_r, next_s, next_r, g_s, g_r, v_s, v_r, f_s, f_r,
):
    pn = plan
    lon, lat, lead = (lax.axis_index(n) for n in ("lon", "lat", "lead"))
    mesh_id = pl.DeviceIdType.MESH
    other = 1 - lon
    barrier = pltpu.get_barrier_semaphore()
    pl.semaphore_signal(barrier, inc=1, device_id={"lon": other}, device_id_type=mesh_id)
    loads = []
    pairs = (
        (lon_h.at[lon], lon_t), (pre_h, pre), (cot_h, cot), (act_h, act), (lw_h, lw), (fan_h, fan),
        (block_h, block), (lat_th, lat_t), (lead_th, lead_t),
        (lead_fh, lead_f), (lat_lh, lat_l), (lead_bh, lead_b), (lat_bh, lat_b), (tile_h, tile),
    )
    for n, (source, target) in enumerate(pairs):
        copy = pltpu.make_async_copy(source, target, in_sem.at[n])
        copy.start()
        loads.append(copy)
        if n == 3:
            for d in range(1, pn.nlat):
                pl.semaphore_signal(
                    barrier, inc=1, device_id={"lat": lax.rem(lat + d, pn.nlat)}, device_id_type=mesh_id
                )
            for d in range(1, pn.nlead):
                pl.semaphore_signal(
                    barrier, inc=1, device_id={"lead": lax.rem(lead + d, pn.nlead)}, device_id_type=mesh_id
                )
    wcopy = pltpu.make_async_copy(
        weight.at[pl.ds(pl.multiple_of(lat * (pn.kp * pn.lq), 8), pn.kp * pn.lq), :], wbuf, wsem
    )
    c = pn.c
    zy = pn.zy
    lanes = lax.broadcasted_iota(jnp.int32, (c, 256), 1) % c
    mask = jnp.where(lanes == lax.broadcasted_iota(jnp.int32, (c, 256), 0), 1.0, 0.0).astype(BF16)
    loads[0].wait()
    for k in range(MX):
        for h in range(2):
            tt[h, k * c : (k + 1) * c, :] = lon_t[h, k : k + 1, :] * mask

    lon_copies = {}

    def along_lon(f, field):
        for n, (one, two) in enumerate(waves16(field)):
            for m, value in enumerate((one, two)):
                high, low = cut(value)
                xg[f, n, 0:zy, m * 128 : (m + 1) * 128] = high
                xg[f, n, zy : 2 * zy, m * 128 : (m + 1) * 128] = low
        first = 0
        deep = pn.kc // 2
        for n, rows in enumerate(pn.groups):
            part = slice(first, first + c * len(rows))
            p = mm(tt[0, part, :], xg[f, n], NT)
            q = mm(tt[1, part, :], xg[f, n, 0:zy], NT)
            total = p[:, 0:zy] + p[:, zy:] + q
            for m, (who, place, _) in enumerate(rows):
                base = place // pn.kp * deep
                for piece in range(0, c, 16):
                    at = place % pn.kp * c + piece
                    side = at // deep
                    sbuf[f, who, base + at - side * deep : base + at - side * deep + 16, side * zy : (side + 1) * zy] = (
                        total[m * c + piece : m * c + piece + 16]
                    )
            first += c * len(rows)
        if f == 1:
            pl.semaphore_wait(barrier, 1 + (pn.nlat - 1) + (pn.nlead - 1))
        copy = pltpu.make_async_remote_copy(
            src_ref=sbuf.at[f, other], dst_ref=lonbuf.at[f], send_sem=lon_s.at[f], recv_sem=lon_r.at[f],
            device_id={"lon": other}, device_id_type=mesh_id,
        )
        copy.start()
        lon_copies[f] = copy

    first_copies, next_copies, g_copies = {}, {}, {}

    def send(f, d, axis, source, target, send_sem, recv_sem):
        copy = pltpu.make_async_remote_copy(
            src_ref=source, dst_ref=target, send_sem=send_sem.at[f, d - 1], recv_sem=recv_sem.at[f, d - 1],
            device_id={axis: peer(lat if axis == "lat" else lead, d)}, device_id_type=mesh_id,
        )
        copy.start()
        return copy

    def send_first(f):
        axis, me = ("lat", lat) if f else ("lead", lead)
        lon_copies[f].wait()
        deep = pn.kc // 2
        for d in FAR + (0,):
            p = peer(me, d) if d else me
            rows = pl.ds(pl.multiple_of(p * deep, deep), deep)
            value = sbuf[f, lon, rows, :] + lonbuf[f, rows, :]
            if d == 0:
                firstrecv[f, me] = value
            else:
                firstsend[f, d - 1] = value
                first_copies[f, d] = send(
                    f, d, axis, firstsend.at[f, d - 1], firstrecv.at[f, me], first_s, first_r
                )

    loads[1].wait()
    loads[2].wait()
    columns = []
    for n in range(STEPS):
        cols = slice(n * 128, (n + 1) * 128)
        v = pre[:, cols].astype(F32)
        cdf = 0.5 * (1.0 + lax.erf(v * (1.0 / math.sqrt(2.0))))
        density = jnp.exp(-0.5 * v * v) * (1.0 / math.sqrt(2.0 * math.pi))
        grad = cot[:, cols].astype(F32) * (cdf + v * density)
        gh, gl = cut(grad)
        gs[0, :, cols] = gh
        gs[1, :, cols] = gl
        columns.append(grad)
    along_lon(1, columns)
    loads[3].wait()
    wcopy.start()
    along_lon(0, [act[:, n * 128 : (n + 1) * 128].astype(F32) for n in range(STEPS)])
    send_first(1)
    send_first(0)
    for copy in loads[4:]:
        copy.wait()
    highest = lax.Precision.HIGHEST
    left = lax.dot_general(fan[...], lw[...], (((0,), (1,)), ((), ())), precision=highest, preferred_element_type=F32)
    both = jnp.dot(left, fan[...], precision=highest, preferred_element_type=F32) * block[...]
    bh, bl = cut(both)
    for t in range(pn.xl * c // 256):
        cols = slice(t * 256, (t + 1) * 256)
        hi, lo = gs[0, :, cols], gs[1, :, cols]
        loc_out[:, cols] = mm(hi, bh) + mm(lo, bh) + mm(hi, bl)
    for k in range(pn.kp + 1):
        spread[k] = placed((128, pn.cc), 1, c, k * c)
    def send_next(f):
        axis, me, count, buf, table = (
            ("lead", lead, pn.nlat, leadbuf, lat_t) if f else ("lat", lat, pn.nlead, latbuf, lead_f)
        )
        for d in FAR:
            first_copies[f, d].wait()
        got = [firstrecv[f, p] for p in range(count)]
        wide = jnp.concatenate(
            [jnp.concatenate([v[:, side * zy : (side + 1) * zy] for v in got], axis=1) for side in range(2)], axis=0
        )
        buf[me] = fold(mm3((table[0], table[1]), wide, NT))
        for d in FAR:
            next_copies[f, d] = send(f, d, axis, buf.at[me], buf.at[me], next_s, next_r)

    send_next(1)
    send_next(0)

    def finish(f):
        axis, me, count, buf, table = (
            ("lat", lat, pn.nlead, leadbuf, lead_t) if f else ("lead", lead, pn.nlat, latbuf, lat_l)
        )
        for d in FAR:
            next_copies[f, d].wait()
        got = jnp.concatenate([unfold(buf[s]) for s in range(count)], axis=0)
        total = mm3((table[0], table[1]), got)
        if f == 1:
            total = total * pn.gain
        modes_out[f, me] = fold(total)
        for d in (FAR if f else (2, 1, 3)):
            g_copies[f, d] = send(f, d, axis, modes_out.at[f, me], modes_out.at[f, me], g_s, g_r)
        return total

    finish(0)
    spectral = finish(1)
    wcopy.wait()
    sh, sl = cut(spectral)
    pick = tile[0 : pn.kc, 0 : pn.kp * 128]
    wide = mm(sh, pick) + mm(sl, pick)
    adjoint = None
    for k in range(pn.kp):
        four = wide[:, k * 128 : (k + 1) * 128]
        prod = wbuf[k * pn.lq : (k + 1) * pn.lq, :] * jnp.concatenate([four] * (pn.cc // 128), axis=1)
        ph, plow = cut(prod)
        pick = placed((pn.cc, pn.kc), 0, c, k * c)
        term = mm(ph, pick) + mm(plow, pick)
        adjoint = term if adjoint is None else adjoint + term
    back = mm3((lead_b[0, lead], lead_b[1, lead]), adjoint)
    cells = mm3((lat_b[0], lat_b[1]), back)
    for p in range(pn.nlat):
        vbuf[p] = fold(cells[p * zy : (p + 1) * zy, :])
    h_out[lon, lat] = vbuf[lat]
    v_copies = {}
    for d in FAR:
        p = peer(lat, d)
        copy = pltpu.make_async_remote_copy(
            src_ref=vbuf.at[p], dst_ref=h_out.at[lon, lat],
            send_sem=v_s.at[d - 1], recv_sem=v_r.at[d - 1],
            device_id={"lat": p}, device_id_type=mesh_id,
        )
        copy.start()
        v_copies[d] = copy
    f_copies = []
    for d in range(pn.nlat):
        if d > 0:
            v_copies[d].wait_recv()
        s = peer(lat, d) if d else lat
        copy = pltpu.make_async_remote_copy(
            src_ref=h_out.at[lon, s], dst_ref=h_out.at[lon, s],
            send_sem=f_s.at[d], recv_sem=f_r.at[d],
            device_id={"lon": other}, device_id_type=mesh_id,
        )
        copy.start()
        f_copies.append(copy)
    for d in FAR:
        g_copies[1, d].wait()
    products(pn, modes_out, lead, tile, spread, product)
    for copy in f_copies:
        copy.wait()
    chunks = [[unfold(h_out[a, b]) for b in range(pn.nlat)] for a in range(pn.nlon)]
    waves = []
    first = 0
    for rows in pn.groups:
        part = slice(first, first + c * len(rows))
        pieces = []
        for who, place, _ in rows:
            at = place % pn.kp * c
            pieces.append(chunks[who][place // pn.kp][:, at : at + c])
        hh, hl = cut(jnp.concatenate(pieces, axis=1))
        wave = mm(hh, tt[0, part, :]) + mm(hl, tt[0, part, :]) + mm(hh, tt[1, part, :])
        waves.append((wave[:, :128], wave[:, 128:]))
        first += c * len(rows)
    for n, value in enumerate(cells16(waves)):
        cols = slice(n * 128, (n + 1) * 128)
        grad_out[:, cols] = (loc_out[:, cols] + value).astype(BF16)
    for d in FAR:
        v_copies[d].wait_send()
        g_copies[0, d].wait()


def finish_kernel(plan, product, modes, grad, tile, spread, grad_out, mode_grad, buf, sem, grad_sem):
    pn = plan
    lead = lax.axis_index("lead")
    size = pn.kp * pn.lq
    copies = []

    def write(source, p, n):
        rows = pl.ds(pl.multiple_of(p * size, size), size)
        copy = pltpu.make_async_copy(source, mode_grad.at[rows, :], sem.at[n])
        copy.start()
        copies.append(copy)

    write(product, lead, 0)
    copy = pltpu.make_async_copy(grad, grad_out, grad_sem)
    copy.start()
    copies.append(copy)
    for d in range(1, pn.nlat):
        p = peer(lead, d)
        products(pn, modes, p, tile, spread, buf.at[d - 1])
        write(buf.at[d - 1], p, d)
    for copy in copies:
        copy.wait()


def fast_device(plan, activation, pre_activation, cotangent, mode_weight, local_weight):
    pn = plan
    merged = activation.shape[2]
    flat = [v.reshape(pn.zy, merged) for v in (activation, pre_activation, cotangent)]
    vm = pl.BlockSpec(memory_space=pltpu.VMEM)
    hbm = pl.BlockSpec(memory_space=pltpu.HBM)
    half = MX // pn.nlon * pn.c
    dma = pltpu.SemaphoreType.DMA
    tables = (
        pn.lon_table, pn.lat_table, pn.lead_table, pn.lead_first, pn.lat_last, pn.lead_back, pn.lat_back,
        pn.tile, pn.fan, pn.block,
    )
    size = pn.kp * pn.lq
    product, modes, grad, tile, spread = pl.pallas_call(
        functools.partial(remote_kernel, pn),
        out_shape=(
            pltpu.VMEM((size, pn.cc), F32),
            pltpu.VMEM((2, pn.nlat, pn.lq // 4 * 3, 128), F32),
            pltpu.VMEM((pn.zy, merged), BF16),
            pltpu.VMEM(pn.tile.shape, BF16),
            pltpu.VMEM((pn.kp + 1, 128, pn.cc), BF16),
        ),
        in_specs=[hbm] * 15,
        out_specs=(vm,) * 5,
        scratch_shapes=[
            pltpu.VMEM((pn.zy, merged), BF16),
            pltpu.VMEM((pn.zy, merged), BF16),
            pltpu.VMEM((pn.zy, merged), BF16),
            pltpu.VMEM(local_weight.shape, F32),
            pltpu.VMEM(pn.lon_table.shape[1:], BF16),
        ]
        + [pltpu.VMEM(v.shape, v.dtype) for v in tables[1:7] + tables[8:]]
        + [
            pltpu.VMEM((pn.nlon, pn.nlat, pn.zy // 4 * 3, 128), F32),
            pltpu.VMEM((pn.zy, merged), F32),
            pltpu.VMEM((2, MX * pn.c, 256), BF16),
            pltpu.VMEM((2, STEPS // 2, 2 * pn.zy, 256), BF16),
            pltpu.VMEM((2, pn.zy, merged), BF16),
            pltpu.VMEM((2, pn.nlon, half // 2, 2 * pn.zy), F32),
            pltpu.VMEM((2, half // 2, 2 * pn.zy), F32),
            pltpu.VMEM((2, pn.nlat - 1, pn.kc // 2, 2 * pn.zy), F32),
            pltpu.VMEM((2, pn.nlat, pn.kc // 2, 2 * pn.zy), F32),
            pltpu.VMEM((pn.nlead, pn.zl * MY // 4 * 3, 128), F32),
            pltpu.VMEM((pn.nlat, pn.yl * MZ // 4 * 3, 128), F32),
            pltpu.VMEM((pn.kp * pn.lq, pn.cc), F32),
            pltpu.VMEM((pn.nlat, pn.zy // 4 * 3, 128), F32),
            dma((14,)), dma, dma((2,)), dma((2,)),
            dma((2, pn.nlat - 1)), dma((2, pn.nlat - 1)),
            dma((2, pn.nlead - 1)), dma((2, pn.nlead - 1)),
            dma((2, pn.nlat - 1)), dma((2, pn.nlat - 1)),
            dma((pn.nlat - 1,)), dma((pn.nlat - 1,)),
            dma((pn.nlat,)), dma((pn.nlat,)),
        ],
        compiler_params=pltpu.CompilerParams(
            collective_id=0, has_side_effects=True, vmem_limit_bytes=52 * 2**20
        ),
        name="modes",
    )(*flat, mode_weight, local_weight, *tables)
    grad, mode_grad = pl.pallas_call(
        functools.partial(finish_kernel, pn),
        out_shape=(
            jax.ShapeDtypeStruct((pn.zy, merged), BF16),
            jax.ShapeDtypeStruct((pn.nlat * size, pn.cc), F32),
        ),
        in_specs=[vm] * 5,
        out_specs=(hbm, hbm),
        scratch_shapes=[pltpu.VMEM((pn.nlat - 1, size, pn.cc), F32), dma((pn.nlat,)), dma],
        compiler_params=pltpu.CompilerParams(vmem_limit_bytes=24 * 2**20),
        name="finish",
    )(product, modes, grad, tile, spread)
    return grad.reshape(activation.shape), mode_grad


def solution(mesh):
    in_specs = (
        P("lead", "lat", "lon"),
        P("lead", "lat", "lon"),
        P("lead", "lat", "lon"),
        P("lon", None),
        P(),
    )
    out_specs = (P("lead", "lat", "lon"), P("lon", None))

    def whole(*args):
        shape = args[0].shape
        channels = args[4].shape[0]
        body = on_device
        if (
            mesh.shape["lon"] == 2
            and mesh.shape["lat"] == 4
            and mesh.shape["lead"] == 4
            and MX % (mesh.shape["lon"] * mesh.shape["lat"]) == 0
            and MX * MY * MZ == args[3].shape[0]
            and shape[2] == mesh.shape["lon"] * STEPS * 128
            and 4 * channels == 128
            and MX * channels == 96 * mesh.shape["lon"] * mesh.shape["lat"]
            and mesh.shape["lead"] * 4 == shape[0]
        ):
            body = functools.partial(fast_device, Plan(mesh, shape, channels))
        return jax.shard_map(
            body, mesh=mesh, in_specs=in_specs, out_specs=out_specs, check_vma=False
        )(*args)

    return whole
```

```python
import functools
import math

import jax
import jax.numpy as jnp
import ml_dtypes
import numpy as np
from jax import lax
from jax.experimental import pallas as pl
from jax.experimental.pallas import tpu as pltpu
from jax.sharding import PartitionSpec as P

MX = 24
MY = 24
MZ = 8
MODES = 4608


def make_basis(length, modes, start, count, stride):
    half = modes // 2
    order = jnp.arange(modes, dtype=jnp.int32)
    freq = jnp.where(order < half, order, order - half + 1)
    cells = start + stride * jnp.arange(count, dtype=jnp.int32)
    turns = freq[:, None] * cells[None, :] % length
    angle = 2.0 * math.pi / length * turns.astype(jnp.float32)
    waves = jnp.where(order[:, None] < half, jnp.cos(angle), jnp.sin(angle))
    weights = jnp.where(
        order == 0, jnp.float32(math.sqrt(1.0 / length)), jnp.float32(math.sqrt(2.0 / length))
    )
    return waves * weights[:, None]


def gelu_slope(value):
    normal_cdf = 0.5 * (1.0 + jax.scipy.special.erf(value / math.sqrt(2.0)))
    density = jnp.exp(-0.5 * value * value) / math.sqrt(2.0 * math.pi)
    return normal_cdf + value * density


def back_cells(coeffs, lon_basis, lat_basis, lead_basis):
    highest = lax.Precision.HIGHEST
    blocks = coeffs.reshape(
        lon_basis.shape[0], lat_basis.shape[0], lead_basis.shape[0], coeffs.shape[-1]
    )
    step = jnp.einsum("klqc,qz->zklc", blocks, lead_basis, precision=highest)
    step = jnp.einsum("zklc,ly->zykc", step, lat_basis, precision=highest)
    return jnp.einsum("zykc,kx->zyxc", step, lon_basis, precision=highest)


def on_device(activation, pre_activation, cotangent, mode_weight, local_weight):
    highest = lax.Precision.HIGHEST
    channels = local_weight.shape[0]
    lead_cells, lat_cells, merged = activation.shape
    lon_cells = merged // channels
    lon_count = lax.axis_size("lon")
    lon_total = lon_cells * lon_count
    lat_total = lat_cells * lax.axis_size("lat")
    lead_total = lead_cells * lax.axis_size("lead")
    lon_basis = make_basis(lon_total, MX, lax.axis_index("lon"), lon_cells, lon_count)
    lat_basis = make_basis(lat_total, MY, lax.axis_index("lat") * lat_cells, lat_cells, 1)
    lead_basis = make_basis(lead_total, MZ, lax.axis_index("lead") * lead_cells, lead_cells, 1)
    shape4 = (lead_cells, lat_cells, lon_cells, channels)
    grad_pre = cotangent.astype(jnp.float32).reshape(shape4) * gelu_slope(
        pre_activation.astype(jnp.float32).reshape(shape4)
    )
    stacked = jnp.concatenate([activation.astype(jnp.float32).reshape(shape4), grad_pre], axis=3)
    doubled = 2 * channels
    along_lon = jnp.einsum("zyxc,kx->zykc", stacked, lon_basis, precision=highest)
    along_lat = jnp.einsum("zykc,ly->zklc", along_lon, lat_basis, precision=highest)
    partial_sum = jnp.einsum("zklc,qz->klqc", along_lat, lead_basis, precision=highest).reshape(
        -1, doubled
    )
    summed = lax.psum(partial_sum, ("lat", "lead"))
    owned = lax.psum_scatter(summed, "lon", scatter_dimension=0, tiled=True)
    gain = math.sqrt(lon_total * lat_total * lead_total / MODES)
    coef = owned[:, :channels]
    spectral = gain * owned[:, channels:]
    owned_count = owned.shape[0]
    mode_grad = (coef[:, :, None] * spectral[:, None, :]).reshape(owned_count, channels * channels)
    mixing = mode_weight.reshape(owned_count, channels, channels)
    owned_adjoint = jnp.sum(mixing * spectral[:, None, :], axis=2)
    every_mode = lax.all_gather(owned_adjoint, "lon", axis=0, tiled=True)
    spread = back_cells(every_mode, lon_basis, lat_basis, lead_basis)
    local = jnp.einsum("zyxo,io->zyxi", grad_pre, local_weight, precision=highest)
    input_grad = (spread + local).reshape(lead_cells, lat_cells, merged)
    return (input_grad.astype(jnp.bfloat16), mode_grad)


F32 = jnp.float32
BF16 = jnp.bfloat16


def host_basis(length, modes):
    half = modes // 2
    order = np.arange(modes)
    freq = np.where(order < half, order, order - half + 1)
    turns = (freq[:, None] * np.arange(length)[None, :]) % length
    angle = 2.0 * np.pi / length * turns
    waves = np.where(order[:, None] < half, np.cos(angle), np.sin(angle))
    weights = np.where(order == 0, np.sqrt(1.0 / length), np.sqrt(2.0 / length))
    return waves * weights[:, None]


def halves(table):
    table = np.asarray(table, np.float32)
    high = table.astype(ml_dtypes.bfloat16)
    low = (table - high.astype(np.float32)).astype(ml_dtypes.bfloat16)
    return np.stack([high, low])


def cut(value):
    high = value.astype(BF16)
    return high, (value - high.astype(F32)).astype(BF16)


NN = (((1,), (0,)), ((), ()))
NT = (((1,), (1,)), ((), ()))


def mm(a, b, dims=NN):
    return lax.dot_general(a, b, dims, preferred_element_type=F32)


def mm3(table, b, dims=NN):
    bh, bl = cut(b)
    return mm(table[0], bh, dims) + mm(table[0], bl, dims) + mm(table[1], bh, dims)


def placed(shape, axis, channels, base):
    wide = lax.broadcasted_iota(jnp.int32, shape, axis) // channels
    narrow = lax.broadcasted_iota(jnp.int32, shape, 1 - axis) - base
    return jnp.where(wide == narrow, 1.0, 0.0).astype(BF16)


def fold(value):
    r, lanes = value.shape[0] // 4, value.shape[1] // 3
    last = jnp.concatenate([value[3 * r :, g * lanes : (g + 1) * lanes] for g in range(3)], axis=0)
    return jnp.concatenate([value[: 3 * r], last], axis=1)


def unfold(value):
    r, lanes = value.shape[0] // 3, value.shape[1] // 4
    last = jnp.concatenate([value[g * r : (g + 1) * r, 3 * lanes :] for g in range(3)], axis=1)
    return jnp.concatenate([value[:, : 3 * lanes], last], axis=0)


STEPS = 16
FAR = (3, 2, 1)
ROOT, BIG, SMALL = (float(np.cos(np.pi / v)) for v in (4, 8, 8 / 3))


def waves16(x):
    e = [x[n] + x[n + 8] for n in range(8)]
    o = [x[n] - x[n + 8] for n in range(8)]
    ee = [e[n] + e[n + 4] for n in range(4)]
    eo = [e[n] - e[n + 4] for n in range(4)]
    even, odd = ee[0] + ee[2], ee[1] + ee[3]
    minus, plus = ROOT * (eo[1] - eo[3]), ROOT * (eo[1] + eo[3])
    d1, d2, d3 = o[1] - o[7], ROOT * (o[2] - o[6]), o[3] - o[5]
    s1, s2, s3 = o[1] + o[7], ROOT * (o[2] + o[6]), o[3] + o[5]
    a, b = BIG * d1 + SMALL * d3, SMALL * d1 - BIG * d3
    g, h = SMALL * s1 + BIG * s3, BIG * s1 - SMALL * s3
    up, down = o[0] + d2, o[0] - d2
    high, low = o[4] + s2, o[4] - s2
    return [
        (even + odd, even - odd),
        (up + a, high + g),
        (eo[0] + minus, plus + eo[2]),
        (down + b, h - low),
        (ee[0] - ee[2], ee[1] - ee[3]),
        (down - b, h + low),
        (eo[0] - minus, plus - eo[2]),
        (up - a, g - high),
    ]


def cells16(u):
    (c0, c8), (c1, s1), (c2, s2), (c3, s3), (c4, s4), (c5, s5), (c6, s6), (c7, s7) = u
    even, odd = c0 + c8, c0 - c8
    ee = [even + c4, odd + s4, even - c4, odd - s4]
    m, p = ROOT * (c2 - c6), ROOT * (s2 + s6)
    eo = [c2 + c6, p + m, s2 - s6, p - m]
    e = [ee[n] + eo[n] for n in range(4)] + [ee[n] - eo[n] for n in range(4)]
    c17, c35, m17, m35 = c1 + c7, c3 + c5, c1 - c7, c3 - c5
    s17, s35, n17, n35 = s1 + s7, s3 + s5, s1 - s7, s3 - s5
    t1, r1 = BIG * m17 + SMALL * m35, SMALL * s17 + BIG * s35
    t2, r2 = ROOT * (c17 - c35), ROOT * (n17 + n35)
    t3, r3 = SMALL * m17 - BIG * m35, BIG * s17 - SMALL * s35
    o = [c17 + c35, r1 + t1, r2 + t2, r3 + t3, n17 - n35, r3 - t3, r2 - t2, r1 - t1]
    return [e[n] + o[n] for n in range(8)] + [e[n] - o[n] for n in range(8)]


def wave_groups(half):
    groups = []
    for g in range(STEPS // 2):
        orders = [0, 8] if g == 0 else [v for v in (g, STEPS - g) if v <= half]
        rows = []
        for order in orders:
            if order < half:
                rows.append((0, order, order))
            if order > 0:
                rows.append((1, order - 1, order))
        groups.append(rows)
    return groups


def wave_table(total, count, half, channels):
    fine = 128 // channels
    tables = []
    for d in range(count):
        rows = []
        for g, group in enumerate(wave_groups(half)):
            for sine, _, order in group:
                angle = 2 * np.pi * order * (count * np.arange(fine) + d) / total
                size = np.sqrt((1.0 if order == 0 else 2.0) / total)
                cos, sin = size * np.cos(angle), size * np.sin(angle)
                sign = 1.0 if order == g else -1.0
                first, last = (sin, sign * cos) if sine else (cos, -sign * sin)
                if g == 0:
                    zero = np.zeros(fine)
                    first, last = (first, zero) if order == 0 else (zero, first)
                rows.append(np.repeat(np.concatenate([first, last]), channels))
        tables.append(np.stack(rows))
    return np.stack(tables)


class Plan:
    def __init__(self, mesh, arg_shape, channels):
        self.nlon, self.nlat, self.nlead = (mesh.shape[n] for n in ("lon", "lat", "lead"))
        nz, ny, merged = arg_shape
        self.c = channels
        self.zl, self.yl = nz // self.nlead, ny // self.nlat
        self.nx = merged // channels
        self.xl = self.nx // self.nlon
        self.kp = MX // (self.nlon * self.nlat)
        self.kc = self.kp * channels
        self.lq = MY * MZ
        self.zy = self.zl * self.yl
        self.gain = math.sqrt(self.nx * ny * nz / MODES)
        eye_z, eye_l = np.eye(self.zl), np.eye(MY)
        by, bz = host_basis(ny, MY), host_basis(nz, MZ)
        c = channels
        self.groups = wave_groups(MX // 2)
        self.lon_table = halves(wave_table(self.nx, self.nlon, MX // 2, c)).transpose(1, 0, 2, 3)
        by_p = by.reshape(MY, self.nlat, self.yl)
        bz_s = bz.reshape(MZ, self.nlead, self.zl)
        self.lat_table = halves(
            np.einsum("lpy,zw->zlpwy", by_p, eye_z).reshape(self.zl * MY, self.nlat * self.zy)
        )
        lead = np.einsum("qsz,lm->slqzm", bz_s, eye_l)
        self.lead_table = halves(
            lead.reshape(self.nlead, self.lq, self.zl * MY).transpose(1, 0, 2).reshape(self.lq, -1)
        )
        self.lead_first = halves(
            np.einsum("qsz,yw->qyszw", bz_s, np.eye(self.yl)).reshape(MZ * self.yl, self.nlead * self.zy)
        )
        self.lat_last = halves(
            np.einsum("lpy,qr->lqpry", by_p, np.eye(MZ)).reshape(self.lq, self.nlat * MZ * self.yl)
        )
        self.lead_back = halves(
            lead.transpose(0, 3, 4, 1, 2).reshape(self.nlead, self.zl * MY, self.lq)
        )
        back = np.einsum("lpy,zw->pzywl", by_p, eye_z)
        self.lat_back = halves(back.reshape(self.nlat * self.zy, self.zl * MY))
        cc = c * c
        groups = 128 // c
        self.tile = np.concatenate(
            [np.kron(np.eye(groups)[:, [k]], np.tile(np.eye(c), (1, groups))) for k in range(groups)],
            axis=1,
        ).astype(ml_dtypes.bfloat16)
        wide = 256 // c
        self.fan = np.tile(np.eye(c), (1, wide)).astype(np.float32)
        self.block = np.kron(np.eye(wide), np.ones((c, c))).astype(np.float32)
        self.cc = cc


def peer(me, d):
    if d == 1:
        return me + 1 - 2 * lax.rem(me, 2)
    if d == 2:
        return lax.rem(me + 2, 4)
    return 3 - me


def products(plan, modes, chunk, tile, spread, product):
    pn = plan
    quarter = pn.lq // 4
    high, low = cut(modes[0, chunk])
    sh, sl = cut(modes[1, chunk])
    s4 = mm(sh, tile[...]) + mm(sl, tile[...])
    for k in range(pn.kp):
        part = slice(k * quarter, (k + 1) * quarter)
        whole = (slice(0, 3 * quarter), k, k * pn.lq)
        for source, which, offset in (whole, (part, pn.kp, k * pn.lq + 3 * quarter)):
            four = s4[source, which * 128 : (which + 1) * 128]
            two = jnp.concatenate([four, four], axis=1)
            rows = slice(offset, offset + four.shape[0])
            for j in range(pn.cc // 256):
                cols = slice(j * 256, (j + 1) * 256)
                table = spread[which, :, cols]
                product[rows, cols] = (mm(high[source], table) + mm(low[source], table)) * two


def remote_kernel(
    plan, act_h, pre_h, cot_h, weight, lw_h, lon_h, lat_th, lead_th, lead_fh, lat_lh, lead_bh, lat_bh, tile_h, fan_h, block_h,
    product, modes_out, grad_out, tile, spread,
    act, pre, cot, lw, lon_t, lat_t, lead_t, lead_f, lat_l, lead_b, lat_b, fan, block,
    h_out, loc_out, tt, xg, gs, sbuf, lonbuf, firstsend, firstrecv, leadbuf, latbuf, wbuf, vbuf,
    in_sem, wsem, lon_s, lon_r, first_s, first_r, next_s, next_r, g_s, g_r, v_s, v_r, f_s, f_r,
):
    pn = plan
    lon, lat, lead = (lax.axis_index(n) for n in ("lon", "lat", "lead"))
    mesh_id = pl.DeviceIdType.MESH
    other = 1 - lon
    barrier = pltpu.get_barrier_semaphore()
    pl.semaphore_signal(barrier, inc=1, device_id={"lon": other}, device_id_type=mesh_id)
    loads = []
    pairs = (
        (lon_h.at[lon], lon_t), (pre_h, pre), (cot_h, cot), (act_h, act), (lw_h, lw), (fan_h, fan),
        (block_h, block), (lat_th, lat_t), (lead_th, lead_t),
        (lead_fh, lead_f), (lat_lh, lat_l), (lead_bh, lead_b), (lat_bh, lat_b), (tile_h, tile),
    )
    for n, (source, target) in enumerate(pairs):
        copy = pltpu.make_async_copy(source, target, in_sem.at[n])
        copy.start()
        loads.append(copy)
        if n == 3:
            for d in range(1, pn.nlat):
                pl.semaphore_signal(
                    barrier, inc=1, device_id={"lat": lax.rem(lat + d, pn.nlat)}, device_id_type=mesh_id
                )
            for d in range(1, pn.nlead):
                pl.semaphore_signal(
                    barrier, inc=1, device_id={"lead": lax.rem(lead + d, pn.nlead)}, device_id_type=mesh_id
                )
    wcopy = pltpu.make_async_copy(
        weight.at[pl.ds(pl.multiple_of(lat * (pn.kp * pn.lq), 8), pn.kp * pn.lq), :], wbuf, wsem
    )
    c = pn.c
    zy = pn.zy
    lanes = lax.broadcasted_iota(jnp.int32, (c, 256), 1) % c
    mask = jnp.where(lanes == lax.broadcasted_iota(jnp.int32, (c, 256), 0), 1.0, 0.0).astype(BF16)
    loads[0].wait()
    for k in range(MX):
        for h in range(2):
            tt[h, k * c : (k + 1) * c, :] = lon_t[h, k : k + 1, :] * mask

    lon_copies = {}

    def along_lon(f, field):
        for n, (one, two) in enumerate(waves16(field)):
            for m, value in enumerate((one, two)):
                high, low = cut(value)
                xg[f, n, 0:zy, m * 128 : (m + 1) * 128] = high
                xg[f, n, zy : 2 * zy, m * 128 : (m + 1) * 128] = low
        first = 0
        deep = pn.kc // 2
        for n, rows in enumerate(pn.groups):
            part = slice(first, first + c * len(rows))
            p = mm(tt[0, part, :], xg[f, n], NT)
            q = mm(tt[1, part, :], xg[f, n, 0:zy], NT)
            total = p[:, 0:zy] + p[:, zy:] + q
            for m, (who, place, _) in enumerate(rows):
                base = place // pn.kp * deep
                for piece in range(0, c, 16):
                    at = place % pn.kp * c + piece
                    side = at // deep
                    sbuf[f, who, base + at - side * deep : base + at - side * deep + 16, side * zy : (side + 1) * zy] = (
                        total[m * c + piece : m * c + piece + 16]
                    )
            first += c * len(rows)
        if f == 1:
            pl.semaphore_wait(barrier, 1 + (pn.nlat - 1) + (pn.nlead - 1))
        copy = pltpu.make_async_remote_copy(
            src_ref=sbuf.at[f, other], dst_ref=lonbuf.at[f], send_sem=lon_s.at[f], recv_sem=lon_r.at[f],
            device_id={"lon": other}, device_id_type=mesh_id,
        )
        copy.start()
        lon_copies[f] = copy

    first_copies, next_copies, g_copies = {}, {}, {}

    def send(f, d, axis, source, target, send_sem, recv_sem, start=True):
        copy = pltpu.make_async_remote_copy(
            src_ref=source, dst_ref=target, send_sem=send_sem.at[f, d - 1], recv_sem=recv_sem.at[f, d - 1],
            device_id={axis: peer(lat if axis == "lat" else lead, d)}, device_id_type=mesh_id,
        )
        if start:
            copy.start()
        return copy

    def send_first(f):
        axis, me = ("lat", lat) if f else ("lead", lead)
        lon_copies[f].wait()
        deep = pn.kc // 2
        for d in FAR + (0,):
            p = peer(me, d) if d else me
            rows = pl.ds(pl.multiple_of(p * deep, deep), deep)
            value = sbuf[f, lon, rows, :] + lonbuf[f, rows, :]
            if d == 0:
                firstrecv[f, me] = value
            else:
                firstsend[f, d - 1] = value
                first_copies[f, d] = send(
                    f, d, axis, firstsend.at[f, d - 1], firstrecv.at[f, me], first_s, first_r
                )

    loads[1].wait()
    loads[2].wait()
    columns = []
    for n in range(STEPS):
        cols = slice(n * 128, (n + 1) * 128)
        v = pre[:, cols].astype(F32)
        cdf = 0.5 * (1.0 + lax.erf(v * (1.0 / math.sqrt(2.0))))
        density = jnp.exp(-0.5 * v * v) * (1.0 / math.sqrt(2.0 * math.pi))
        grad = cot[:, cols].astype(F32) * (cdf + v * density)
        gh, gl = cut(grad)
        gs[0, :, cols] = gh
        gs[1, :, cols] = gl
        columns.append(grad)
    along_lon(1, columns)
    loads[3].wait()
    wcopy.start()
    along_lon(0, [act[:, n * 128 : (n + 1) * 128].astype(F32) for n in range(STEPS)])
    send_first(1)
    send_first(0)
    for copy in loads[4:]:
        copy.wait()
    highest = lax.Precision.HIGHEST
    left = lax.dot_general(fan[...], lw[...], (((0,), (1,)), ((), ())), precision=highest, preferred_element_type=F32)
    both = jnp.dot(left, fan[...], precision=highest, preferred_element_type=F32) * block[...]
    bh, bl = cut(both)
    for t in range(pn.xl * c // 256):
        cols = slice(t * 256, (t + 1) * 256)
        hi, lo = gs[0, :, cols], gs[1, :, cols]
        loc_out[:, cols] = mm(hi, bh) + mm(lo, bh) + mm(hi, bl)
    for k in range(pn.kp + 1):
        spread[k] = placed((128, pn.cc), 1, c, k * c)
    def send_next(f):
        axis, me, count, buf, table = (
            ("lead", lead, pn.nlat, leadbuf, lat_t) if f else ("lat", lat, pn.nlead, latbuf, lead_f)
        )
        for d in FAR:
            first_copies[f, d].wait()
        got = [firstrecv[f, p] for p in range(count)]
        wide = jnp.concatenate(
            [jnp.concatenate([v[:, side * zy : (side + 1) * zy] for v in got], axis=1) for side in range(2)], axis=0
        )
        buf[me] = fold(mm3((table[0], table[1]), wide, NT))
        for d in FAR:
            next_copies[f, d] = send(f, d, axis, buf.at[me], buf.at[me], next_s, next_r)

    send_next(1)
    send_next(0)

    def start_last(core):
        @pl.when(lon == core)
        def _():
            for d in (2, 1, 3):
                g_copies[0, d].start()

    def finish(f):
        axis, me, count, buf, table = (
            ("lat", lat, pn.nlead, leadbuf, lead_t) if f else ("lead", lead, pn.nlat, latbuf, lat_l)
        )
        for d in FAR:
            next_copies[f, d].wait()
        got = jnp.concatenate([unfold(buf[s]) for s in range(count)], axis=0)
        total = mm3((table[0], table[1]), got)
        if f == 1:
            total = total * pn.gain
        modes_out[f, me] = fold(total)
        for d in (FAR if f else (2, 1, 3)):
            g_copies[f, d] = send(f, d, axis, modes_out.at[f, me], modes_out.at[f, me], g_s, g_r, f == 1)
        if f == 0:
            start_last(0)
        return total

    finish(0)
    spectral = finish(1)
    start_last(1)
    wcopy.wait()
    sh, sl = cut(spectral)
    pick = tile[0 : pn.kc, 0 : pn.kp * 128]
    wide = mm(sh, pick) + mm(sl, pick)
    adjoint = None
    for k in range(pn.kp):
        four = wide[:, k * 128 : (k + 1) * 128]
        prod = wbuf[k * pn.lq : (k + 1) * pn.lq, :] * jnp.concatenate([four] * (pn.cc // 128), axis=1)
        ph, plow = cut(prod)
        pick = placed((pn.cc, pn.kc), 0, c, k * c)
        term = mm(ph, pick) + mm(plow, pick)
        adjoint = term if adjoint is None else adjoint + term
    back = mm3((lead_b[0, lead], lead_b[1, lead]), adjoint)
    cells = mm3((lat_b[0], lat_b[1]), back)
    for p in range(pn.nlat):
        vbuf[p] = fold(cells[p * zy : (p + 1) * zy, :])
    h_out[lon, lat] = vbuf[lat]
    v_copies = {}
    for d in FAR:
        p = peer(lat, d)
        copy = pltpu.make_async_remote_copy(
            src_ref=vbuf.at[p], dst_ref=h_out.at[lon, lat],
            send_sem=v_s.at[d - 1], recv_sem=v_r.at[d - 1],
            device_id={"lat": p}, device_id_type=mesh_id,
        )
        copy.start()
        v_copies[d] = copy
    f_copies = []
    for d in range(pn.nlat):
        if d > 0:
            v_copies[d].wait_recv()
        s = peer(lat, d) if d else lat
        copy = pltpu.make_async_remote_copy(
            src_ref=h_out.at[lon, s], dst_ref=h_out.at[lon, s],
            send_sem=f_s.at[d], recv_sem=f_r.at[d],
            device_id={"lon": other}, device_id_type=mesh_id,
        )
        copy.start()
        f_copies.append(copy)
    for d in FAR:
        g_copies[1, d].wait()
    products(pn, modes_out, lead, tile, spread, product)
    for copy in f_copies:
        copy.wait()
    chunks = [[unfold(h_out[a, b]) for b in range(pn.nlat)] for a in range(pn.nlon)]
    waves = []
    first = 0
    for rows in pn.groups:
        part = slice(first, first + c * len(rows))
        pieces = []
        for who, place, _ in rows:
            at = place % pn.kp * c
            pieces.append(chunks[who][place // pn.kp][:, at : at + c])
        hh, hl = cut(jnp.concatenate(pieces, axis=1))
        wave = mm(hh, tt[0, part, :]) + mm(hl, tt[0, part, :]) + mm(hh, tt[1, part, :])
        waves.append((wave[:, :128], wave[:, 128:]))
        first += c * len(rows)
    for n, value in enumerate(cells16(waves)):
        cols = slice(n * 128, (n + 1) * 128)
        grad_out[:, cols] = (loc_out[:, cols] + value).astype(BF16)
    for d in FAR:
        v_copies[d].wait_send()
        g_copies[0, d].wait()


def finish_kernel(plan, product, modes, grad, tile, spread, grad_out, mode_grad, buf, sem, grad_sem):
    pn = plan
    lead = lax.axis_index("lead")
    size = pn.kp * pn.lq
    copies = []

    def write(source, p, n):
        rows = pl.ds(pl.multiple_of(p * size, size), size)
        copy = pltpu.make_async_copy(source, mode_grad.at[rows, :], sem.at[n])
        copy.start()
        copies.append(copy)

    write(product, lead, 0)
    copy = pltpu.make_async_copy(grad, grad_out, grad_sem)
    copy.start()
    copies.append(copy)
    for d in range(1, pn.nlat):
        p = peer(lead, d)
        products(pn, modes, p, tile, spread, buf.at[d - 1])
        write(buf.at[d - 1], p, d)
    for copy in copies:
        copy.wait()


def fast_device(plan, activation, pre_activation, cotangent, mode_weight, local_weight):
    pn = plan
    merged = activation.shape[2]
    flat = [v.reshape(pn.zy, merged) for v in (activation, pre_activation, cotangent)]
    vm = pl.BlockSpec(memory_space=pltpu.VMEM)
    hbm = pl.BlockSpec(memory_space=pltpu.HBM)
    half = MX // pn.nlon * pn.c
    dma = pltpu.SemaphoreType.DMA
    tables = (
        pn.lon_table, pn.lat_table, pn.lead_table, pn.lead_first, pn.lat_last, pn.lead_back, pn.lat_back,
        pn.tile, pn.fan, pn.block,
    )
    size = pn.kp * pn.lq
    product, modes, grad, tile, spread = pl.pallas_call(
        functools.partial(remote_kernel, pn),
        out_shape=(
            pltpu.VMEM((size, pn.cc), F32),
            pltpu.VMEM((2, pn.nlat, pn.lq // 4 * 3, 128), F32),
            pltpu.VMEM((pn.zy, merged), BF16),
            pltpu.VMEM(pn.tile.shape, BF16),
            pltpu.VMEM((pn.kp + 1, 128, pn.cc), BF16),
        ),
        in_specs=[hbm] * 15,
        out_specs=(vm,) * 5,
        scratch_shapes=[
            pltpu.VMEM((pn.zy, merged), BF16),
            pltpu.VMEM((pn.zy, merged), BF16),
            pltpu.VMEM((pn.zy, merged), BF16),
            pltpu.VMEM(local_weight.shape, F32),
            pltpu.VMEM(pn.lon_table.shape[1:], BF16),
        ]
        + [pltpu.VMEM(v.shape, v.dtype) for v in tables[1:7] + tables[8:]]
        + [
            pltpu.VMEM((pn.nlon, pn.nlat, pn.zy // 4 * 3, 128), F32),
            pltpu.VMEM((pn.zy, merged), F32),
            pltpu.VMEM((2, MX * pn.c, 256), BF16),
            pltpu.VMEM((2, STEPS // 2, 2 * pn.zy, 256), BF16),
            pltpu.VMEM((2, pn.zy, merged), BF16),
            pltpu.VMEM((2, pn.nlon, half // 2, 2 * pn.zy), F32),
            pltpu.VMEM((2, half // 2, 2 * pn.zy), F32),
            pltpu.VMEM((2, pn.nlat - 1, pn.kc // 2, 2 * pn.zy), F32),
            pltpu.VMEM((2, pn.nlat, pn.kc // 2, 2 * pn.zy), F32),
            pltpu.VMEM((pn.nlead, pn.zl * MY // 4 * 3, 128), F32),
            pltpu.VMEM((pn.nlat, pn.yl * MZ // 4 * 3, 128), F32),
            pltpu.VMEM((pn.kp * pn.lq, pn.cc), F32),
            pltpu.VMEM((pn.nlat, pn.zy // 4 * 3, 128), F32),
            dma((14,)), dma, dma((2,)), dma((2,)),
            dma((2, pn.nlat - 1)), dma((2, pn.nlat - 1)),
            dma((2, pn.nlead - 1)), dma((2, pn.nlead - 1)),
            dma((2, pn.nlat - 1)), dma((2, pn.nlat - 1)),
            dma((pn.nlat - 1,)), dma((pn.nlat - 1,)),
            dma((pn.nlat,)), dma((pn.nlat,)),
        ],
        compiler_params=pltpu.CompilerParams(
            collective_id=0, has_side_effects=True, vmem_limit_bytes=52 * 2**20
        ),
        name="modes",
    )(*flat, mode_weight, local_weight, *tables)
    grad, mode_grad = pl.pallas_call(
        functools.partial(finish_kernel, pn),
        out_shape=(
            jax.ShapeDtypeStruct((pn.zy, merged), BF16),
            jax.ShapeDtypeStruct((pn.nlat * size, pn.cc), F32),
        ),
        in_specs=[vm] * 5,
        out_specs=(hbm, hbm),
        scratch_shapes=[pltpu.VMEM((pn.nlat - 1, size, pn.cc), F32), dma((pn.nlat,)), dma],
        compiler_params=pltpu.CompilerParams(vmem_limit_bytes=24 * 2**20),
        name="finish",
    )(product, modes, grad, tile, spread)
    return grad.reshape(activation.shape), mode_grad


def solution(mesh):
    in_specs = (
        P("lead", "lat", "lon"),
        P("lead", "lat", "lon"),
        P("lead", "lat", "lon"),
        P("lon", None),
        P(),
    )
    out_specs = (P("lead", "lat", "lon"), P("lon", None))

    def whole(*args):
        shape = args[0].shape
        channels = args[4].shape[0]
        body = on_device
        if (
            mesh.shape["lon"] == 2
            and mesh.shape["lat"] == 4
            and mesh.shape["lead"] == 4
            and MX % (mesh.shape["lon"] * mesh.shape["lat"]) == 0
            and MX * MY * MZ == args[3].shape[0]
            and shape[2] == mesh.shape["lon"] * STEPS * 128
            and 4 * channels == 128
            and MX * channels == 96 * mesh.shape["lon"] * mesh.shape["lat"]
            and mesh.shape["lead"] * 4 == shape[0]
        ):
            body = functools.partial(fast_device, Plan(mesh, shape, channels))
        return jax.shard_map(
            body, mesh=mesh, in_specs=in_specs, out_specs=out_specs, check_vma=False
        )(*args)

    return whole
```

```python
import functools
import math

import jax
import jax.numpy as jnp
import ml_dtypes
import numpy as np
from jax import lax
from jax.experimental import pallas as pl
from jax.experimental.pallas import tpu as pltpu
from jax.sharding import PartitionSpec as P

MX = 24
MY = 24
MZ = 8
MODES = 4608


def make_basis(length, modes, start, count, stride):
    half = modes // 2
    order = jnp.arange(modes, dtype=jnp.int32)
    freq = jnp.where(order < half, order, order - half + 1)
    cells = start + stride * jnp.arange(count, dtype=jnp.int32)
    turns = freq[:, None] * cells[None, :] % length
    angle = 2.0 * math.pi / length * turns.astype(jnp.float32)
    waves = jnp.where(order[:, None] < half, jnp.cos(angle), jnp.sin(angle))
    weights = jnp.where(
        order == 0, jnp.float32(math.sqrt(1.0 / length)), jnp.float32(math.sqrt(2.0 / length))
    )
    return waves * weights[:, None]


def gelu_slope(value):
    normal_cdf = 0.5 * (1.0 + jax.scipy.special.erf(value / math.sqrt(2.0)))
    density = jnp.exp(-0.5 * value * value) / math.sqrt(2.0 * math.pi)
    return normal_cdf + value * density


def back_cells(coeffs, lon_basis, lat_basis, lead_basis):
    highest = lax.Precision.HIGHEST
    blocks = coeffs.reshape(
        lon_basis.shape[0], lat_basis.shape[0], lead_basis.shape[0], coeffs.shape[-1]
    )
    step = jnp.einsum("klqc,qz->zklc", blocks, lead_basis, precision=highest)
    step = jnp.einsum("zklc,ly->zykc", step, lat_basis, precision=highest)
    return jnp.einsum("zykc,kx->zyxc", step, lon_basis, precision=highest)


def on_device(activation, pre_activation, cotangent, mode_weight, local_weight):
    highest = lax.Precision.HIGHEST
    channels = local_weight.shape[0]
    lead_cells, lat_cells, merged = activation.shape
    lon_cells = merged // channels
    lon_count = lax.axis_size("lon")
    lon_total = lon_cells * lon_count
    lat_total = lat_cells * lax.axis_size("lat")
    lead_total = lead_cells * lax.axis_size("lead")
    lon_basis = make_basis(lon_total, MX, lax.axis_index("lon"), lon_cells, lon_count)
    lat_basis = make_basis(lat_total, MY, lax.axis_index("lat") * lat_cells, lat_cells, 1)
    lead_basis = make_basis(lead_total, MZ, lax.axis_index("lead") * lead_cells, lead_cells, 1)
    shape4 = (lead_cells, lat_cells, lon_cells, channels)
    grad_pre = cotangent.astype(jnp.float32).reshape(shape4) * gelu_slope(
        pre_activation.astype(jnp.float32).reshape(shape4)
    )
    stacked = jnp.concatenate([activation.astype(jnp.float32).reshape(shape4), grad_pre], axis=3)
    doubled = 2 * channels
    along_lon = jnp.einsum("zyxc,kx->zykc", stacked, lon_basis, precision=highest)
    along_lat = jnp.einsum("zykc,ly->zklc", along_lon, lat_basis, precision=highest)
    partial_sum = jnp.einsum("zklc,qz->klqc", along_lat, lead_basis, precision=highest).reshape(
        -1, doubled
    )
    summed = lax.psum(partial_sum, ("lat", "lead"))
    owned = lax.psum_scatter(summed, "lon", scatter_dimension=0, tiled=True)
    gain = math.sqrt(lon_total * lat_total * lead_total / MODES)
    coef = owned[:, :channels]
    spectral = gain * owned[:, channels:]
    owned_count = owned.shape[0]
    mode_grad = (coef[:, :, None] * spectral[:, None, :]).reshape(owned_count, channels * channels)
    mixing = mode_weight.reshape(owned_count, channels, channels)
    owned_adjoint = jnp.sum(mixing * spectral[:, None, :], axis=2)
    every_mode = lax.all_gather(owned_adjoint, "lon", axis=0, tiled=True)
    spread = back_cells(every_mode, lon_basis, lat_basis, lead_basis)
    local = jnp.einsum("zyxo,io->zyxi", grad_pre, local_weight, precision=highest)
    input_grad = (spread + local).reshape(lead_cells, lat_cells, merged)
    return (input_grad.astype(jnp.bfloat16), mode_grad)


F32 = jnp.float32
BF16 = jnp.bfloat16


def host_basis(length, modes):
    half = modes // 2
    order = np.arange(modes)
    freq = np.where(order < half, order, order - half + 1)
    turns = (freq[:, None] * np.arange(length)[None, :]) % length
    angle = 2.0 * np.pi / length * turns
    waves = np.where(order[:, None] < half, np.cos(angle), np.sin(angle))
    weights = np.where(order == 0, np.sqrt(1.0 / length), np.sqrt(2.0 / length))
    return waves * weights[:, None]


def halves(table):
    table = np.asarray(table, np.float32)
    high = table.astype(ml_dtypes.bfloat16)
    low = (table - high.astype(np.float32)).astype(ml_dtypes.bfloat16)
    return np.stack([high, low])


def cut(value):
    high = value.astype(BF16)
    return high, (value - high.astype(F32)).astype(BF16)


NN = (((1,), (0,)), ((), ()))
NT = (((1,), (1,)), ((), ()))


def mm(a, b, dims=NN):
    return lax.dot_general(a, b, dims, preferred_element_type=F32)


def mm3(table, b, dims=NN):
    bh, bl = cut(b)
    return mm(table[0], bh, dims) + mm(table[0], bl, dims) + mm(table[1], bh, dims)


def placed(shape, axis, channels, base):
    wide = lax.broadcasted_iota(jnp.int32, shape, axis) // channels
    narrow = lax.broadcasted_iota(jnp.int32, shape, 1 - axis) - base
    return jnp.where(wide == narrow, 1.0, 0.0).astype(BF16)


def fold(value):
    r, lanes = value.shape[0] // 4, value.shape[1] // 3
    last = jnp.concatenate([value[3 * r :, g * lanes : (g + 1) * lanes] for g in range(3)], axis=0)
    return jnp.concatenate([value[: 3 * r], last], axis=1)


def unfold(value):
    r, lanes = value.shape[0] // 3, value.shape[1] // 4
    last = jnp.concatenate([value[g * r : (g + 1) * r, 3 * lanes :] for g in range(3)], axis=1)
    return jnp.concatenate([value[:, : 3 * lanes], last], axis=0)


STEPS = 16
FAR = (3, 2, 1)
ROOT, BIG, SMALL = (float(np.cos(np.pi / v)) for v in (4, 8, 8 / 3))


def waves16(x):
    e = [x[n] + x[n + 8] for n in range(8)]
    o = [x[n] - x[n + 8] for n in range(8)]
    ee = [e[n] + e[n + 4] for n in range(4)]
    eo = [e[n] - e[n + 4] for n in range(4)]
    even, odd = ee[0] + ee[2], ee[1] + ee[3]
    minus, plus = ROOT * (eo[1] - eo[3]), ROOT * (eo[1] + eo[3])
    d1, d2, d3 = o[1] - o[7], ROOT * (o[2] - o[6]), o[3] - o[5]
    s1, s2, s3 = o[1] + o[7], ROOT * (o[2] + o[6]), o[3] + o[5]
    a, b = BIG * d1 + SMALL * d3, SMALL * d1 - BIG * d3
    g, h = SMALL * s1 + BIG * s3, BIG * s1 - SMALL * s3
    up, down = o[0] + d2, o[0] - d2
    high, low = o[4] + s2, o[4] - s2
    return [
        (even + odd, even - odd),
        (up + a, high + g),
        (eo[0] + minus, plus + eo[2]),
        (down + b, h - low),
        (ee[0] - ee[2], ee[1] - ee[3]),
        (down - b, h + low),
        (eo[0] - minus, plus - eo[2]),
        (up - a, g - high),
    ]


def cells16(u):
    (c0, c8), (c1, s1), (c2, s2), (c3, s3), (c4, s4), (c5, s5), (c6, s6), (c7, s7) = u
    even, odd = c0 + c8, c0 - c8
    ee = [even + c4, odd + s4, even - c4, odd - s4]
    m, p = ROOT * (c2 - c6), ROOT * (s2 + s6)
    eo = [c2 + c6, p + m, s2 - s6, p - m]
    e = [ee[n] + eo[n] for n in range(4)] + [ee[n] - eo[n] for n in range(4)]
    c17, c35, m17, m35 = c1 + c7, c3 + c5, c1 - c7, c3 - c5
    s17, s35, n17, n35 = s1 + s7, s3 + s5, s1 - s7, s3 - s5
    t1, r1 = BIG * m17 + SMALL * m35, SMALL * s17 + BIG * s35
    t2, r2 = ROOT * (c17 - c35), ROOT * (n17 + n35)
    t3, r3 = SMALL * m17 - BIG * m35, BIG * s17 - SMALL * s35
    o = [c17 + c35, r1 + t1, r2 + t2, r3 + t3, n17 - n35, r3 - t3, r2 - t2, r1 - t1]
    return [e[n] + o[n] for n in range(8)] + [e[n] - o[n] for n in range(8)]


def wave_groups(half):
    groups = []
    for g in range(STEPS // 2):
        orders = [0, 8] if g == 0 else [v for v in (g, STEPS - g) if v <= half]
        rows = []
        for order in orders:
            if order < half:
                rows.append((0, order, order))
            if order > 0:
                rows.append((1, order - 1, order))
        groups.append(rows)
    return groups


def wave_table(total, count, half, channels):
    fine = 128 // channels
    tables = []
    for d in range(count):
        rows = []
        for g, group in enumerate(wave_groups(half)):
            for sine, _, order in group:
                angle = 2 * np.pi * order * (count * np.arange(fine) + d) / total
                size = np.sqrt((1.0 if order == 0 else 2.0) / total)
                cos, sin = size * np.cos(angle), size * np.sin(angle)
                sign = 1.0 if order == g else -1.0
                first, last = (sin, sign * cos) if sine else (cos, -sign * sin)
                if g == 0:
                    zero = np.zeros(fine)
                    first, last = (first, zero) if order == 0 else (zero, first)
                rows.append(np.repeat(np.concatenate([first, last]), channels))
        tables.append(np.stack(rows))
    return np.stack(tables)


class Plan:
    def __init__(self, mesh, arg_shape, channels):
        self.nlon, self.nlat, self.nlead = (mesh.shape[n] for n in ("lon", "lat", "lead"))
        nz, ny, merged = arg_shape
        self.c = channels
        self.zl, self.yl = nz // self.nlead, ny // self.nlat
        self.nx = merged // channels
        self.xl = self.nx // self.nlon
        self.kp = MX // (self.nlon * self.nlat)
        self.kc = self.kp * channels
        self.lq = MY * MZ
        self.zy = self.zl * self.yl
        self.gain = math.sqrt(self.nx * ny * nz / MODES)
        eye_z, eye_l = np.eye(self.zl), np.eye(MY)
        by, bz = host_basis(ny, MY), host_basis(nz, MZ)
        c = channels
        self.groups = wave_groups(MX // 2)
        self.lon_table = halves(wave_table(self.nx, self.nlon, MX // 2, c)).transpose(1, 0, 2, 3)
        by_p = by.reshape(MY, self.nlat, self.yl)
        bz_s = bz.reshape(MZ, self.nlead, self.zl)
        self.lat_table = halves(
            np.einsum("lpy,zw->zlpwy", by_p, eye_z).reshape(self.zl * MY, self.nlat * self.zy)
        )
        lead = np.einsum("qsz,lm->slqzm", bz_s, eye_l)
        self.lead_table = halves(
            lead.reshape(self.nlead, self.lq, self.zl * MY).transpose(1, 0, 2).reshape(self.lq, -1)
        )
        self.lead_first = halves(
            np.einsum("qsz,yw->qyszw", bz_s, np.eye(self.yl)).reshape(MZ * self.yl, self.nlead * self.zy)
        )
        self.lat_last = halves(
            np.einsum("lpy,qr->lqpry", by_p, np.eye(MZ)).reshape(self.lq, self.nlat * MZ * self.yl)
        )
        self.lead_back = halves(
            lead.transpose(0, 3, 4, 1, 2).reshape(self.nlead, self.zl * MY, self.lq)
        )
        back = np.einsum("lpy,zw->pzywl", by_p, eye_z)
        self.lat_back = halves(back.reshape(self.nlat * self.zy, self.zl * MY))
        cc = c * c
        groups = 128 // c
        self.tile = np.concatenate(
            [np.kron(np.eye(groups)[:, [k]], np.tile(np.eye(c), (1, groups))) for k in range(groups)],
            axis=1,
        ).astype(ml_dtypes.bfloat16)
        wide = 256 // c
        self.fan = np.tile(np.eye(c), (1, wide)).astype(np.float32)
        self.block = np.kron(np.eye(wide), np.ones((c, c))).astype(np.float32)
        self.cc = cc


def peer(me, d):
    if d == 1:
        return me + 1 - 2 * lax.rem(me, 2)
    if d == 2:
        return lax.rem(me + 2, 4)
    return 3 - me


def products(plan, modes, chunk, tile, spread, product):
    pn = plan
    quarter = pn.lq // 4
    high, low = cut(modes[0, chunk])
    sh, sl = cut(modes[1, chunk])
    s4 = mm(sh, tile[...]) + mm(sl, tile[...])
    for k in range(pn.kp):
        part = slice(k * quarter, (k + 1) * quarter)
        whole = (slice(0, 3 * quarter), k, k * pn.lq)
        for source, which, offset in (whole, (part, pn.kp, k * pn.lq + 3 * quarter)):
            four = s4[source, which * 128 : (which + 1) * 128]
            two = jnp.concatenate([four, four], axis=1)
            rows = slice(offset, offset + four.shape[0])
            for j in range(pn.cc // 256):
                cols = slice(j * 256, (j + 1) * 256)
                table = spread[which, :, cols]
                product[rows, cols] = (mm(high[source], table) + mm(low[source], table)) * two


def remote_kernel(
    plan, act_h, pre_h, cot_h, weight, lw_h, lon_h, lat_th, lead_th, lead_fh, lat_lh, lead_bh, lat_bh, tile_h, fan_h, block_h,
    product, modes_out, grad_out, tile, spread,
    act, pre, cot, lw, lon_t, lat_t, lead_t, lead_f, lat_l, lead_b, lat_b, fan, block,
    h_out, loc_out, tt, xg, gs, sbuf, lonbuf, firstsend, firstrecv, leadbuf, latbuf, wbuf, vbuf,
    in_sem, wsem, lon_s, lon_r, first_s, first_r, next_s, next_r, g_s, g_r, v_s, v_r, f_s, f_r,
):
    pn = plan
    lon, lat, lead = (lax.axis_index(n) for n in ("lon", "lat", "lead"))
    mesh_id = pl.DeviceIdType.MESH
    other = 1 - lon
    barrier = pltpu.get_barrier_semaphore()
    pl.semaphore_signal(barrier, inc=1, device_id={"lon": other}, device_id_type=mesh_id)
    loads = []
    pairs = (
        (lon_h.at[lon], lon_t), (pre_h, pre), (cot_h, cot), (act_h, act), (lw_h, lw), (fan_h, fan),
        (block_h, block), (lat_th, lat_t), (lead_th, lead_t),
        (lead_fh, lead_f), (lat_lh, lat_l), (lead_bh, lead_b), (lat_bh, lat_b), (tile_h, tile),
    )
    for n, (source, target) in enumerate(pairs):
        copy = pltpu.make_async_copy(source, target, in_sem.at[n])
        copy.start()
        loads.append(copy)
        if n == 3:
            for d in range(1, pn.nlat):
                pl.semaphore_signal(
                    barrier, inc=1, device_id={"lat": lax.rem(lat + d, pn.nlat)}, device_id_type=mesh_id
                )
            for d in range(1, pn.nlead):
                pl.semaphore_signal(
                    barrier, inc=1, device_id={"lead": lax.rem(lead + d, pn.nlead)}, device_id_type=mesh_id
                )
    wcopy = pltpu.make_async_copy(
        weight.at[pl.ds(pl.multiple_of(lat * (pn.kp * pn.lq), 8), pn.kp * pn.lq), :], wbuf, wsem
    )
    c = pn.c
    zy = pn.zy
    lanes = lax.broadcasted_iota(jnp.int32, (c, 256), 1) % c
    mask = jnp.where(lanes == lax.broadcasted_iota(jnp.int32, (c, 256), 0), 1.0, 0.0).astype(BF16)
    loads[0].wait()
    for k in range(MX):
        for h in range(2):
            tt[h, k * c : (k + 1) * c, :] = lon_t[h, k : k + 1, :] * mask

    lon_copies = {}

    def along_lon(f, field):
        for n, (one, two) in enumerate(waves16(field)):
            for m, value in enumerate((one, two)):
                high, low = cut(value)
                xg[f, n, 0:zy, m * 128 : (m + 1) * 128] = high
                xg[f, n, zy : 2 * zy, m * 128 : (m + 1) * 128] = low
        first = 0
        deep = pn.kc // 2
        for n, rows in enumerate(pn.groups):
            part = slice(first, first + c * len(rows))
            p = mm(tt[0, part, :], xg[f, n], NT)
            q = mm(tt[1, part, :], xg[f, n, 0:zy], NT)
            total = p[:, 0:zy] + p[:, zy:] + q
            for m, (who, place, _) in enumerate(rows):
                base = place // pn.kp * deep
                for piece in range(0, c, 16):
                    at = place % pn.kp * c + piece
                    side = at // deep
                    sbuf[f, who, base + at - side * deep : base + at - side * deep + 16, side * zy : (side + 1) * zy] = (
                        total[m * c + piece : m * c + piece + 16]
                    )
            first += c * len(rows)
        if f == 1:
            pl.semaphore_wait(barrier, 1 + (pn.nlat - 1) + (pn.nlead - 1))
        copy = pltpu.make_async_remote_copy(
            src_ref=sbuf.at[f, other], dst_ref=lonbuf.at[f], send_sem=lon_s.at[f], recv_sem=lon_r.at[f],
            device_id={"lon": other}, device_id_type=mesh_id,
        )
        copy.start()
        lon_copies[f] = copy

    first_copies, next_copies, g_copies = {}, {}, {}

    def send(f, d, axis, source, target, send_sem, recv_sem):
        copy = pltpu.make_async_remote_copy(
            src_ref=source, dst_ref=target, send_sem=send_sem.at[f, d - 1], recv_sem=recv_sem.at[f, d - 1],
            device_id={axis: peer(lat if axis == "lat" else lead, d)}, device_id_type=mesh_id,
        )
        copy.start()
        return copy

    def send_first(f):
        axis, me = ("lat", lat) if f else ("lead", lead)
        lon_copies[f].wait()
        deep = pn.kc // 2
        for d in FAR + (0,):
            p = peer(me, d) if d else me
            rows = pl.ds(pl.multiple_of(p * deep, deep), deep)
            value = sbuf[f, lon, rows, :] + lonbuf[f, rows, :]
            if d == 0:
                firstrecv[f, me] = value
            else:
                firstsend[f, d - 1] = value
                first_copies[f, d] = send(
                    f, d, axis, firstsend.at[f, d - 1], firstrecv.at[f, me], first_s, first_r
                )

    loads[1].wait()
    loads[2].wait()
    columns = []
    for n in range(STEPS):
        cols = slice(n * 128, (n + 1) * 128)
        v = pre[:, cols].astype(F32)
        cdf = 0.5 * (1.0 + lax.erf(v * (1.0 / math.sqrt(2.0))))
        density = jnp.exp(-0.5 * v * v) * (1.0 / math.sqrt(2.0 * math.pi))
        grad = cot[:, cols].astype(F32) * (cdf + v * density)
        gh, gl = cut(grad)
        gs[0, :, cols] = gh
        gs[1, :, cols] = gl
        columns.append(grad)
    along_lon(1, columns)
    loads[3].wait()
    wcopy.start()
    along_lon(0, [act[:, n * 128 : (n + 1) * 128].astype(F32) for n in range(STEPS)])
    send_first(1)
    send_first(0)
    for copy in loads[4:]:
        copy.wait()
    highest = lax.Precision.HIGHEST
    left = lax.dot_general(fan[...], lw[...], (((0,), (1,)), ((), ())), precision=highest, preferred_element_type=F32)
    both = jnp.dot(left, fan[...], precision=highest, preferred_element_type=F32) * block[...]
    bh, bl = cut(both)
    for t in range(pn.xl * c // 256):
        cols = slice(t * 256, (t + 1) * 256)
        hi, lo = gs[0, :, cols], gs[1, :, cols]
        loc_out[:, cols] = mm(hi, bh) + mm(lo, bh) + mm(hi, bl)
    for k in range(pn.kp + 1):
        spread[k] = placed((128, pn.cc), 1, c, k * c)
    def send_next(f):
        axis, me, count, buf, table = (
            ("lead", lead, pn.nlat, leadbuf, lat_t) if f else ("lat", lat, pn.nlead, latbuf, lead_f)
        )
        for d in FAR:
            first_copies[f, d].wait()
        got = [firstrecv[f, p] for p in range(count)]
        wide = jnp.concatenate(
            [jnp.concatenate([v[:, side * zy : (side + 1) * zy] for v in got], axis=1) for side in range(2)], axis=0
        )
        buf[me] = fold(mm3((table[0], table[1]), wide, NT))
        for d in (2, 1, 3) if f else FAR:
            next_copies[f, d] = send(f, d, axis, buf.at[me], buf.at[me], next_s, next_r)

    send_next(1)
    send_next(0)

    def finish(f):
        axis, me, count, buf, table = (
            ("lat", lat, pn.nlead, leadbuf, lead_t) if f else ("lead", lead, pn.nlat, latbuf, lat_l)
        )
        for d in FAR:
            next_copies[f, d].wait()
        got = jnp.concatenate([unfold(buf[s]) for s in range(count)], axis=0)
        total = mm3((table[0], table[1]), got)
        if f == 1:
            total = total * pn.gain
        modes_out[f, me] = fold(total)
        for d in (FAR if f else (2, 1, 3)):
            g_copies[f, d] = send(f, d, axis, modes_out.at[f, me], modes_out.at[f, me], g_s, g_r)
        return total

    finish(0)
    spectral = finish(1)
    wcopy.wait()
    sh, sl = cut(spectral)
    pick = tile[0 : pn.kc, 0 : pn.kp * 128]
    wide = mm(sh, pick) + mm(sl, pick)
    adjoint = None
    for k in range(pn.kp):
        four = wide[:, k * 128 : (k + 1) * 128]
        prod = wbuf[k * pn.lq : (k + 1) * pn.lq, :] * jnp.concatenate([four] * (pn.cc // 128), axis=1)
        ph, plow = cut(prod)
        pick = placed((pn.cc, pn.kc), 0, c, k * c)
        term = mm(ph, pick) + mm(plow, pick)
        adjoint = term if adjoint is None else adjoint + term
    back = mm3((lead_b[0, lead], lead_b[1, lead]), adjoint)
    cells = mm3((lat_b[0], lat_b[1]), back)
    for p in range(pn.nlat):
        vbuf[p] = fold(cells[p * zy : (p + 1) * zy, :])
    h_out[lon, lat] = vbuf[lat]
    v_copies = {}
    for d in FAR:
        p = peer(lat, d)
        copy = pltpu.make_async_remote_copy(
            src_ref=vbuf.at[p], dst_ref=h_out.at[lon, lat],
            send_sem=v_s.at[d - 1], recv_sem=v_r.at[d - 1],
            device_id={"lat": p}, device_id_type=mesh_id,
        )
        copy.start()
        v_copies[d] = copy
    f_copies = []
    for d in range(pn.nlat):
        if d > 0:
            v_copies[d].wait_recv()
        s = peer(lat, d) if d else lat
        copy = pltpu.make_async_remote_copy(
            src_ref=h_out.at[lon, s], dst_ref=h_out.at[lon, s],
            send_sem=f_s.at[d], recv_sem=f_r.at[d],
            device_id={"lon": other}, device_id_type=mesh_id,
        )
        copy.start()
        f_copies.append(copy)
    for d in FAR:
        g_copies[1, d].wait()
    products(pn, modes_out, lead, tile, spread, product)
    for copy in f_copies:
        copy.wait()
    chunks = [[unfold(h_out[a, b]) for b in range(pn.nlat)] for a in range(pn.nlon)]
    waves = []
    first = 0
    for rows in pn.groups:
        part = slice(first, first + c * len(rows))
        pieces = []
        for who, place, _ in rows:
            at = place % pn.kp * c
            pieces.append(chunks[who][place // pn.kp][:, at : at + c])
        hh, hl = cut(jnp.concatenate(pieces, axis=1))
        wave = mm(hh, tt[0, part, :]) + mm(hl, tt[0, part, :]) + mm(hh, tt[1, part, :])
        waves.append((wave[:, :128], wave[:, 128:]))
        first += c * len(rows)
    for n, value in enumerate(cells16(waves)):
        cols = slice(n * 128, (n + 1) * 128)
        grad_out[:, cols] = (loc_out[:, cols] + value).astype(BF16)
    for d in FAR:
        v_copies[d].wait_send()
        g_copies[0, d].wait()


def finish_kernel(plan, product, modes, grad, tile, spread, grad_out, mode_grad, buf, sem, grad_sem):
    pn = plan
    lead = lax.axis_index("lead")
    size = pn.kp * pn.lq
    copies = []

    def write(source, p, n):
        rows = pl.ds(pl.multiple_of(p * size, size), size)
        copy = pltpu.make_async_copy(source, mode_grad.at[rows, :], sem.at[n])
        copy.start()
        copies.append(copy)

    write(product, lead, 0)
    copy = pltpu.make_async_copy(grad, grad_out, grad_sem)
    copy.start()
    copies.append(copy)
    for d in range(1, pn.nlat):
        p = peer(lead, d)
        products(pn, modes, p, tile, spread, buf.at[d - 1])
        write(buf.at[d - 1], p, d)
    for copy in copies:
        copy.wait()


def fast_device(plan, activation, pre_activation, cotangent, mode_weight, local_weight):
    pn = plan
    merged = activation.shape[2]
    flat = [v.reshape(pn.zy, merged) for v in (activation, pre_activation, cotangent)]
    vm = pl.BlockSpec(memory_space=pltpu.VMEM)
    hbm = pl.BlockSpec(memory_space=pltpu.HBM)
    half = MX // pn.nlon * pn.c
    dma = pltpu.SemaphoreType.DMA
    tables = (
        pn.lon_table, pn.lat_table, pn.lead_table, pn.lead_first, pn.lat_last, pn.lead_back, pn.lat_back,
        pn.tile, pn.fan, pn.block,
    )
    size = pn.kp * pn.lq
    product, modes, grad, tile, spread = pl.pallas_call(
        functools.partial(remote_kernel, pn),
        out_shape=(
            pltpu.VMEM((size, pn.cc), F32),
            pltpu.VMEM((2, pn.nlat, pn.lq // 4 * 3, 128), F32),
            pltpu.VMEM((pn.zy, merged), BF16),
            pltpu.VMEM(pn.tile.shape, BF16),
            pltpu.VMEM((pn.kp + 1, 128, pn.cc), BF16),
        ),
        in_specs=[hbm] * 15,
        out_specs=(vm,) * 5,
        scratch_shapes=[
            pltpu.VMEM((pn.zy, merged), BF16),
            pltpu.VMEM((pn.zy, merged), BF16),
            pltpu.VMEM((pn.zy, merged), BF16),
            pltpu.VMEM(local_weight.shape, F32),
            pltpu.VMEM(pn.lon_table.shape[1:], BF16),
        ]
        + [pltpu.VMEM(v.shape, v.dtype) for v in tables[1:7] + tables[8:]]
        + [
            pltpu.VMEM((pn.nlon, pn.nlat, pn.zy // 4 * 3, 128), F32),
            pltpu.VMEM((pn.zy, merged), F32),
            pltpu.VMEM((2, MX * pn.c, 256), BF16),
            pltpu.VMEM((2, STEPS // 2, 2 * pn.zy, 256), BF16),
            pltpu.VMEM((2, pn.zy, merged), BF16),
            pltpu.VMEM((2, pn.nlon, half // 2, 2 * pn.zy), F32),
            pltpu.VMEM((2, half // 2, 2 * pn.zy), F32),
            pltpu.VMEM((2, pn.nlat - 1, pn.kc // 2, 2 * pn.zy), F32),
            pltpu.VMEM((2, pn.nlat, pn.kc // 2, 2 * pn.zy), F32),
            pltpu.VMEM((pn.nlead, pn.zl * MY // 4 * 3, 128), F32),
            pltpu.VMEM((pn.nlat, pn.yl * MZ // 4 * 3, 128), F32),
            pltpu.VMEM((pn.kp * pn.lq, pn.cc), F32),
            pltpu.VMEM((pn.nlat, pn.zy // 4 * 3, 128), F32),
            dma((14,)), dma, dma((2,)), dma((2,)),
            dma((2, pn.nlat - 1)), dma((2, pn.nlat - 1)),
            dma((2, pn.nlead - 1)), dma((2, pn.nlead - 1)),
            dma((2, pn.nlat - 1)), dma((2, pn.nlat - 1)),
            dma((pn.nlat - 1,)), dma((pn.nlat - 1,)),
            dma((pn.nlat,)), dma((pn.nlat,)),
        ],
        compiler_params=pltpu.CompilerParams(
            collective_id=0, has_side_effects=True, vmem_limit_bytes=52 * 2**20
        ),
        name="modes",
    )(*flat, mode_weight, local_weight, *tables)
    grad, mode_grad = pl.pallas_call(
        functools.partial(finish_kernel, pn),
        out_shape=(
            jax.ShapeDtypeStruct((pn.zy, merged), BF16),
            jax.ShapeDtypeStruct((pn.nlat * size, pn.cc), F32),
        ),
        in_specs=[vm] * 5,
        out_specs=(hbm, hbm),
        scratch_shapes=[pltpu.VMEM((pn.nlat - 1, size, pn.cc), F32), dma((pn.nlat,)), dma],
        compiler_params=pltpu.CompilerParams(vmem_limit_bytes=24 * 2**20),
        name="finish",
    )(product, modes, grad, tile, spread)
    return grad.reshape(activation.shape), mode_grad


def solution(mesh):
    in_specs = (
        P("lead", "lat", "lon"),
        P("lead", "lat", "lon"),
        P("lead", "lat", "lon"),
        P("lon", None),
        P(),
    )
    out_specs = (P("lead", "lat", "lon"), P("lon", None))

    def whole(*args):
        shape = args[0].shape
        channels = args[4].shape[0]
        body = on_device
        if (
            mesh.shape["lon"] == 2
            and mesh.shape["lat"] == 4
            and mesh.shape["lead"] == 4
            and MX % (mesh.shape["lon"] * mesh.shape["lat"]) == 0
            and MX * MY * MZ == args[3].shape[0]
            and shape[2] == mesh.shape["lon"] * STEPS * 128
            and 4 * channels == 128
            and MX * channels == 96 * mesh.shape["lon"] * mesh.shape["lat"]
            and mesh.shape["lead"] * 4 == shape[0]
        ):
            body = functools.partial(fast_device, Plan(mesh, shape, channels))
        return jax.shard_map(
            body, mesh=mesh, in_specs=in_specs, out_specs=out_specs, check_vma=False
        )(*args)

    return whole
```
